128 devices in a mesh: gz: 2 (over core), row: 4 (over x), col: 16 (over z, y).
Axes of the slice: x: 4, y: 4, z: 4, core: 2. Of those that a mesh axis runs over, the one named last changes fastest.
Arguments:
- right_side: float32 [4, 64, 16384], P(None, 'col', 'row'), may hold values from -6 to 6
- layer_sums: float32 [2, 4, 64, 16384], P('gz', None, 'col', 'row'), may hold values from -6 to 6
- lower_blocks: float32 [6, 64, 256, 256], P(None, 'col', 'row'), may hold values from -0.1875 to 0.1875
- upper_blocks: float32 [6, 64, 256, 256], P(None, 'col', 'row'), may hold values from -0.1875 to 0.1875
- lower_inverse: float32 [4, 64, 256, 256], P(None, 'col'), may hold values from -1 to 2, as said below
- upper_diagonal_inverses: float32 [4, 64, 256, 256], P(None, 'col'), may hold values from -1 to 2
- pattern: int32 [6, 64], P(None, 'col'), may hold values 0 or 1
- parents: int32 [3, 64], replicated, may hold values from 0 to 63
Outputs:
- forward_solution: float32 [4, 64, 16384], P(None, 'col')
- solution: float32 [4, 64, 16384], P(None, 'col')
The draws below stay inside these ranges and needn't reach their ends.
Inputs may be any that keep to these rules, and one draw needn't show every extreme that they name: `lower_inverse`: inverses of the diagonal blocks of L.
All inputs are finite; a program needn't handle non-finite values. No bound on the sum of `pattern` on one device may be relied on, other than what follows from the above.
Results may differ from the reference program's by a relative error of at most 0.00013.
Values sent between devices are 32-bit elements; how exact they have to be, the bound alone decides.
A program may use at most 128 MiB of HBM per device.

```python
import math
import jax
import jax.numpy as jnp
import numpy as np
from jax import lax

WIDTH = 256
COLUMNS = 64
NODES = 64
N_GZ = 2


def leading_block_rows(key):
    first, second = jax.random.split(key)
    shape = (4, NODES, WIDTH, WIDTH)
    diagonal = jax.random.uniform(first, (4, NODES, WIDTH), jnp.float32, 0.75, 1.5)
    spread = jax.random.normal(second, shape, jnp.float32)
    spread = spread * (0.6 / WIDTH ** 0.5)
    return spread + diagonal[..., None] * jnp.eye(WIDTH, dtype=jnp.float32)


def draw_lower_inverse(key, part):
    return leading_block_rows(jax.random.fold_in(key, 11))


def draw_upper_diagonal_inverses(key, part):
    return leading_block_rows(jax.random.fold_in(key, 23))


def plant(values, rng, smallest, largest):
    dims = values.shape
    index_at = [jax.random.randint(jax.random.fold_in(rng, axis), (), 0, dims[axis]) for axis in range(len(dims))]
    values = values.at[tuple(index_at)].set(smallest)
    longest = dims.index(max(dims))
    index_at[longest] = (index_at[longest] + 1) % dims[longest]
    return values.at[tuple(index_at)].set(largest)


def block_levels(stream_key, extent, cuts, low, largest):
    def one(position, shards_of):
        draws = jax.random.uniform(jax.random.fold_in(jax.random.fold_in(stream_key, 6), position), (shards_of,), jnp.float32, low / len(cuts), largest / len(cuts))
        return jnp.repeat(jnp.exp(draws), extent[position] // shards_of).reshape((-1,) + (1,) * (len(extent) - position - 1))

    level = one(*cuts[0])
    for cut in cuts[1:]:
        level = level * one(*cut)
    return level


def rank_table(count, slope):
    weights = [(1 << 20) // math.isqrt(rank ** slope) + 1 for rank in range(1, count + 1)]
    width = 1 + sum(weights) // (1 << 30)
    return np.cumsum(np.array([max(1, weight // width) for weight in weights]))


def skewed_ids(rng, shape, number_of, skew):
    grid = rank_table(number_of, skew)
    lot = jax.random.randint(jax.random.fold_in(rng, 1), shape, 0, int(grid[number_of - 1]))
    rank = jnp.searchsorted(jnp.asarray(grid, jnp.int32), lot, side="right")
    return jax.random.permutation(jax.random.fold_in(rng, 2), number_of)[rank].astype(jnp.int32)


def scatter_about(stream_key, shape, scale, bound, cuts=(), kind=jnp.bfloat16):
    gain = block_levels(stream_key, shape, cuts, -0.22, 0.18) if cuts else 1.0
    drawn = jax.random.normal(stream_key, shape, jnp.float32) * scale * gain
    return jnp.minimum(jnp.maximum(drawn, -bound), bound).astype(kind)


def setup_inputs(seed: int = 0) -> dict:
    keys = jax.random.split(jax.random.key(seed), 9)
    return {
        "right_side": scatter_about(keys[0], (4, NODES, WIDTH * COLUMNS), 1.0, 6.0, ((1, 16), (2, 4)), jnp.float32),
        "layer_sums": scatter_about(keys[1], (N_GZ, 4, NODES, WIDTH * COLUMNS), 1.0, 6.0, ((0, 2), (2, 16), (3, 4)), jnp.float32),
        "lower_blocks": scatter_about(keys[2], (6, NODES, WIDTH, WIDTH), (4 * WIDTH) ** -0.5, 0.1875, ((1, 16), (2, 4)), jnp.float32),
        "upper_blocks": scatter_about(keys[3], (6, NODES, WIDTH, WIDTH), (4 * WIDTH) ** -0.5, 0.1875, ((1, 16), (2, 4)), jnp.float32),
        "lower_inverse": draw_lower_inverse(jax.random.fold_in(keys[8], 71), 0),
        "upper_diagonal_inverses": draw_upper_diagonal_inverses(jax.random.fold_in(keys[8], 71), 0),
        "pattern": plant((jax.random.randint(keys[6], (6, NODES), 0, 4) < 3).astype(jnp.int32), jax.random.fold_in(keys[6], 1), 0, 1),
        "parents": plant(skewed_ids(keys[7], (3, NODES), NODES, 1), jax.random.fold_in(keys[7], 3), 0, NODES - 1).astype(jnp.int32),
    }


def place_of(height, distance):
    return height * (height - 1) // 2 + distance - 1


def ancestor_table(parents):
    ancestors = {}
    for height in range(1, 4):
        current = parents[height - 1]
        ancestors[(height, 1)] = current
        for distance in range(2, height + 1):
            current = parents[height - distance][current]
            ancestors[(height, distance)] = current
    return ancestors


def reference(right_side, layer_sums, lower_blocks, upper_blocks, lower_inverse, upper_diagonal_inverses, pattern, parents):
    present = pattern.astype(jnp.float32)
    ancestors = ancestor_table(parents)
    initial = (right_side - jnp.sum(layer_sums, axis=0)).reshape(4, NODES, WIDTH, COLUMNS)
    pending = [jnp.zeros((NODES, WIDTH, COLUMNS), jnp.float32) for height in range(4)]
    forward = [None] * 4
    for height in (3, 2, 1, 0):
        solved = jnp.einsum("jvw,jwk->jvk", lower_inverse[height], initial[height] - pending[height], precision=lax.Precision.HIGHEST)
        forward[height] = solved
        for distance in range(1, height + 1):
            block_place = place_of(height, distance)
            blocks = lower_blocks[block_place] * present[block_place][:, None, None]
            product = jnp.einsum("jvw,jwk->jvk", blocks, solved, precision=lax.Precision.HIGHEST)
            destination_rows = height - distance
            pending[destination_rows] = pending[destination_rows] + jax.ops.segment_sum(product, ancestors[(height, distance)], num_segments=NODES)
    backward = [None] * 4
    for height in range(4):
        accumulated = jnp.zeros((NODES, WIDTH, COLUMNS), jnp.float32)
        for distance in range(1, height + 1):
            block_place = place_of(height, distance)
            blocks = upper_blocks[block_place] * present[block_place][:, None, None]
            chosen = backward[height - distance][ancestors[(height, distance)]]
            accumulated = accumulated + jnp.einsum("jvw,jwk->jvk", blocks, chosen, precision=lax.Precision.HIGHEST)
        backward[height] = jnp.einsum("jvw,jwk->jvk", upper_diagonal_inverses[height], forward[height] - accumulated, precision=lax.Precision.HIGHEST)
    forward_all = jnp.stack(forward).reshape(4, NODES, WIDTH * COLUMNS)
    backward_sweep_levels = jnp.stack(backward).reshape(4, NODES, WIDTH * COLUMNS)
    return forward_all, backward_sweep_levels
```

```python
import jax
import jax.numpy as jnp
from jax import lax
from jax.experimental import pallas as pl
from jax.experimental.pallas import tpu as pltpu
from jax.sharding import PartitionSpec as P

MESH = pl.DeviceIdType.MESH
F32 = jnp.float32
BF16 = jnp.bfloat16
LANES = 128
PART = 64
NODES_HERE = 4
OFFSETS = sorted(
    [(dz, dy) for dz in range(4) for dy in range(4) if dz or dy],
    key=lambda o: -(min(o[0], 4 - o[0]) + min(o[1], 4 - o[1])),
)
GZ_TOP, GZ_REST, ROW_IN, SCATTER, GATHER, ROW_OUT, FWD_OUT, BWD_OUT, U_SWAP, PHASES = (
    0, 1, 2, 6, 9, 12, 15, 19, 23, 24,
)
BLOCK = PART * LANES


def place_of(height, distance):
    return height * (height - 1) // 2 + distance - 1


def split(x):
    high = x.astype(BF16)
    return high, (x - high.astype(F32)).astype(BF16)


def dot(a, b):
    return jnp.dot(a, b, preferred_element_type=F32)


def pair_of(b):
    high, low = split(b)
    return high, jnp.concatenate([high, low], axis=1)


def product(a_high, a_low, b_pair):
    b_high, b_both = b_pair
    wide = dot(a_high, b_both)
    return wide[:, :LANES] + wide[:, LANES:] + dot(a_low, b_high)


def roll_groups(x, groups):
    groups = groups % 4
    return pltpu.roll(x, 32 * groups, 1) if groups else x


def kernel(
    right_hbm, sums_hbm, lower_hbm, upper_hbm, linv_hbm, uinv_hbm, pattern_ref, parents_ref,
    fwd_hbm, bwd_hbm,
    right, sums, lower, upper, linv, uinv,
    zsend, zrecv, init, rows_in, sbuf, qbuf, gbuf0, gbuf1, gbuf2, pbuf, prec,
    fbuf, ybuf, ustage, uswap, vhi, vlo, whi, wlo, ulhi, ullo, zpart, out_f, out_b,
    send_sem, recv_sem, load_sem, store_sem,
):
    g = lax.axis_index("gz")
    r = lax.axis_index("row")
    c = lax.axis_index("col")
    z, y = c // 4, c % 4
    gbuf = (gbuf0, gbuf1, gbuf2)

    def column(offset):
        return ((z + offset[0]) % 4) * 4 + (y + offset[1]) % 4

    loads = {}

    def load(name, source, target):
        loads[name] = pltpu.make_async_copy(source, target, load_sem.at[len(loads)])
        loads[name].start()

    load("right", right_hbm, right)
    load("sums", sums_hbm, sums)
    load("lower", lower_hbm, lower)
    load("linv3", linv_hbm.at[3], linv.at[3])
    load("linv2", linv_hbm.at[2], linv.at[2])
    load("upper", upper_hbm, upper)
    load("linv1", linv_hbm.at[1], linv.at[1])
    load("linv0", linv_hbm.at[0], linv.at[0])
    for height in (3, 0, 1, 2):
        load("uinv%d" % height, uinv_hbm.at[height], uinv.at[height])

    barrier = pltpu.get_barrier_semaphore()
    for offset in OFFSETS:
        pl.semaphore_signal(
            barrier, inc=1, device_id={"col": column(offset)}, device_id_type=MESH
        )
    others = []
    for step in range(4):
        others.append({"gz": 1 - g, "row": (r + step) % 4})
    for step in range(1, 4):
        others.append({"gz": g, "row": (r + step) % 4})
    for place in others:
        pl.semaphore_signal(barrier, inc=1, device_id=place, device_id_type=MESH)

    def send(source, target, phase, place):
        pltpu.make_async_remote_copy(
            src_ref=source, dst_ref=target, send_sem=send_sem.at[phase],
            recv_sem=recv_sem.at[phase], device_id=place, device_id_type=MESH,
        ).start()

    def wait_blocks(sem, blocks):
        whole = qbuf.at[0, pl.ds(0, blocks)] if blocks <= 16 else uswap.at[pl.ds(0, blocks // 12)]
        pltpu.make_async_copy(whole, whole, sem).wait()

    my_rows = pl.ds(pl.multiple_of(r * PART, PART), PART)
    row_steps = (2, 1, 3)

    ancestor, stored = {}, {}
    for height in (1, 2, 3):
        for m in range(NODES_HERE):
            current = parents_ref[height - 1, c * NODES_HERE + m]
            for distance in range(1, height + 1):
                if distance > 1:
                    current = parents_ref[height - distance, current]
                ancestor[height, distance, m] = current
                stored[height, distance, m] = pattern_ref[place_of(height, distance), m] != 0

    group = lax.broadcasted_iota(jnp.int32, (PART, LANES), 1) // 32

    def regroup(x, shift_of, rows):
        lanes = lax.broadcasted_iota(jnp.int32, (rows, LANES), 1) // 32
        total = None
        for m in range(4):
            block, source = shift_of(m)
            moved = roll_groups(x[block], m - source)
            total = moved if total is None else jnp.where(lanes == m, moved, total)
        return total

    def take_input(height):
        for parity in range(2):
            blocks_r = [right[pl.ds(height * 128 + m, 32, stride=4), :] for m in range(4)]
            blocks_s = [sums[pl.ds(height * 128 + m, 32, stride=4), :] for m in range(4)]
            diff = [a - b for a, b in zip(blocks_r, blocks_s)]
            halves_d = [regroup(diff, lambda m: (m, 2 * parity + half), 32) for half in range(2)]
            halves_s = [regroup(blocks_s, lambda m: (m, 2 * parity + half), 32) for half in range(2)]
            mine = pl.ds(parity, 32, stride=2)
            init[height, mine, :] = jnp.where(g == 0, halves_d[0], halves_d[1])
            zsend[height, mine, :] = jnp.where(g == 0, halves_s[1], halves_s[0])

    loads["right"].wait()
    loads["sums"].wait()
    take_input(3)
    pl.semaphore_wait(barrier, len(OFFSETS) + len(others))
    send(zsend.at[3], zrecv.at[3], GZ_TOP, {"gz": 1 - g})
    for height in (2, 1, 0):
        take_input(height)
    send(zsend.at[pl.ds(0, 3)], zrecv.at[pl.ds(0, 3)], GZ_REST, {"gz": 1 - g})

    def make_v(height):
        def one(m, carry):
            b_high, b_low = split(linv[height, m])
            for distance in range(1, height + 1):
                q = place_of(height, distance)
                a_high, a_low = split(lower[q, m])
                v_high, v_low = split(dot(a_high, b_high) + dot(a_high, b_low) + dot(a_low, b_high))
                vhi[q, m] = v_high
                vlo[q, m] = v_low
            return carry
        lax.fori_loop(0, NODES_HERE, one, 0)

    def share_rows(height, value):
        rows_in[height, my_rows, :] = value
        for step in row_steps:
            send(
                rows_in.at[height, my_rows, :], rows_in.at[height, my_rows, :],
                ROW_IN + height, {"row": (r + step) % 4},
            )

    def scatter_terms(height, distance, b_pair, first, out):
        q = place_of(height, distance)
        target = height - distance
        terms = []
        for m in range(NODES_HERE):
            own = product(vhi[q, m], vlo[q, m], b_pair)
            spread = own
            for t in range(4):
                if t != m:
                    spread = jnp.where(group == t, roll_groups(own, t - m), spread)
            terms.append(spread)
        wanted = [
            jnp.where(stored[height, distance, m], ancestor[height, distance, m], -1)
            for m in range(NODES_HERE)
        ]
        for offset in OFFSETS + [(0, 0)]:
            slot = offset[0] * 4 + offset[1]
            base = column(offset) * NODES_HERE
            total = jnp.zeros((PART, LANES), F32) if first else sbuf[target, slot]
            for m in range(NODES_HERE):
                total = total + jnp.where(group == wanted[m] - base, terms[m], 0.0)
            sbuf[target, slot] = total
            if out and slot:
                send(
                    sbuf.at[target, slot], qbuf.at[target, slot], SCATTER + target,
                    {"col": column(offset)},
                )

    def solve_into(inverse, height, b_pair, target):
        lanes = lax.broadcasted_iota(jnp.int32, (256, LANES), 1) // 32

        def one(m, carry):
            a_high, a_low = split(inverse[height, m])
            whole = product(a_high, a_low, b_pair)
            target[...] = jnp.where(lanes == m, whole, target[...])
            return carry

        target[...] = jnp.zeros((256, LANES), F32)
        lax.fori_loop(0, NODES_HERE, one, 0)

    def write_out(source, out, hbm, height, slot):
        lanes = lax.broadcasted_iota(jnp.int32, (128, LANES), 1) // 32
        pieces = [
            source[height, half, pl.ds(parity, 128, stride=2), :]
            for parity in range(2) for half in range(2)
        ]
        for m in range(NODES_HERE):
            total = None
            for place in range(4):
                moved = roll_groups(pieces[place], place - m)
                total = moved if total is None else jnp.where(lanes == place, moved, total)
            out[pl.ds(height * 512 + m, 128, stride=4), :] = total
        pltpu.make_async_copy(
            out.at[pl.ds(height * 512, 512)], hbm.at[pl.ds(height * 512, 512)], store_sem.at[slot]
        ).start()

    def sum_received(target):
        total = init[target] - sbuf[target, 0]
        for slot in range(1, 16):
            total = total - qbuf[target, slot]
        return total

    def stage_upper():
        lanes = lax.broadcasted_iota(jnp.int32, (PART, LANES), 1)

        def one(m, carry):
            for index, (first, second) in enumerate(((1, 2), (3, 4), (5, 0))):
                for part in range(4):
                    tile = slice(LANES * (part // 2), LANES * (part // 2) + LANES)
                    a, b = upper[first, m, :, tile], upper[second, m, :, tile]
                    if part % 2 == 0:
                        b = pltpu.roll(b, 64, 1)
                    else:
                        a = pltpu.roll(a, 64, 1)
                    ustage[part, index, m] = jnp.where(lanes < 64, a, b)
            return carry

        lax.fori_loop(0, NODES_HERE, one, 0)

    def make_w(height):
        pairs = {1: (2,), 2: (0,), 3: (1, 2)}[height]

        def one(m, carry):
            a_high, a_low = split(uinv[height, m])
            for place, index in enumerate(pairs):
                b = jnp.concatenate([uswap[part, index, m] for part in range(4)], axis=0)
                w_high, w_low = split(product(a_high, a_low, pair_of(b)))
                whi[height + place - 1, m] = w_high
                wlo[height + place - 1, m] = w_low
            return carry

        lax.fori_loop(0, NODES_HERE, one, 0)

    def make_z(height):
        b_pair = pair_of(fbuf[height, g])
        total = None
        for m in range(NODES_HERE):
            a_high, a_low = split(uinv[height, m, my_rows, :])
            own = product(a_high, a_low, b_pair)
            total = own if total is None else jnp.where(group == m, own, total)
        zpart[height - 1] = total

    def finish_forward(height, b_pair):
        solve_into(linv, height, b_pair, fbuf.at[height, g])
        send(fbuf.at[height, g], fbuf.at[height, g], FWD_OUT + height, {"gz": 1 - g})

    loads["lower"].wait()
    loads["linv3"].wait()
    make_v(3)
    wait_blocks(recv_sem.at[GZ_TOP], 1)
    share_rows(3, init[3] - zrecv[3])
    loads["upper"].wait()
    stage_upper()
    wait_blocks(recv_sem.at[ROW_IN + 3], 3)
    b_pair = pair_of(rows_in[3])
    scatter_terms(3, 1, b_pair, True, True)
    for step in row_steps:
        send(ustage.at[(r + step) % 4], uswap.at[r], U_SWAP, {"row": (r + step) % 4})
    own_upper = pltpu.make_async_copy(ustage.at[r], uswap.at[r], load_sem.at[len(loads)])
    own_upper.start()
    scatter_terms(3, 2, b_pair, True, False)
    scatter_terms(3, 3, b_pair, True, False)
    finish_forward(3, b_pair)
    loads["linv2"].wait()
    make_v(2)
    wait_blocks(recv_sem.at[GZ_REST], 3)
    for height in range(3):
        init[height] = init[height] - zrecv[height]

    wait_blocks(recv_sem.at[SCATTER + 2], 15)
    share_rows(2, sum_received(2))
    loads["linv1"].wait()
    make_v(1)
    wait_blocks(recv_sem.at[ROW_IN + 2], 3)
    b_pair = pair_of(rows_in[2])
    scatter_terms(2, 1, b_pair, False, True)
    scatter_terms(2, 2, b_pair, False, False)
    finish_forward(2, b_pair)
    loads["uinv3"].wait()
    make_z(3)
    wait_blocks(recv_sem.at[FWD_OUT + 3], 4)
    write_out(fbuf, out_f, fwd_hbm, 3, 0)

    wait_blocks(recv_sem.at[SCATTER + 1], 15)
    share_rows(1, sum_received(1))
    wait_blocks(recv_sem.at[ROW_IN + 1], 3)
    b_pair = pair_of(rows_in[1])
    scatter_terms(1, 1, b_pair, False, True)
    finish_forward(1, b_pair)
    loads["linv0"].wait()
    loads["uinv0"].wait()

    def make_ul(m, carry):
        b_high, b_low = split(linv[0, m])
        a_high, a_low = split(uinv[0, m, my_rows, :])
        ul_high, ul_low = split(dot(a_high, b_high) + dot(a_high, b_low) + dot(a_low, b_high))
        ulhi[m] = ul_high
        ullo[m] = ul_low
        return carry

    lax.fori_loop(0, NODES_HERE, make_ul, 0)
    loads["uinv1"].wait()
    loads["uinv2"].wait()
    wait_blocks(recv_sem.at[U_SWAP], 36)
    own_upper.wait()
    make_w(1)

    wait_blocks(recv_sem.at[SCATTER + 0], 15)
    share_rows(0, sum_received(0))
    make_z(2)
    wait_blocks(recv_sem.at[ROW_IN + 0], 3)
    b_pair = pair_of(rows_in[0])

    def share_solution(height, value):
        gbuf[height][0] = value
        for offset in OFFSETS:
            slot = offset[0] * 4 + offset[1]
            send(
                gbuf[height].at[0], gbuf[height].at[slot], GATHER + height,
                {"col": column(offset)},
            )

    top = None
    for m in range(NODES_HERE):
        own = product(ulhi[m], ullo[m], b_pair)
        top = own if top is None else jnp.where(group == m, own, top)
    share_solution(0, top)
    finish_forward(0, b_pair)
    make_z(1)
    solve_into(uinv, 0, pair_of(fbuf[0, g]), ybuf.at[0, g])
    send(ybuf.at[0, g], ybuf.at[0, g], BWD_OUT, {"gz": 1 - g})
    make_w(2)

    def chosen(height, distance):
        total = jnp.zeros((PART, LANES), F32)
        for m in range(NODES_HERE):
            a = ancestor[height, distance, m]
            chip = a // NODES_HERE
            slot = ((z + 4 - chip // 4) % 4) * 4 + (y + 4 - chip % 4) % 4
            block = gbuf[height - distance][slot]
            present = stored[height, distance, m]
            for source in range(4):
                here = jnp.where(jnp.logical_and(present, a % NODES_HERE == source), m, -1)
                total = jnp.where(group == here, roll_groups(block, m - source), total)
        return total

    row_lanes = lax.broadcasted_iota(jnp.int32, (256, LANES), 1) // 32

    def row_terms(height, pieces):
        zero = jnp.zeros((PART, LANES), F32)
        pieces = {1: [zero] + pieces, 2: pieces, 3: pieces + [zero]}[height]
        pairs = [pair_of(jnp.concatenate(pieces[i:i + 2], axis=0)) for i in range(0, len(pieces), 2)]

        def one(m, carry):
            whole = product(whi[height - 1, m], wlo[height - 1, m], pairs[0])
            if height == 3:
                whole = whole + product(whi[3, m], wlo[3, m], pairs[1])
            pbuf[height - 1] = jnp.where(row_lanes == m, whole, pbuf[height - 1])
            return carry

        pbuf[height - 1] = jnp.zeros((256, LANES), F32)
        for m in range(NODES_HERE):
            one(m, 0)
        for step in row_steps:
            to = (r + step) % 4
            send(
                pbuf.at[height - 1, pl.ds(pl.multiple_of(to * PART, PART), PART), :],
                prec.at[height - 1, step - 1], ROW_OUT + height - 1, {"row": to},
            )

    def take_rows(height):
        wait_blocks(recv_sem.at[ROW_OUT + height - 1], 3)
        total = zpart[height - 1] - pbuf[height - 1, my_rows, :]
        for step in range(3):
            total = total - prec[height - 1, step]
        return total

    def spread_out(height, value):
        ybuf[height, g, my_rows, :] = value
        for place in others:
            send(
                ybuf.at[height, g, my_rows, :], ybuf.at[height, g, my_rows, :],
                BWD_OUT + height, place,
            )

    wait_blocks(recv_sem.at[GATHER + 0], 15)
    row_terms(1, [chosen(1, 1)])
    wait_blocks(recv_sem.at[FWD_OUT + 2], 4)
    write_out(fbuf, out_f, fwd_hbm, 2, 1)
    value = take_rows(1)
    share_solution(1, value)
    spread_out(1, value)
    make_w(3)
    early2 = chosen(2, 2)
    early3 = chosen(3, 3)
    wait_blocks(recv_sem.at[FWD_OUT + 1], 4)
    write_out(fbuf, out_f, fwd_hbm, 1, 2)

    wait_blocks(recv_sem.at[GATHER + 1], 15)
    row_terms(2, [chosen(2, 1), early2])
    wait_blocks(recv_sem.at[FWD_OUT + 0], 4)
    write_out(fbuf, out_f, fwd_hbm, 0, 3)
    value = take_rows(2)
    share_solution(2, value)
    spread_out(2, value)
    early32 = chosen(3, 2)
    wait_blocks(recv_sem.at[BWD_OUT + 0], 4)
    write_out(ybuf, out_b, bwd_hbm, 0, 4)
    wait_blocks(recv_sem.at[BWD_OUT + 1], 7)
    write_out(ybuf, out_b, bwd_hbm, 1, 5)

    wait_blocks(recv_sem.at[GATHER + 2], 15)
    row_terms(3, [chosen(3, 1), early32, early3])
    wait_blocks(recv_sem.at[BWD_OUT + 2], 7)
    write_out(ybuf, out_b, bwd_hbm, 2, 6)
    spread_out(3, take_rows(3))
    wait_blocks(recv_sem.at[BWD_OUT + 3], 7)
    write_out(ybuf, out_b, bwd_hbm, 3, 7)

    for phase, blocks in (
        [(GZ_TOP, 1), (GZ_REST, 3), (U_SWAP, 36)]
        + [(ROW_IN + h, 3) for h in range(4)]
        + [(SCATTER + t, 15) for t in range(3)]
        + [(GATHER + t, 15) for t in range(3)]
        + [(ROW_OUT + h, 3) for h in range(3)]
        + [(FWD_OUT + h, 4) for h in range(4)]
        + [(BWD_OUT + h, 4 if h == 0 else 7) for h in range(4)]
    ):
        wait_blocks(send_sem.at[phase], blocks)
    for slot, (height, out, hbm) in enumerate(
        [(h, out_f, fwd_hbm) for h in (3, 2, 1, 0)] + [(h, out_b, bwd_hbm) for h in (0, 1, 2, 3)]
    ):
        rows = pl.ds(height * 512, 512)
        pltpu.make_async_copy(out.at[rows], hbm.at[rows], store_sem.at[slot]).wait()


def body(
    right_side, layer_sums, lower_blocks, upper_blocks, lower_inverse, upper_diagonal_inverses,
    pattern, parents,
):
    def tiled(x):
        return x.reshape(4, 4, 32, 128).transpose(0, 2, 1, 3).reshape(512, 128)

    anywhere = pl.BlockSpec(memory_space=pl.ANY)
    scalar = pl.BlockSpec(memory_space=pltpu.SMEM)
    forward, backward = pl.pallas_call(
        kernel,
        out_shape=[jax.ShapeDtypeStruct((2048, 128), F32)] * 2,
        in_specs=[anywhere] * 6 + [scalar] * 2,
        out_specs=[anywhere] * 2,
        scratch_shapes=[
            pltpu.VMEM((512, 128), F32),
            pltpu.VMEM((512, 128), F32),
            pltpu.VMEM((6, 4, 64, 256), F32),
            pltpu.VMEM((6, 4, 64, 256), F32),
            pltpu.VMEM((4, 4, 256, 256), F32),
            pltpu.VMEM((4, 4, 256, 256), F32),
            pltpu.VMEM((4, 64, 128), F32),
            pltpu.VMEM((4, 64, 128), F32),
            pltpu.VMEM((4, 64, 128), F32),
            pltpu.VMEM((4, 256, 128), F32),
            pltpu.VMEM((3, 16, 64, 128), F32),
            pltpu.VMEM((3, 16, 64, 128), F32),
            pltpu.VMEM((16, 64, 128), F32),
            pltpu.VMEM((16, 64, 128), F32),
            pltpu.VMEM((16, 64, 128), F32),
            pltpu.VMEM((3, 256, 128), F32),
            pltpu.VMEM((3, 3, 64, 128), F32),
            pltpu.VMEM((4, 2, 256, 128), F32),
            pltpu.VMEM((4, 2, 256, 128), F32),
            pltpu.VMEM((4, 3, 4, 64, 128), F32),
            pltpu.VMEM((4, 3, 4, 64, 128), F32),
            pltpu.VMEM((6, 4, 64, 256), BF16),
            pltpu.VMEM((6, 4, 64, 256), BF16),
            pltpu.VMEM((4, 4, 256, 128), BF16),
            pltpu.VMEM((4, 4, 256, 128), BF16),
            pltpu.VMEM((4, 64, 256), BF16),
            pltpu.VMEM((4, 64, 256), BF16),
            pltpu.VMEM((3, 64, 128), F32),
            pltpu.VMEM((2048, 128), F32),
            pltpu.VMEM((2048, 128), F32),
            pltpu.SemaphoreType.DMA((PHASES,)),
            pltpu.SemaphoreType.DMA((PHASES,)),
            pltpu.SemaphoreType.DMA((16,)),
            pltpu.SemaphoreType.DMA((8,)),
        ],
        compiler_params=pltpu.CompilerParams(
            collective_id=0, has_side_effects=True, vmem_limit_bytes=56 * 1024 * 1024
        ),
    )(
        tiled(right_side), tiled(layer_sums[0]), lower_blocks, upper_blocks, lower_inverse,
        upper_diagonal_inverses, pattern, parents,
    )

    def untiled(x):
        return x.reshape(4, 128, 4, 128).transpose(0, 2, 1, 3).reshape(4, 4, 16384)

    return untiled(forward), untiled(backward)


def solution(mesh):
    in_specs = (
        P(None, "col", "row"),
        P("gz", None, "col", "row"),
        P(None, "col", "row", None),
        P(None, "col", "row", None),
        P(None, "col", None, None),
        P(None, "col", None, None),
        P(None, "col"),
        P(),
    )
    out_specs = (P(None, "col", None), P(None, "col", None))
    return jax.shard_map(body, mesh=mesh, in_specs=in_specs, out_specs=out_specs, check_vma=False)
```

```python
import jax
import jax.numpy as jnp
from jax import lax
from jax.experimental import pallas as pl
from jax.experimental.pallas import tpu as pltpu
from jax.sharding import PartitionSpec as P

MESH = pl.DeviceIdType.MESH
F32 = jnp.float32
BF16 = jnp.bfloat16
LANES = 128
PART = 64
NODES_HERE = 4
OFFSETS = sorted(
    [(dz, dy) for dz in range(4) for dy in range(4) if dz or dy],
    key=lambda o: -(min(o[0], 4 - o[0]) + min(o[1], 4 - o[1])),
)
INPUT, SCATTER, GATHER, FWD_OUT, BWD_OUT, L_ROW, L_GZ, U_ROW, U_GZ, PHASES = (
    0, 1, 4, 7, 11, 15, 21, 27, 33, 39,
)


def place_of(height, distance):
    return height * (height - 1) // 2 + distance - 1


def lane_ids(rows):
    return lax.broadcasted_iota(jnp.int32, (rows, LANES), 1)


def split(x):
    high = x.astype(BF16)
    return high, (x - high.astype(F32)).astype(BF16)


def dot(a, b):
    return jnp.dot(a, b, preferred_element_type=F32)


def wide_of(a):
    return jnp.concatenate(split(a), axis=1)


def rolled(x, lanes):
    lanes = lanes % LANES
    return pltpu.roll(x, lanes, 1) if lanes else x


def operand_of(x):
    full = jnp.concatenate([rolled(x, -32 * part) for part in range(4)], axis=0)
    high = full.astype(BF16).astype(F32)
    low = full - high
    lanes = lane_ids(256)
    both = jnp.where(lanes < 32, high, rolled(low.astype(BF16).astype(F32), 32))
    alone = jnp.where(lanes < 32, high, 0.0)
    return jnp.concatenate([both.astype(BF16), alone.astype(BF16)], axis=0)


def apply(matrix_of, operand):
    node = (lane_ids(256) // 8) % 4
    total = None
    for m in range(NODES_HERE):
        out = dot(matrix_of(m), operand)
        total = out if total is None else jnp.where(node == m, out, total)
    total = total + rolled(total, -32)
    quarter = lane_ids(PART) // 32
    packed = None
    for part in range(4):
        moved = rolled(total[part * PART:(part + 1) * PART], 32 * part)
        packed = moved if packed is None else jnp.where(quarter == part, moved, packed)
    return packed


def exchange(arrays):
    octet = lane_ids(arrays[0].shape[0]) // 8
    arrays = list(arrays)
    for bit in (1, 2, 4, 8):
        low = (octet // bit) % 2 == 0
        for i in range(16):
            if i & bit:
                continue
            a, b = arrays[i], arrays[i | bit]
            arrays[i] = jnp.where(low, a, rolled(b, 8 * bit))
            arrays[i | bit] = jnp.where(low, rolled(a, -8 * bit), b)
    return arrays


def kernel(
    right_hbm, sums_hbm, lower_hbm, upper_hbm, linv_hbm, uinv_hbm, pattern_ref, parents_ref,
    fwd_hbm, bwd_hbm,
    right, sums, lower, upper, linv, uinv,
    xsend, xrecv, init, sbuf, qbuf, gbuf0, gbuf1, gbuf2,
    fbuf, ybuf, top_inv, v21, v11, ul, w11, w21, w31, out_f, out_b,
    send_sem, recv_sem, load_sem, store_sem,
):
    g = lax.axis_index("gz")
    r = lax.axis_index("row")
    c = lax.axis_index("col")
    z, y = c // 4, c % 4
    me = g * 4 + r
    gbuf = (gbuf0, gbuf1, gbuf2)

    def column(offset):
        return ((z + offset[0]) % 4) * 4 + (y + offset[1]) % 4

    loads = {}

    def load(name, source, target):
        loads[name] = pltpu.make_async_copy(source, target, load_sem.at[len(loads)])
        loads[name].start()

    my_rows = pl.ds(pl.multiple_of(r * PART, PART), PART)
    my_nodes = pl.ds(g * 2, 2)
    load("right", right_hbm, right)
    load("sums", sums_hbm, sums)
    load("linv3", linv_hbm.at[3], linv.at[3])
    load("lower", lower_hbm.at[:, my_nodes], lower.at[:, my_nodes, my_rows, :])
    load("linv2", linv_hbm.at[2], linv.at[2])
    load("linv1", linv_hbm.at[1], linv.at[1])
    load("upper", upper_hbm.at[:, my_nodes], upper.at[:, my_nodes, my_rows, :])
    load("linv0", linv_hbm.at[0], linv.at[0])
    for height in (0, 1, 2, 3):
        load("uinv%d" % height, uinv_hbm.at[height], uinv.at[height])

    barrier = pltpu.get_barrier_semaphore()
    for offset in OFFSETS:
        pl.semaphore_signal(
            barrier, inc=1, device_id={"col": column(offset)}, device_id_type=MESH
        )
    row_steps = (2, 1, 3)
    others = []
    for step in (2, 1, 3):
        others.append((g, (r + step) % 4))
        others.append((1 - g, (r + step) % 4))
    others.append((1 - g, r))
    for place in others:
        pl.semaphore_signal(
            barrier, inc=1, device_id={"gz": place[0], "row": place[1]}, device_id_type=MESH
        )

    def send(source, target, phase, place):
        pltpu.make_async_remote_copy(
            src_ref=source, dst_ref=target, send_sem=send_sem.at[phase],
            recv_sem=recv_sem.at[phase], device_id=place, device_id_type=MESH,
        ).start()

    def wait_bytes(whole, sem):
        pltpu.make_async_copy(whole, whole, sem).wait()

    def wait_blocks(sem, blocks):
        wait_bytes(qbuf.at[0, pl.ds(0, blocks)], sem)

    ancestor, stored = {}, {}
    for height in (1, 2, 3):
        for m in range(NODES_HERE):
            current = parents_ref[height - 1, c * NODES_HERE + m]
            for distance in range(1, height + 1):
                if distance > 1:
                    current = parents_ref[height - distance, current]
                ancestor[height, distance, m] = current
                stored[height, distance, m] = pattern_ref[m, place_of(height, distance)] != 0

    node_of = (lane_ids(PART) // 8) % 4

    def gather_matrix(source, target, phase, q):
        for step in row_steps:
            send(
                source.at[q, my_nodes], target.at[q, my_nodes, my_rows, :], phase + q,
                {"row": (r + step) % 4},
            )

    def hand_over(target, phase_row, phase_gz, q):
        wait_bytes(target.at[q, pl.ds(0, 2), pl.ds(0, 192), :], recv_sem.at[phase_row + q])
        send(target.at[q, my_nodes], target.at[q, my_nodes], phase_gz + q, {"gz": 1 - g})

    def wait_matrix(target, phase_gz, q):
        wait_bytes(target.at[q, pl.ds(0, 2)], recv_sem.at[phase_gz + q])

    def lower_send(q):
        gather_matrix(lower_hbm, lower, L_ROW, q)

    def upper_send(q):
        gather_matrix(upper_hbm, upper, U_ROW, q)

    def lower_hand(q):
        hand_over(lower, L_ROW, L_GZ, q)

    def upper_hand(q):
        hand_over(upper, U_ROW, U_GZ, q)

    def multiply(target, a_of, b_of):
        def one(m, carry):
            a_high, a_low = split(a_of(m))
            b_high, b_low = split(b_of(m))
            target[m] = wide_of(dot(a_high, b_high) + dot(a_high, b_low) + dot(a_low, b_high))
            return carry
        lax.fori_loop(0, NODES_HERE, one, 0)

    def scatter_terms(height, distance, product, first, out):
        target = height - distance
        moved = {shift: rolled(product, 8 * shift) for shift in range(-3, 4)}
        terms = []
        for m in range(NODES_HERE):
            spread = moved[-m]
            for t in range(1, 4):
                spread = jnp.where(node_of == t, moved[t - m], spread)
            terms.append(spread)
        wanted = [
            jnp.where(stored[height, distance, m], ancestor[height, distance, m], -1)
            for m in range(NODES_HERE)
        ]
        for offset in OFFSETS + [(0, 0)]:
            slot = offset[0] * 4 + offset[1]
            base = column(offset) * NODES_HERE
            total = jnp.zeros((PART, LANES), F32) if first else sbuf[target, slot]
            for m in range(NODES_HERE):
                total = total + jnp.where(node_of == wanted[m] - base, terms[m], 0.0)
            sbuf[target, slot] = total
            if out and slot:
                send(
                    sbuf.at[target, slot], qbuf.at[target, slot], SCATTER + target,
                    {"col": column(offset)},
                )

    def sum_received(target):
        wait_blocks(recv_sem.at[SCATTER + target], 15)
        total = init[target] - sbuf[target, 0]
        for slot in range(1, 16):
            total = total - qbuf[target, slot]
        return total

    def spread_out(buffer, phase, height, value):
        buffer[height, me] = value
        for place in others:
            send(
                buffer.at[height, me], buffer.at[height, me], phase + height,
                {"gz": place[0], "row": place[1]},
            )

    def write_out(buffer, phase, out, hbm, height, slot):
        wait_blocks(recv_sem.at[phase + height], 7)
        pieces = exchange([
            buffer[height, octet, pl.ds(parity, 32, stride=2), :]
            for parity in range(2) for octet in range(8)
        ])
        for index in range(16):
            part, m = index // 4, index % 4
            out[pl.ds(height * 512 + part * 128 + m, 32, stride=4), :] = pieces[index]
        rows = pl.ds(height * 512, 512)
        pltpu.make_async_copy(out.at[rows], hbm.at[rows], store_sem.at[slot]).start()

    def chosen(height, distance):
        total = jnp.zeros((PART, LANES), F32)
        for m in range(NODES_HERE):
            a = ancestor[height, distance, m]
            chip = a // NODES_HERE
            slot = ((z + 4 - chip // 4) % 4) * 4 + (y + 4 - chip % 4) % 4
            block = gbuf[height - distance][slot]
            present = stored[height, distance, m]
            for source in range(4):
                here = jnp.where(jnp.logical_and(present, a % NODES_HERE == source), m, -1)
                total = jnp.where(node_of == here, rolled(block, 8 * (m - source)), total)
        return total

    def share_solution(height, value):
        gbuf[height][0] = value
        for offset in OFFSETS:
            slot = offset[0] * 4 + offset[1]
            send(
                gbuf[height].at[0], gbuf[height].at[slot], GATHER + height,
                {"col": column(offset)},
            )

    loads["right"].wait()
    loads["sums"].wait()
    sources = []
    for height in range(4):
        for m in range(NODES_HERE):
            rows = pl.ds(height * 128 + m, 32, stride=4)
            sources.append(jnp.where(g == 0, right[rows, :], 0.0) - sums[rows, :])
    pieces = exchange(sources)
    for parity in range(2):
        for octet in range(8):
            xsend[octet, pl.ds(parity, 32, stride=2), :] = pieces[parity * 8 + octet]
    pl.semaphore_wait(barrier, len(OFFSETS) + len(others))
    for place in others:
        send(
            xsend.at[place[0] * 4 + place[1]], xrecv.at[me], INPUT,
            {"gz": place[0], "row": place[1]},
        )
    lower_send(3)
    xrecv[me] = xsend[me]
    loads["linv3"].wait()

    def widen_top(m, carry):
        top_inv[m] = wide_of(linv[3, m])
        return carry

    lax.fori_loop(0, NODES_HERE, widen_top, 0)
    lower_send(1)
    lower_send(4)
    wait_blocks(recv_sem.at[INPUT], 7)
    sums_of_part = [xrecv[part] + xrecv[4 + part] for part in range(4)]
    quarter = lane_ids(PART) // 32
    for height in (3, 2, 1, 0):
        total = None
        for part in range(4):
            moved = rolled(sums_of_part[part], 32 * (part - height))
            total = moved if total is None else jnp.where(quarter == part, moved, total)
        init[height] = total

    solved = apply(lambda m: top_inv[m], operand_of(init[3]))
    operand3 = operand_of(solved)
    loads["lower"].wait()
    lower_hand(3)
    wait_matrix(lower, L_GZ, 3)
    scatter_terms(3, 1, apply(lambda m: wide_of(lower[3, m]), operand3), True, True)
    spread_out(fbuf, FWD_OUT, 3, solved)
    for q in (0, 2, 5):
        lower_send(q)
    lower_hand(1)
    lower_hand(4)
    loads["linv2"].wait()
    wait_matrix(lower, L_GZ, 1)
    multiply(v21, lambda m: lower[1, m], lambda m: linv[2, m])
    wait_matrix(lower, L_GZ, 4)
    scatter_terms(3, 2, apply(lambda m: wide_of(lower[4, m]), operand3), True, False)

    operand = operand_of(sum_received(2))
    scatter_terms(2, 1, apply(lambda m: v21[m], operand), False, True)
    for q in (0, 2, 1):
        upper_send(q)
    lower_hand(0)
    lower_hand(2)
    lower_hand(5)
    loads["linv1"].wait()
    wait_matrix(lower, L_GZ, 0)
    multiply(v11, lambda m: lower[0, m], lambda m: linv[1, m])
    solved = apply(lambda m: wide_of(linv[2, m]), operand)
    spread_out(fbuf, FWD_OUT, 2, solved)
    wait_matrix(lower, L_GZ, 5)
    scatter_terms(3, 3, apply(lambda m: wide_of(lower[5, m]), operand3), True, False)
    wait_matrix(lower, L_GZ, 2)
    scatter_terms(2, 2, apply(lambda m: wide_of(lower[2, m]), operand_of(solved)), False, False)

    operand = operand_of(sum_received(1))
    scatter_terms(1, 1, apply(lambda m: v11[m], operand), False, True)
    for q in (5, 4, 3):
        upper_send(q)
    solved = apply(lambda m: wide_of(linv[1, m]), operand)
    spread_out(fbuf, FWD_OUT, 1, solved)
    loads["linv0"].wait()
    loads["uinv0"].wait()
    multiply(ul, lambda m: uinv[0, m], lambda m: linv[0, m])
    loads["uinv1"].wait()
    rest1 = apply(lambda m: wide_of(uinv[1, m]), operand_of(solved))
    loads["upper"].wait()
    upper_hand(0)

    operand = operand_of(sum_received(0))
    value = apply(lambda m: ul[m], operand)
    share_solution(0, value)
    spread_out(fbuf, FWD_OUT, 0, apply(lambda m: wide_of(linv[0, m]), operand))
    spread_out(ybuf, BWD_OUT, 0, value)
    wait_matrix(upper, U_GZ, 0)
    multiply(w11, lambda m: uinv[1, m], lambda m: upper[0, m])
    upper_hand(2)
    upper_hand(1)
    write_out(fbuf, FWD_OUT, out_f, fwd_hbm, 3, 0)
    write_out(fbuf, FWD_OUT, out_f, fwd_hbm, 2, 1)

    wait_blocks(recv_sem.at[GATHER + 0], 15)
    value = rest1 - apply(lambda m: w11[m], operand_of(chosen(1, 1)))
    share_solution(1, value)
    spread_out(ybuf, BWD_OUT, 1, value)
    wait_matrix(upper, U_GZ, 1)
    loads["uinv2"].wait()
    multiply(w21, lambda m: uinv[2, m], lambda m: upper[1, m])
    wait_matrix(upper, U_GZ, 2)
    rest = fbuf[2, me] - apply(lambda m: wide_of(upper[2, m]), operand_of(chosen(2, 2)))
    rest2 = apply(lambda m: wide_of(uinv[2, m]), operand_of(rest))
    upper_hand(5)
    write_out(fbuf, FWD_OUT, out_f, fwd_hbm, 1, 2)
    write_out(fbuf, FWD_OUT, out_f, fwd_hbm, 0, 3)

    wait_blocks(recv_sem.at[GATHER + 1], 15)
    value = rest2 - apply(lambda m: w21[m], operand_of(chosen(2, 1)))
    share_solution(2, value)
    spread_out(ybuf, BWD_OUT, 2, value)
    upper_hand(4)
    upper_hand(3)
    wait_matrix(upper, U_GZ, 5)
    rest = fbuf[3, me] - apply(lambda m: wide_of(upper[5, m]), operand_of(chosen(3, 3)))
    wait_matrix(upper, U_GZ, 4)
    rest = rest - apply(lambda m: wide_of(upper[4, m]), operand_of(chosen(3, 2)))
    loads["uinv3"].wait()
    rest3 = apply(lambda m: wide_of(uinv[3, m]), operand_of(rest))
    wait_matrix(upper, U_GZ, 3)
    multiply(w31, lambda m: uinv[3, m], lambda m: upper[3, m])
    write_out(ybuf, BWD_OUT, out_b, bwd_hbm, 0, 4)
    write_out(ybuf, BWD_OUT, out_b, bwd_hbm, 1, 5)

    wait_blocks(recv_sem.at[GATHER + 2], 15)
    value = rest3 - apply(lambda m: w31[m], operand_of(chosen(3, 1)))
    spread_out(ybuf, BWD_OUT, 3, value)
    write_out(ybuf, BWD_OUT, out_b, bwd_hbm, 2, 6)
    write_out(ybuf, BWD_OUT, out_b, bwd_hbm, 3, 7)

    for phase, blocks in (
        [(INPUT, 7)]
        + [(SCATTER + t, 15) for t in range(3)]
        + [(GATHER + t, 15) for t in range(3)]
        + [(FWD_OUT + h, 7) for h in range(4)]
        + [(BWD_OUT + h, 7) for h in range(4)]
    ):
        wait_blocks(send_sem.at[phase], blocks)
    for q in range(6):
        for phase_row, phase_gz in ((L_ROW, L_GZ), (U_ROW, U_GZ)):
            wait_bytes(lower.at[q, pl.ds(0, 2), pl.ds(0, 192), :], send_sem.at[phase_row + q])
            wait_bytes(lower.at[q, pl.ds(0, 2)], send_sem.at[phase_gz + q])
    for slot, (height, out, hbm) in enumerate(
        [(h, out_f, fwd_hbm) for h in (3, 2, 1, 0)] + [(h, out_b, bwd_hbm) for h in (0, 1, 2, 3)]
    ):
        rows = pl.ds(height * 512, 512)
        pltpu.make_async_copy(out.at[rows], hbm.at[rows], store_sem.at[slot]).wait()


def body(
    right_side, layer_sums, lower_blocks, upper_blocks, lower_inverse, upper_diagonal_inverses,
    pattern, parents,
):
    def tiled(x):
        return x.reshape(4, 4, 32, 128).transpose(0, 2, 1, 3).reshape(512, 128)

    anywhere = pl.BlockSpec(memory_space=pl.ANY)
    scalar = pl.BlockSpec(memory_space=pltpu.SMEM)
    forward, backward = pl.pallas_call(
        kernel,
        out_shape=[jax.ShapeDtypeStruct((2048, 128), F32)] * 2,
        in_specs=[anywhere] * 6 + [scalar] * 2,
        out_specs=[anywhere] * 2,
        scratch_shapes=[
            pltpu.VMEM((512, 128), F32),
            pltpu.VMEM((512, 128), F32),
            pltpu.VMEM((6, 4, 256, 256), F32),
            pltpu.VMEM((6, 4, 256, 256), F32),
            pltpu.VMEM((4, 4, 256, 256), F32),
            pltpu.VMEM((4, 4, 256, 256), F32),
            pltpu.VMEM((8, 64, 128), F32),
            pltpu.VMEM((8, 64, 128), F32),
            pltpu.VMEM((4, 64, 128), F32),
            pltpu.VMEM((3, 16, 64, 128), F32),
            pltpu.VMEM((3, 16, 64, 128), F32),
            pltpu.VMEM((16, 64, 128), F32),
            pltpu.VMEM((16, 64, 128), F32),
            pltpu.VMEM((16, 64, 128), F32),
            pltpu.VMEM((4, 8, 64, 128), F32),
            pltpu.VMEM((4, 8, 64, 128), F32),
        ]
        + [pltpu.VMEM((4, 256, 512), BF16)] * 7
        + [
            pltpu.VMEM((2048, 128), F32),
            pltpu.VMEM((2048, 128), F32),
            pltpu.SemaphoreType.DMA((PHASES,)),
            pltpu.SemaphoreType.DMA((PHASES,)),
            pltpu.SemaphoreType.DMA((12,)),
            pltpu.SemaphoreType.DMA((8,)),
        ],
        compiler_params=pltpu.CompilerParams(
            collective_id=0, has_side_effects=True, vmem_limit_bytes=58 * 1024 * 1024
        ),
    )(
        tiled(right_side), tiled(layer_sums[0]), lower_blocks, upper_blocks, lower_inverse,
        upper_diagonal_inverses, pattern.T, parents,
    )

    def untiled(x):
        return x.reshape(4, 128, 4, 128).transpose(0, 2, 1, 3).reshape(4, 4, 16384)

    return untiled(forward), untiled(backward)


def solution(mesh):
    in_specs = (
        P(None, "col", "row"),
        P("gz", None, "col", "row"),
        P(None, "col", "row", None),
        P(None, "col", "row", None),
        P(None, "col", None, None),
        P(None, "col", None, None),
        P(None, "col"),
        P(),
    )
    out_specs = (P(None, "col", None), P(None, "col", None))
    return jax.shard_map(body, mesh=mesh, in_specs=in_specs, out_specs=out_specs, check_vma=False)
```

```python
import jax
import jax.numpy as jnp
from jax import lax
from jax.experimental import pallas as pl
from jax.experimental.pallas import tpu as pltpu
from jax.sharding import PartitionSpec as P

MESH = pl.DeviceIdType.MESH
F32 = jnp.float32
BF16 = jnp.bfloat16
LANES = 128
PART = 64
NODES_HERE = 4
OFFSETS = sorted(
    [(dz, dy) for dz in range(4) for dy in range(4) if dz or dy],
    key=lambda o: -(min(o[0], 4 - o[0]) + min(o[1], 4 - o[1])),
)
INPUT, SCATTER, GATHER, RHS, F_GZ, Y_ROW, Y_GZ, PX = 0, 1, 4, 7, 11, 15, 19, 22
L_NEAR, L_FAR, L_GZ, U_NEAR, U_FAR, U_GZ, PHASES = 25, 28, 31, 34, 40, 46, 52


def place_of(height, distance):
    return height * (height - 1) // 2 + distance - 1


def lane_ids(rows):
    return lax.broadcasted_iota(jnp.int32, (rows, LANES), 1)


def split(x):
    high = x.astype(BF16)
    return high, (x - high.astype(F32)).astype(BF16)


def dot(a, b):
    return jnp.dot(a, b, preferred_element_type=F32)


def wide_of(a):
    return jnp.concatenate(split(a), axis=1)


def rolled(x, lanes):
    lanes = lanes % LANES
    return pltpu.roll(x, lanes, 1) if lanes else x


def operand_of(x):
    full = jnp.concatenate([rolled(x, -8 * part) for part in range(4)], axis=0)
    high = full.astype(BF16).astype(F32)
    low = full - high
    first = (lane_ids(256) // 8) % 4 == 0
    both = jnp.where(first, high, rolled(low.astype(BF16).astype(F32), 8))
    alone = jnp.where(first, high, 0.0)
    return jnp.concatenate([both.astype(BF16), alone.astype(BF16)], axis=0)


def apply(matrix_of, operand):
    node = lane_ids(256) // 32
    total = None
    for m in range(NODES_HERE):
        out = dot(matrix_of(m), operand)
        total = out if total is None else jnp.where(node == m, out, total)
    total = total + rolled(total, -8)
    quarter = (lane_ids(PART) // 8) % 4
    packed = None
    for part in range(4):
        moved = rolled(total[part * PART:(part + 1) * PART], 8 * part)
        packed = moved if packed is None else jnp.where(quarter == part, moved, packed)
    return packed


def pair_of(b):
    high, low = split(b)
    return high, jnp.concatenate([high, low], axis=1)


def product(a, b_pair):
    a_high, a_low = split(a)
    b_high, b_both = b_pair
    wide = dot(a_high, b_both)
    return wide[:, :LANES] + wide[:, LANES:] + dot(a_low, b_high)


def exchange(arrays):
    octet = lane_ids(arrays[0].shape[0]) // 8
    arrays = list(arrays)
    for bit in (1, 2, 4, 8)[: len(arrays).bit_length() - 1]:
        low = (octet // bit) % 2 == 0
        for i in range(len(arrays)):
            if i & bit:
                continue
            a, b = arrays[i], arrays[i | bit]
            arrays[i] = jnp.where(low, a, rolled(b, 8 * bit))
            arrays[i | bit] = jnp.where(low, rolled(a, -8 * bit), b)
    return arrays


def kernel(
    right_hbm, sums_hbm, lower_hbm, upper_hbm, linv_hbm, uinv_hbm, pattern_ref, parents_ref,
    fwd_hbm, bwd_hbm,
    right, sums, lower, lpart, upper, linv, uinv,
    xsend, xrecv, init, sbuf, qbuf, gbuf0, gbuf1, gbuf2, rbuf, pxsend, pxrecv,
    full, fbuf, fown, ybuf, vpart, top_inv, v21, v11, ul, w11, w21, w31, out_f, out_b,
    send_sem, recv_sem, load_sem, store_sem,
):
    g = lax.axis_index("gz")
    r = lax.axis_index("row")
    c = lax.axis_index("col")
    z, y = c // 4, c % 4
    me = g * 4 + r
    gbuf = (gbuf0, gbuf1, gbuf2)

    def column(offset):
        return ((z + offset[0]) % 4) * 4 + (y + offset[1]) % 4

    loads = {}

    def load(name, source, target):
        loads[name] = pltpu.make_async_copy(source, target, load_sem.at[len(loads)])
        loads[name].start()

    my_rows = pl.ds(pl.multiple_of(r * PART, PART), PART)
    my_nodes = pl.ds(g * 2, 2)
    load("right", right_hbm, right)
    load("sums", sums_hbm, sums)
    load("linv3", linv_hbm.at[3], linv.at[3])
    for height in (3, 2, 1):
        load(
            "lower%d" % height, lower_hbm.at[place_of(height, 1), my_nodes],
            lower.at[height - 1, my_nodes, my_rows, :],
        )
        for distance in range(2, height + 1):
            place = height + distance - 4
            load("lpart%d" % place, lower_hbm.at[place_of(height, distance)], lpart.at[place])
    load("linv2", linv_hbm.at[2], linv.at[2])
    load("linv1", linv_hbm.at[1], linv.at[1])
    load("upper", upper_hbm.at[:, my_nodes], upper.at[:, my_nodes, my_rows, :])
    load("linv0", linv_hbm.at[0], linv.at[0])
    for height in (0, 1, 2, 3):
        load("uinv%d" % height, uinv_hbm.at[height], uinv.at[height])

    barrier = pltpu.get_barrier_semaphore()
    for offset in OFFSETS:
        pl.semaphore_signal(
            barrier, inc=1, device_id={"col": column(offset)}, device_id_type=MESH
        )
    row_steps = (2, 1, 3)
    others = []
    for step in (2, 1, 3):
        others.append((g, (r + step) % 4))
        others.append((1 - g, (r + step) % 4))
    others.append((1 - g, r))
    for place in others:
        pl.semaphore_signal(
            barrier, inc=1, device_id={"gz": place[0], "row": place[1]}, device_id_type=MESH
        )

    def send(source, target, phase, place):
        pltpu.make_async_remote_copy(
            src_ref=source, dst_ref=target, send_sem=send_sem.at[phase],
            recv_sem=recv_sem.at[phase], device_id=place, device_id_type=MESH,
        ).start()

    def wait_bytes(whole, sem):
        pltpu.make_async_copy(whole, whole, sem).wait()

    def wait_blocks(sem, blocks):
        wait_bytes(qbuf.at[0, pl.ds(0, blocks)], sem)

    ancestor, stored = {}, {}
    for height in (1, 2, 3):
        for m in range(NODES_HERE):
            current = parents_ref[height - 1, c * NODES_HERE + m]
            for distance in range(1, height + 1):
                if distance > 1:
                    current = parents_ref[height - distance, current]
                ancestor[height, distance, m] = current
                stored[height, distance, m] = pattern_ref[m, place_of(height, distance)] != 0

    node_of = lane_ids(PART) // 32
    right_mate, left_mate = (r + 1) % 4, (r + 3) % 4

    def rows_of(part):
        return pl.ds(pl.multiple_of(part * PART, PART), PART)

    def near(source, q, target, at, phase):
        for mate in (right_mate, left_mate):
            send(
                source.at[q, my_nodes], target.at[at, my_nodes, my_rows, :], phase + at,
                {"row": mate},
            )

    def far(target, at, phase_near, phase_far):
        wait_bytes(upper.at[0, pl.ds(0, 2), pl.ds(0, 128), :], recv_sem.at[phase_near + at])
        for node, part, mate in ((2 * g, left_mate, right_mate), (2 * g + 1, right_mate, left_mate)):
            block = target.at[at, node, rows_of(part), :]
            send(block, block, phase_far + at, {"row": mate})

    def hand(target, at, phase_far, phase_gz):
        wait_bytes(upper.at[0, pl.ds(0, 2), pl.ds(0, 64), :], recv_sem.at[phase_far + at])
        send(target.at[at, my_nodes], target.at[at, my_nodes], phase_gz + at, {"gz": 1 - g})

    def l_near(height):
        near(lower_hbm, place_of(height, 1), lower, height - 1, L_NEAR)

    def l_far(height):
        far(lower, height - 1, L_NEAR, L_FAR)

    def l_hand(height):
        loads["lower%d" % height].wait()
        hand(lower, height - 1, L_FAR, L_GZ)

    def l_wait(height):
        wait_bytes(upper.at[0, pl.ds(0, 2)], recv_sem.at[L_GZ + height - 1])

    def u_near(q):
        near(upper_hbm, q, upper, q, U_NEAR)

    def u_far(q):
        far(upper, q, U_NEAR, U_FAR)

    def u_hand(q):
        hand(upper, q, U_FAR, U_GZ)

    def u_wait(q):
        wait_bytes(upper.at[0, pl.ds(0, 2)], recv_sem.at[U_GZ + q])

    def multiply(target, a_of, b_of):
        def one(m, carry):
            a_high, a_low = split(a_of(m))
            b_high, b_low = split(b_of(m))
            target[m] = wide_of(dot(a_high, b_high) + dot(a_high, b_low) + dot(a_low, b_high))
            return carry
        lax.fori_loop(0, NODES_HERE, one, 0)

    def scatter_terms(height, distance, terms_in, first, out):
        target = height - distance
        moved = {shift: rolled(terms_in, 32 * shift) for shift in range(-3, 4)}
        terms = []
        for m in range(NODES_HERE):
            spread = moved[-m]
            for t in range(1, 4):
                spread = jnp.where(node_of == t, moved[t - m], spread)
            terms.append(spread)
        wanted = [
            jnp.where(stored[height, distance, m], ancestor[height, distance, m], -1)
            for m in range(NODES_HERE)
        ]
        for offset in OFFSETS + [(0, 0)]:
            slot = offset[0] * 4 + offset[1]
            base = column(offset) * NODES_HERE
            total = jnp.zeros((PART, LANES), F32) if first else sbuf[target, slot]
            for m in range(NODES_HERE):
                total = total + jnp.where(node_of == wanted[m] - base, terms[m], 0.0)
            sbuf[target, slot] = total
            if out and slot:
                send(
                    sbuf.at[target, slot], qbuf.at[target, slot], SCATTER + target,
                    {"col": column(offset)},
                )

    def sum_received(target):
        wait_blocks(recv_sem.at[SCATTER + target], 15)
        total = init[target] - sbuf[target, 0]
        for slot in range(1, 16):
            total = total - qbuf[target, slot]
        return total

    def spread_rhs(height, value):
        rbuf[height, r] = value
        for step in row_steps:
            send(
                rbuf.at[height, r], rbuf.at[height, r], RHS + height, {"row": (r + step) % 4}
            )

    def take_rhs(height):
        wait_blocks(recv_sem.at[RHS + height], 3)
        blocks = exchange([rbuf[height, mate] for mate in range(4)])
        return pair_of(jnp.concatenate(blocks, axis=0))

    def make_vpart(height, distance):
        place = height + distance - 4
        q_rows = lpart.at[place]

        def one(m, carry):
            a_high, a_low = split(q_rows[m])
            b_high, b_low = split(linv[height, m])
            vpart[place, m] = dot(a_high, b_high) + dot(a_high, b_low) + dot(a_low, b_high)
            return carry

        lax.fori_loop(0, NODES_HERE, one, 0)

    def send_terms(height, distance, b_pair):
        place = height + distance - 4
        total = None
        for m in range(NODES_HERE):
            out = product(vpart[place, m], b_pair)
            total = out if total is None else jnp.where(node_of == m, out, total)
        pxrecv[place, r] = total
        for step in row_steps:
            moved = jnp.where(r + step < 4, rolled(total, -8 * step), rolled(total, 8 * (4 - step)))
            pxsend[place, step - 1] = moved
            send(
                pxsend.at[place, step - 1], pxrecv.at[place, r], PX + place,
                {"row": (r + step) % 4},
            )

    def take_terms(height, distance):
        place = height + distance - 4
        wait_blocks(recv_sem.at[PX + place], 3)
        quarter = (lane_ids(PART) // 8) % 4
        total = pxrecv[place, 0]
        for part in range(1, 4):
            total = jnp.where(quarter == part, pxrecv[place, part], total)
        return total

    def finish_forward(height, b_pair):
        node = lane_ids(256) // 32

        def one(m, carry):
            full[...] = jnp.where(node == m, product(linv[height, m], b_pair), full[...])
            return carry

        lax.fori_loop(0, NODES_HERE, one, 0)
        fbuf[height, g] = full[...]
        send(fbuf.at[height, g], fbuf.at[height, g], F_GZ + height, {"gz": 1 - g})
        if height:
            own = exchange([full[part * PART:(part + 1) * PART, :] for part in range(4)])
            for mate in range(4):
                fown[height - 1, mate] = own[mate]

    def write_forward(height, slot):
        wait_blocks(recv_sem.at[F_GZ + height], 4)
        group = lane_ids(128) // 32
        pieces = [
            fbuf[height, half, pl.ds(parity, 128, stride=2), :]
            for parity in range(2) for half in range(2)
        ]
        for m in range(NODES_HERE):
            total = None
            for place in range(4):
                moved = rolled(pieces[place], 32 * (place - m))
                total = moved if total is None else jnp.where(group == place, moved, total)
            out_f[pl.ds(height * 512 + m, 128, stride=4), :] = total
        rows = pl.ds(height * 512, 512)
        pltpu.make_async_copy(out_f.at[rows], fwd_hbm.at[rows], store_sem.at[slot]).start()

    my_octets = pl.ds(pl.multiple_of(g * 4, 4), 4)

    def spread_solution(height, value):
        ybuf[height, me] = value
        places = others if height == 3 else [(g, (r + step) % 4) for step in row_steps]
        for place in places:
            send(
                ybuf.at[height, me], ybuf.at[height, me], Y_ROW + height,
                {"gz": place[0], "row": place[1]},
            )

    def hand_solution(height):
        wait_blocks(recv_sem.at[Y_ROW + height], 3)
        send(ybuf.at[height, my_octets], ybuf.at[height, my_octets], Y_GZ + height, {"gz": 1 - g})

    def write_backward(height, slot):
        if height == 3:
            wait_blocks(recv_sem.at[Y_ROW + height], 7)
        else:
            wait_blocks(recv_sem.at[Y_GZ + height], 4)
        pieces = exchange([
            ybuf[height, octet, pl.ds(parity, 32, stride=2), :]
            for parity in range(2) for octet in range(8)
        ])
        for index in range(16):
            m, part = index // 4, index % 4
            out_b[pl.ds(height * 512 + part * 128 + m, 32, stride=4), :] = pieces[index]
        rows = pl.ds(height * 512, 512)
        pltpu.make_async_copy(out_b.at[rows], bwd_hbm.at[rows], store_sem.at[slot]).start()

    def chosen(height, distance):
        total = jnp.zeros((PART, LANES), F32)
        for m in range(NODES_HERE):
            a = ancestor[height, distance, m]
            chip = a // NODES_HERE
            slot = ((z + 4 - chip // 4) % 4) * 4 + (y + 4 - chip % 4) % 4
            block = gbuf[height - distance][slot]
            present = stored[height, distance, m]
            for source in range(4):
                here = jnp.where(jnp.logical_and(present, a % NODES_HERE == source), m, -1)
                total = jnp.where(node_of == here, rolled(block, 32 * (m - source)), total)
        return total

    def share_solution(height, value):
        gbuf[height][0] = value
        for offset in OFFSETS:
            slot = offset[0] * 4 + offset[1]
            send(
                gbuf[height].at[0], gbuf[height].at[slot], GATHER + height,
                {"col": column(offset)},
            )

    loads["right"].wait()
    loads["sums"].wait()
    sources = []
    for m in range(NODES_HERE):
        for height in range(4):
            rows = pl.ds(height * 128 + m, 32, stride=4)
            sources.append(jnp.where(g == 0, right[rows, :], 0.0) - sums[rows, :])
    pieces = exchange(sources)
    for parity in range(2):
        for octet in range(8):
            xsend[octet, pl.ds(parity, 32, stride=2), :] = pieces[parity * 8 + octet]
    pl.semaphore_wait(barrier, len(OFFSETS) + len(others))
    for place in others:
        send(
            xsend.at[place[0] * 4 + place[1]], xrecv.at[me], INPUT,
            {"gz": place[0], "row": place[1]},
        )
    l_near(3)
    xrecv[me] = xsend[me]
    loads["linv3"].wait()

    def widen_top(m, carry):
        top_inv[m] = wide_of(linv[3, m])
        return carry

    lax.fori_loop(0, NODES_HERE, widen_top, 0)
    loads["lpart1"].wait()
    make_vpart(3, 2)
    l_far(3)
    l_near(2)
    wait_blocks(recv_sem.at[INPUT], 7)
    parts = exchange([xrecv[part] + xrecv[4 + part] for part in range(4)])
    for height in range(4):
        init[height] = parts[height]

    spread_rhs(3, init[3])
    l_hand(3)
    operand = operand_of(apply(lambda m: top_inv[m], operand_of(init[3])))
    loads["lpart2"].wait()
    make_vpart(3, 3)
    l_wait(3)
    scatter_terms(3, 1, apply(lambda m: wide_of(lower[2, m]), operand), True, True)
    b_pair = take_rhs(3)
    send_terms(3, 2, b_pair)
    l_far(2)
    send_terms(3, 3, b_pair)
    l_near(1)
    finish_forward(3, b_pair)
    loads["linv2"].wait()
    loads["lpart0"].wait()
    make_vpart(2, 2)
    l_hand(2)
    l_wait(2)
    multiply(v21, lambda m: lower[1, m], lambda m: linv[2, m])
    l_far(1)
    scatter_terms(3, 2, take_terms(3, 2), True, False)

    rhs = sum_received(2)
    spread_rhs(2, rhs)
    scatter_terms(2, 1, apply(lambda m: v21[m], operand_of(rhs)), False, True)
    u_near(0)
    scatter_terms(3, 3, take_terms(3, 3), True, False)
    l_hand(1)
    b_pair = take_rhs(2)
    send_terms(2, 2, b_pair)
    finish_forward(2, b_pair)
    loads["linv1"].wait()
    l_wait(1)
    multiply(v11, lambda m: lower[0, m], lambda m: linv[1, m])
    u_far(0)
    u_near(2)
    scatter_terms(2, 2, take_terms(2, 2), False, False)

    rhs = sum_received(1)
    spread_rhs(1, rhs)
    scatter_terms(1, 1, apply(lambda m: v11[m], operand_of(rhs)), False, True)
    loads["upper"].wait()
    u_hand(0)
    u_far(2)
    u_near(1)
    finish_forward(1, take_rhs(1))
    loads["linv0"].wait()
    loads["uinv0"].wait()
    multiply(ul, lambda m: uinv[0, m], lambda m: linv[0, m])
    loads["uinv1"].wait()
    rest1 = apply(lambda m: wide_of(uinv[1, m]), operand_of(fown[0, r]))
    u_hand(2)
    u_far(1)
    u_near(5)
    u_wait(0)
    multiply(w11, lambda m: uinv[1, m], lambda m: upper[0, m])

    rhs = sum_received(0)
    value = apply(lambda m: ul[m], operand_of(rhs))
    share_solution(0, value)
    spread_rhs(0, rhs)
    spread_solution(0, value)
    u_hand(1)
    u_far(5)
    u_near(4)
    finish_forward(0, take_rhs(0))
    hand_solution(0)
    u_wait(1)
    loads["uinv2"].wait()
    multiply(w21, lambda m: uinv[2, m], lambda m: upper[1, m])
    write_forward(3, 0)

    wait_blocks(recv_sem.at[GATHER + 0], 15)
    value = rest1 - apply(lambda m: w11[m], operand_of(chosen(1, 1)))
    share_solution(1, value)
    u_far(4)
    u_near(3)
    spread_solution(1, value)
    u_wait(2)
    rest = fown[1, r] - apply(lambda m: wide_of(upper[2, m]), operand_of(chosen(2, 2)))
    rest2 = apply(lambda m: wide_of(uinv[2, m]), operand_of(rest))
    u_hand(5)
    u_hand(4)
    u_far(3)
    write_forward(2, 1)
    hand_solution(1)

    wait_blocks(recv_sem.at[GATHER + 1], 15)
    value = rest2 - apply(lambda m: w21[m], operand_of(chosen(2, 1)))
    share_solution(2, value)
    spread_solution(2, value)
    u_hand(3)
    u_wait(5)
    rest = fown[2, r] - apply(lambda m: wide_of(upper[5, m]), operand_of(chosen(3, 3)))
    u_wait(4)
    rest = rest - apply(lambda m: wide_of(upper[4, m]), operand_of(chosen(3, 2)))
    loads["uinv3"].wait()
    rest3 = apply(lambda m: wide_of(uinv[3, m]), operand_of(rest))
    u_wait(3)
    multiply(w31, lambda m: uinv[3, m], lambda m: upper[3, m])
    hand_solution(2)

    wait_blocks(recv_sem.at[GATHER + 2], 15)
    value = rest3 - apply(lambda m: w31[m], operand_of(chosen(3, 1)))
    spread_solution(3, value)
    write_forward(1, 2)
    write_forward(0, 3)
    write_backward(0, 4)
    write_backward(1, 5)
    write_backward(2, 6)
    write_backward(3, 7)

    for phase, blocks in (
        [(INPUT, 7)]
        + [(SCATTER + t, 15) for t in range(3)]
        + [(GATHER + t, 15) for t in range(3)]
        + [(RHS + h, 3) for h in range(4)]
        + [(F_GZ + h, 4) for h in range(4)]
        + [(Y_ROW + h, 7 if h == 3 else 3) for h in range(4)]
        + [(Y_GZ + h, 4) for h in range(3)]
        + [(PX + p, 3) for p in range(3)]
        + [(L_NEAR + p, 8) for p in range(3)]
        + [(L_FAR + p, 4) for p in range(3)]
        + [(L_GZ + p, 16) for p in range(3)]
        + [(U_NEAR + p, 8) for p in range(6)]
        + [(U_FAR + p, 4) for p in range(6)]
        + [(U_GZ + p, 16) for p in range(6)]
    ):
        wait_blocks(send_sem.at[phase], blocks)
    for slot, (height, out, hbm) in enumerate(
        [(h, out_f, fwd_hbm) for h in (3, 2, 1, 0)] + [(h, out_b, bwd_hbm) for h in (0, 1, 2, 3)]
    ):
        rows = pl.ds(height * 512, 512)
        pltpu.make_async_copy(out.at[rows], hbm.at[rows], store_sem.at[slot]).wait()


def body(
    right_side, layer_sums, lower_blocks, upper_blocks, lower_inverse, upper_diagonal_inverses,
    pattern, parents,
):
    def tiled(x):
        return x.reshape(4, 4, 32, 128).transpose(0, 2, 1, 3).reshape(512, 128)

    anywhere = pl.BlockSpec(memory_space=pl.ANY)
    scalar = pl.BlockSpec(memory_space=pltpu.SMEM)
    forward, backward = pl.pallas_call(
        kernel,
        out_shape=[jax.ShapeDtypeStruct((2048, 128), F32)] * 2,
        in_specs=[anywhere] * 6 + [scalar] * 2,
        out_specs=[anywhere] * 2,
        scratch_shapes=[
            pltpu.VMEM((512, 128), F32),
            pltpu.VMEM((512, 128), F32),
            pltpu.VMEM((3, 4, 256, 256), F32),
            pltpu.VMEM((3, 4, 64, 256), F32),
            pltpu.VMEM((6, 4, 256, 256), F32),
            pltpu.VMEM((4, 4, 256, 256), F32),
            pltpu.VMEM((4, 4, 256, 256), F32),
            pltpu.VMEM((8, 64, 128), F32),
            pltpu.VMEM((8, 64, 128), F32),
            pltpu.VMEM((4, 64, 128), F32),
            pltpu.VMEM((3, 16, 64, 128), F32),
            pltpu.VMEM((3, 16, 64, 128), F32),
            pltpu.VMEM((16, 64, 128), F32),
            pltpu.VMEM((16, 64, 128), F32),
            pltpu.VMEM((16, 64, 128), F32),
            pltpu.VMEM((4, 4, 64, 128), F32),
            pltpu.VMEM((3, 3, 64, 128), F32),
            pltpu.VMEM((3, 4, 64, 128), F32),
            pltpu.VMEM((256, 128), F32),
            pltpu.VMEM((4, 2, 256, 128), F32),
            pltpu.VMEM((3, 4, 64, 128), F32),
            pltpu.VMEM((4, 8, 64, 128), F32),
            pltpu.VMEM((3, 4, 64, 256), F32),
        ]
        + [pltpu.VMEM((4, 256, 512), BF16)] * 7
        + [
            pltpu.VMEM((2048, 128), F32),
            pltpu.VMEM((2048, 128), F32),
            pltpu.SemaphoreType.DMA((PHASES,)),
            pltpu.SemaphoreType.DMA((PHASES,)),
            pltpu.SemaphoreType.DMA((20,)),
            pltpu.SemaphoreType.DMA((8,)),
        ],
        compiler_params=pltpu.CompilerParams(
            collective_id=0, has_side_effects=True, vmem_limit_bytes=58 * 1024 * 1024
        ),
    )(
        tiled(right_side), tiled(layer_sums[0]), lower_blocks, upper_blocks, lower_inverse,
        upper_diagonal_inverses, pattern.T, parents,
    )

    def untiled(x):
        return x.reshape(4, 128, 4, 128).transpose(0, 2, 1, 3).reshape(4, 4, 16384)

    return untiled(forward), untiled(backward)


def solution(mesh):
    in_specs = (
        P(None, "col", "row"),
        P("gz", None, "col", "row"),
        P(None, "col", "row", None),
        P(None, "col", "row", None),
        P(None, "col", None, None),
        P(None, "col", None, None),
        P(None, "col"),
        P(),
    )
    out_specs = (P(None, "col", None), P(None, "col", None))
    return jax.shard_map(body, mesh=mesh, in_specs=in_specs, out_specs=out_specs, check_vma=False)
```

```python
import jax
import jax.numpy as jnp
from jax import lax
from jax.experimental import pallas as pl
from jax.experimental.pallas import tpu as pltpu
from jax.sharding import PartitionSpec as P

MESH = pl.DeviceIdType.MESH
F32 = jnp.float32
BF16 = jnp.bfloat16
LANES = 128
PART = 64
NODES_HERE = 4
OFFSETS = sorted(
    [(dz, dy) for dz in range(4) for dy in range(4) if dz or dy],
    key=lambda o: -(min(o[0], 4 - o[0]) + min(o[1], 4 - o[1])),
)
INPUT, SCATTER, GATHER, RHS, F_GZ, Y_ROW, Y_GZ, PX = 0, 1, 4, 7, 11, 15, 19, 22
L_NEAR, L_FAR, L_GZ, U_NEAR, U_FAR, U_GZ, TOP_IN, NEXT_IN, PHASES = 25, 28, 31, 34, 40, 46, 52, 53, 54


def place_of(height, distance):
    return height * (height - 1) // 2 + distance - 1


def lane_ids(rows):
    return lax.broadcasted_iota(jnp.int32, (rows, LANES), 1)


def split(x):
    high = x.astype(BF16)
    return high, (x - high.astype(F32)).astype(BF16)


def dot(a, b):
    return jnp.dot(a, b, preferred_element_type=F32)


def wide_of(a):
    return jnp.concatenate(split(a), axis=1)


def rolled(x, lanes):
    lanes = lanes % LANES
    return pltpu.roll(x, lanes, 1) if lanes else x


def operand_of(x):
    full = jnp.concatenate([rolled(x, -8 * part) for part in range(4)], axis=0)
    high = full.astype(BF16).astype(F32)
    low = full - high
    first = (lane_ids(256) // 8) % 4 == 0
    both = jnp.where(first, high, rolled(low.astype(BF16).astype(F32), 8))
    alone = jnp.where(first, high, 0.0)
    return jnp.concatenate([both.astype(BF16), alone.astype(BF16)], axis=0)


def apply(matrix_of, operand):
    node = lane_ids(256) // 32
    total = None
    for m in range(NODES_HERE):
        out = dot(matrix_of(m), operand)
        total = out if total is None else jnp.where(node == m, out, total)
    total = total + rolled(total, -8)
    quarter = (lane_ids(PART) // 8) % 4
    packed = None
    for part in range(4):
        moved = rolled(total[part * PART:(part + 1) * PART], 8 * part)
        packed = moved if packed is None else jnp.where(quarter == part, moved, packed)
    return packed


def pair_of(b):
    high, low = split(b)
    return high, jnp.concatenate([high, low], axis=1)


def product(a, b_pair):
    a_high, a_low = split(a)
    b_high, b_both = b_pair
    wide = dot(a_high, b_both)
    return wide[:, :LANES] + wide[:, LANES:] + dot(a_low, b_high)


def exchange(arrays):
    octet = lane_ids(arrays[0].shape[0]) // 8
    arrays = list(arrays)
    for bit in (1, 2, 4, 8)[: len(arrays).bit_length() - 1]:
        low = (octet // bit) % 2 == 0
        for i in range(len(arrays)):
            if i & bit:
                continue
            a, b = arrays[i], arrays[i | bit]
            arrays[i] = jnp.where(low, a, rolled(b, 8 * bit))
            arrays[i | bit] = jnp.where(low, rolled(a, -8 * bit), b)
    return arrays


def kernel(
    right_hbm, sums_hbm, lower_hbm, upper_hbm, linv_hbm, uinv_hbm, pattern_ref, parents_ref,
    fwd_hbm, bwd_hbm,
    right, sums, lower, lpart, upper, linv, uinv,
    topsend, toprecv, nextsend, nextrecv, xsend, xrecv, init, sbuf, qbuf, gbuf0, gbuf1, gbuf2, rbuf, pxsend, pxrecv,
    full, fbuf, fown, ybuf, vpart, ownrhs, v21, v11, ul, w11, w21, w31, out_f, out_b,
    send_sem, recv_sem, load_sem, store_sem,
):
    g = lax.axis_index("gz")
    r = lax.axis_index("row")
    c = lax.axis_index("col")
    z, y = c // 4, c % 4
    me = g * 4 + r
    gbuf = (gbuf0, gbuf1, gbuf2)

    def column(offset):
        return ((z + offset[0]) % 4) * 4 + (y + offset[1]) % 4

    loads = {}

    def load(name, source, target):
        loads[name] = pltpu.make_async_copy(source, target, load_sem.at[len(loads)])
        loads[name].start()

    my_rows = pl.ds(pl.multiple_of(r * PART, PART), PART)
    my_nodes = pl.ds(g * 2, 2)
    load("right", right_hbm, right)
    load("sums", sums_hbm, sums)
    load("linv3", linv_hbm.at[3], linv.at[3])
    for height in (3, 2, 1):
        if height < 3:
            load(
                "lower%d" % height, lower_hbm.at[place_of(height, 1), my_nodes],
                lower.at[height - 1, my_nodes, my_rows, :],
            )
        else:
            load("lpart3", lower_hbm.at[place_of(3, 1)], lpart.at[3])
        for distance in range(2, height + 1):
            place = height + distance - 4
            load("lpart%d" % place, lower_hbm.at[place_of(height, distance)], lpart.at[place])
    load("linv2", linv_hbm.at[2], linv.at[2])
    load("linv1", linv_hbm.at[1], linv.at[1])
    load("upper", upper_hbm.at[:, my_nodes], upper.at[:, my_nodes, my_rows, :])
    load("linv0", linv_hbm.at[0], linv.at[0])
    for height in (0, 1, 2, 3):
        load("uinv%d" % height, uinv_hbm.at[height], uinv.at[height])

    barrier = pltpu.get_barrier_semaphore()
    for offset in OFFSETS:
        pl.semaphore_signal(
            barrier, inc=1, device_id={"col": column(offset)}, device_id_type=MESH
        )
    row_steps = (2, 1, 3)
    others = []
    for step in (2, 1, 3):
        others.append((g, (r + step) % 4))
        others.append((1 - g, (r + step) % 4))
    others.append((1 - g, r))
    for place in others:
        pl.semaphore_signal(
            barrier, inc=1, device_id={"gz": place[0], "row": place[1]}, device_id_type=MESH
        )

    def send(source, target, phase, place):
        pltpu.make_async_remote_copy(
            src_ref=source, dst_ref=target, send_sem=send_sem.at[phase],
            recv_sem=recv_sem.at[phase], device_id=place, device_id_type=MESH,
        ).start()

    def wait_bytes(whole, sem):
        pltpu.make_async_copy(whole, whole, sem).wait()

    def wait_blocks(sem, blocks):
        wait_bytes(qbuf.at[0, pl.ds(0, blocks)], sem)

    ancestor, stored = {}, {}
    for height in (1, 2, 3):
        for m in range(NODES_HERE):
            current = parents_ref[height - 1, c * NODES_HERE + m]
            for distance in range(1, height + 1):
                if distance > 1:
                    current = parents_ref[height - distance, current]
                ancestor[height, distance, m] = current
                stored[height, distance, m] = pattern_ref[m, place_of(height, distance)] != 0

    node_of = lane_ids(PART) // 32
    right_mate, left_mate = (r + 1) % 4, (r + 3) % 4

    def rows_of(part):
        return pl.ds(pl.multiple_of(part * PART, PART), PART)

    def near(source, q, target, at, phase):
        for mate in (right_mate, left_mate):
            send(
                source.at[q, my_nodes], target.at[at, my_nodes, my_rows, :], phase + at,
                {"row": mate},
            )

    def far(target, at, phase_near, phase_far):
        wait_bytes(upper.at[0, pl.ds(0, 2), pl.ds(0, 128), :], recv_sem.at[phase_near + at])
        for node, part, mate in ((2 * g, left_mate, right_mate), (2 * g + 1, right_mate, left_mate)):
            block = target.at[at, node, rows_of(part), :]
            send(block, block, phase_far + at, {"row": mate})

    def hand(target, at, phase_far, phase_gz):
        wait_bytes(upper.at[0, pl.ds(0, 2), pl.ds(0, 64), :], recv_sem.at[phase_far + at])
        send(target.at[at, my_nodes], target.at[at, my_nodes], phase_gz + at, {"gz": 1 - g})

    def l_near(height):
        near(lower_hbm, place_of(height, 1), lower, height - 1, L_NEAR)

    def l_far(height):
        far(lower, height - 1, L_NEAR, L_FAR)

    def l_hand(height):
        loads["lower%d" % height].wait()
        hand(lower, height - 1, L_FAR, L_GZ)

    def l_wait(height):
        wait_bytes(upper.at[0, pl.ds(0, 2)], recv_sem.at[L_GZ + height - 1])

    def u_near(q):
        near(upper_hbm, q, upper, q, U_NEAR)

    def u_far(q):
        far(upper, q, U_NEAR, U_FAR)

    def u_hand(q):
        hand(upper, q, U_FAR, U_GZ)

    def u_wait(q):
        wait_bytes(upper.at[0, pl.ds(0, 2)], recv_sem.at[U_GZ + q])

    def multiply(target, a_of, b_of):
        def one(m, carry):
            a_high, a_low = split(a_of(m))
            b_high, b_low = split(b_of(m))
            target[m] = wide_of(dot(a_high, b_high) + dot(a_high, b_low) + dot(a_low, b_high))
            return carry
        lax.fori_loop(0, NODES_HERE, one, 0)

    def scatter_terms(height, distance, terms_in, first, out):
        target = height - distance
        moved = {shift: rolled(terms_in, 32 * shift) for shift in range(-3, 4)}
        terms = []
        for m in range(NODES_HERE):
            spread = moved[-m]
            for t in range(1, 4):
                spread = jnp.where(node_of == t, moved[t - m], spread)
            terms.append(spread)
        wanted = [
            jnp.where(stored[height, distance, m], ancestor[height, distance, m], -1)
            for m in range(NODES_HERE)
        ]
        for offset in OFFSETS + [(0, 0)]:
            slot = offset[0] * 4 + offset[1]
            base = column(offset) * NODES_HERE
            total = jnp.zeros((PART, LANES), F32) if first else sbuf[target, slot]
            for m in range(NODES_HERE):
                total = total + jnp.where(node_of == wanted[m] - base, terms[m], 0.0)
            sbuf[target, slot] = total
            if out and slot:
                send(
                    sbuf.at[target, slot], qbuf.at[target, slot], SCATTER + target,
                    {"col": column(offset)},
                )

    def sum_received(target):
        wait_blocks(recv_sem.at[SCATTER + target], 15)
        total = init[target] - sbuf[target, 0]
        for slot in range(1, 16):
            total = total - qbuf[target, slot]
        return total

    def spread_rhs(height, value):
        rbuf[height, r] = value
        for step in row_steps:
            send(
                rbuf.at[height, r], rbuf.at[height, r], RHS + height, {"row": (r + step) % 4}
            )

    def take_rhs(height):
        wait_blocks(recv_sem.at[RHS + height], 3)
        blocks = [rbuf[height, mate] for mate in range(4)]
        if height == 2:
            own = exchange(blocks)
            for mate in range(4):
                ownrhs[mate] = own[mate]
        else:
            blocks = exchange(blocks)
        return pair_of(jnp.concatenate(blocks, axis=0))

    def make_vpart(height, distance):
        place = 3 if distance == 1 else height + distance - 4
        q_rows = lpart.at[place]

        def one(m, carry):
            a_high, a_low = split(q_rows[m])
            b_high, b_low = split(linv[height, m])
            vpart[place, m] = dot(a_high, b_high) + dot(a_high, b_low) + dot(a_low, b_high)
            return carry

        lax.fori_loop(0, NODES_HERE, one, 0)

    def part_terms(place, b_pair):
        total = None
        for m in range(NODES_HERE):
            out = product(vpart[place, m], b_pair)
            total = out if total is None else jnp.where(node_of == m, out, total)
        return total

    def send_terms(height, distance, b_pair):
        place = height + distance - 4
        total = part_terms(place, b_pair)
        pxrecv[place, r] = total
        for step in row_steps:
            moved = jnp.where(r + step < 4, rolled(total, -8 * step), rolled(total, 8 * (4 - step)))
            pxsend[place, step - 1] = moved
            send(
                pxsend.at[place, step - 1], pxrecv.at[place, r], PX + place,
                {"row": (r + step) % 4},
            )

    def take_terms(height, distance):
        place = height + distance - 4
        wait_blocks(recv_sem.at[PX + place], 3)
        quarter = (lane_ids(PART) // 8) % 4
        total = pxrecv[place, 0]
        for part in range(1, 4):
            total = jnp.where(quarter == part, pxrecv[place, part], total)
        return total

    def finish_forward(height, b_pair):
        node = lane_ids(256) // 32

        def one(m, carry):
            full[...] = jnp.where(node == m, product(linv[height, m], b_pair), full[...])
            return carry

        lax.fori_loop(0, NODES_HERE, one, 0)
        fbuf[height, g] = full[...]
        send(fbuf.at[height, g], fbuf.at[height, g], F_GZ + height, {"gz": 1 - g})
        if height:
            own = exchange([full[part * PART:(part + 1) * PART, :] for part in range(4)])
            for mate in range(4):
                fown[height - 1, mate] = own[mate]

    def write_forward(height, slot):
        wait_blocks(recv_sem.at[F_GZ + height], 4)
        group = lane_ids(128) // 32
        pieces = [
            fbuf[height, half, pl.ds(parity, 128, stride=2), :]
            for parity in range(2) for half in range(2)
        ]
        for m in range(NODES_HERE):
            total = None
            for place in range(4):
                moved = rolled(pieces[place], 32 * (place - m))
                total = moved if total is None else jnp.where(group == place, moved, total)
            out_f[pl.ds(height * 512 + m, 128, stride=4), :] = total
        rows = pl.ds(height * 512, 512)
        pltpu.make_async_copy(out_f.at[rows], fwd_hbm.at[rows], store_sem.at[slot]).start()

    my_octets = pl.ds(pl.multiple_of(g * 4, 4), 4)

    def spread_solution(height, value):
        ybuf[height, me] = value
        places = others if height == 3 else [(g, (r + step) % 4) for step in row_steps]
        for place in places:
            send(
                ybuf.at[height, me], ybuf.at[height, me], Y_ROW + height,
                {"gz": place[0], "row": place[1]},
            )

    def hand_solution(height):
        wait_blocks(recv_sem.at[Y_ROW + height], 3)
        send(ybuf.at[height, my_octets], ybuf.at[height, my_octets], Y_GZ + height, {"gz": 1 - g})

    def write_backward(height, slot):
        if height == 3:
            wait_blocks(recv_sem.at[Y_ROW + height], 7)
        else:
            wait_blocks(recv_sem.at[Y_GZ + height], 4)
        pieces = exchange([
            ybuf[height, octet, pl.ds(parity, 32, stride=2), :]
            for parity in range(2) for octet in range(8)
        ])
        for index in range(16):
            m, part = index // 4, index % 4
            out_b[pl.ds(height * 512 + part * 128 + m, 32, stride=4), :] = pieces[index]
        rows = pl.ds(height * 512, 512)
        pltpu.make_async_copy(out_b.at[rows], bwd_hbm.at[rows], store_sem.at[slot]).start()

    def chosen(height, distance):
        total = jnp.zeros((PART, LANES), F32)
        for m in range(NODES_HERE):
            a = ancestor[height, distance, m]
            chip = a // NODES_HERE
            slot = ((z + 4 - chip // 4) % 4) * 4 + (y + 4 - chip % 4) % 4
            block = gbuf[height - distance][slot]
            present = stored[height, distance, m]
            for source in range(4):
                here = jnp.where(jnp.logical_and(present, a % NODES_HERE == source), m, -1)
                total = jnp.where(node_of == here, rolled(block, 32 * (m - source)), total)
        return total

    def share_solution(height, value):
        gbuf[height][0] = value
        for offset in OFFSETS:
            slot = offset[0] * 4 + offset[1]
            send(
                gbuf[height].at[0], gbuf[height].at[slot], GATHER + height,
                {"col": column(offset)},
            )

    loads["right"].wait()
    loads["sums"].wait()

    def source_of(height, m):
        rows = pl.ds(height * 128 + m, 32, stride=4)
        return jnp.where(g == 0, right[rows, :], 0.0) - sums[rows, :]

    group32 = lane_ids(32) // 32

    def half_of(blocks, parity, half):
        total = None
        for m in range(NODES_HERE):
            moved = rolled(blocks[m], 32 * (m - 2 * parity - half))
            total = moved if total is None else jnp.where(group32 == m, moved, total)
        return total

    for height in (3, 2):
        blocks = [source_of(height, m) for m in range(NODES_HERE)]
        for parity in range(2):
            rows = pl.ds(parity, 32, stride=2)
            halves = [half_of(blocks, parity, half) for half in range(2)]
            if height == 3:
                topsend[0, rows, :] = halves[0]
                topsend[1, rows, :] = halves[1]
            else:
                init[2, rows, :] = jnp.where(g == 0, halves[0], halves[1])
                nextsend[rows, :] = jnp.where(g == 0, halves[1], halves[0])
    toprecv[me] = topsend[g]
    pl.semaphore_wait(barrier, len(OFFSETS) + len(others))
    for place in others:
        send(
            topsend.at[place[0]], toprecv.at[me], TOP_IN, {"gz": place[0], "row": place[1]},
        )
    send(nextsend, nextrecv, NEXT_IN, {"gz": 1 - g})
    l_near(2)
    loads["linv3"].wait()
    loads["lpart3"].wait()
    make_vpart(3, 1)
    loads["lpart1"].wait()
    make_vpart(3, 2)
    wait_blocks(recv_sem.at[TOP_IN], 7)

    b_pair = pair_of(jnp.concatenate([toprecv[part] + toprecv[4 + part] for part in range(4)], axis=0))
    scatter_terms(3, 1, part_terms(3, b_pair), True, True)
    send_terms(3, 2, b_pair)
    l_far(2)
    loads["lpart2"].wait()
    make_vpart(3, 3)
    send_terms(3, 3, b_pair)
    pieces = exchange([source_of(height, m) for m in range(NODES_HERE) for height in range(4)])
    for parity in range(2):
        for octet in range(8):
            xsend[octet, pl.ds(parity, 32, stride=2), :] = pieces[parity * 8 + octet]
    for place in others:
        send(
            xsend.at[place[0] * 4 + place[1]], xrecv.at[me], INPUT,
            {"gz": place[0], "row": place[1]},
        )
    xrecv[me] = xsend[me]
    l_near(1)
    l_hand(2)
    finish_forward(3, b_pair)
    loads["linv2"].wait()
    loads["lpart0"].wait()
    make_vpart(2, 2)
    wait_blocks(recv_sem.at[NEXT_IN], 1)
    init[2] = init[2] + nextrecv[...]
    l_wait(2)
    multiply(v21, lambda m: lower[1, m], lambda m: linv[2, m])
    scatter_terms(3, 2, take_terms(3, 2), True, False)

    spread_rhs(2, sum_received(2))
    l_far(1)
    scatter_terms(3, 3, take_terms(3, 3), True, False)
    wait_blocks(recv_sem.at[INPUT], 7)
    parts = exchange([xrecv[part] + xrecv[4 + part] for part in range(4)])
    for height in range(2):
        init[height] = parts[height]
    b_pair = take_rhs(2)
    scatter_terms(2, 1, apply(lambda m: v21[m], operand_of(ownrhs[r])), False, True)
    send_terms(2, 2, b_pair)
    u_near(0)
    l_hand(1)
    finish_forward(2, b_pair)
    loads["linv1"].wait()
    l_wait(1)
    multiply(v11, lambda m: lower[0, m], lambda m: linv[1, m])
    u_far(0)
    u_near(2)
    scatter_terms(2, 2, take_terms(2, 2), False, False)

    rhs = sum_received(1)
    spread_rhs(1, rhs)
    scatter_terms(1, 1, apply(lambda m: v11[m], operand_of(rhs)), False, True)
    loads["upper"].wait()
    u_hand(0)
    u_far(2)
    u_near(1)
    finish_forward(1, take_rhs(1))
    loads["linv0"].wait()
    loads["uinv0"].wait()
    multiply(ul, lambda m: uinv[0, m], lambda m: linv[0, m])
    loads["uinv1"].wait()
    rest1 = apply(lambda m: wide_of(uinv[1, m]), operand_of(fown[0, r]))
    u_hand(2)
    u_far(1)
    u_near(5)
    u_wait(0)
    multiply(w11, lambda m: uinv[1, m], lambda m: upper[0, m])

    rhs = sum_received(0)
    value = apply(lambda m: ul[m], operand_of(rhs))
    share_solution(0, value)
    spread_rhs(0, rhs)
    spread_solution(0, value)
    u_hand(1)
    u_far(5)
    u_near(4)
    finish_forward(0, take_rhs(0))
    hand_solution(0)
    u_wait(1)
    loads["uinv2"].wait()
    multiply(w21, lambda m: uinv[2, m], lambda m: upper[1, m])
    write_forward(3, 0)

    wait_blocks(recv_sem.at[GATHER + 0], 15)
    value = rest1 - apply(lambda m: w11[m], operand_of(chosen(1, 1)))
    share_solution(1, value)
    u_far(4)
    u_near(3)
    spread_solution(1, value)
    u_wait(2)
    rest = fown[1, r] - apply(lambda m: wide_of(upper[2, m]), operand_of(chosen(2, 2)))
    rest2 = apply(lambda m: wide_of(uinv[2, m]), operand_of(rest))
    u_hand(5)
    u_hand(4)
    u_far(3)
    write_forward(2, 1)
    hand_solution(1)

    wait_blocks(recv_sem.at[GATHER + 1], 15)
    value = rest2 - apply(lambda m: w21[m], operand_of(chosen(2, 1)))
    share_solution(2, value)
    spread_solution(2, value)
    u_hand(3)
    u_wait(5)
    rest = fown[2, r] - apply(lambda m: wide_of(upper[5, m]), operand_of(chosen(3, 3)))
    u_wait(4)
    rest = rest - apply(lambda m: wide_of(upper[4, m]), operand_of(chosen(3, 2)))
    loads["uinv3"].wait()
    rest3 = apply(lambda m: wide_of(uinv[3, m]), operand_of(rest))
    u_wait(3)
    multiply(w31, lambda m: uinv[3, m], lambda m: upper[3, m])
    hand_solution(2)

    wait_blocks(recv_sem.at[GATHER + 2], 15)
    value = rest3 - apply(lambda m: w31[m], operand_of(chosen(3, 1)))
    spread_solution(3, value)
    write_forward(1, 2)
    write_forward(0, 3)
    write_backward(0, 4)
    write_backward(1, 5)
    write_backward(2, 6)
    write_backward(3, 7)

    for phase, blocks in (
        [(INPUT, 7), (TOP_IN, 7), (NEXT_IN, 1)]
        + [(SCATTER + t, 15) for t in range(3)]
        + [(GATHER + t, 15) for t in range(3)]
        + [(RHS + h, 3) for h in range(3)]
        + [(F_GZ + h, 4) for h in range(4)]
        + [(Y_ROW + h, 7 if h == 3 else 3) for h in range(4)]
        + [(Y_GZ + h, 4) for h in range(3)]
        + [(PX + p, 3) for p in range(3)]
        + [(L_NEAR + p, 8) for p in range(2)]
        + [(L_FAR + p, 4) for p in range(2)]
        + [(L_GZ + p, 16) for p in range(2)]
        + [(U_NEAR + p, 8) for p in range(6)]
        + [(U_FAR + p, 4) for p in range(6)]
        + [(U_GZ + p, 16) for p in range(6)]
    ):
        wait_blocks(send_sem.at[phase], blocks)
    for slot, (height, out, hbm) in enumerate(
        [(h, out_f, fwd_hbm) for h in (3, 2, 1, 0)] + [(h, out_b, bwd_hbm) for h in (0, 1, 2, 3)]
    ):
        rows = pl.ds(height * 512, 512)
        pltpu.make_async_copy(out.at[rows], hbm.at[rows], store_sem.at[slot]).wait()


def body(
    right_side, layer_sums, lower_blocks, upper_blocks, lower_inverse, upper_diagonal_inverses,
    pattern, parents,
):
    def tiled(x):
        return x.reshape(4, 4, 32, 128).transpose(0, 2, 1, 3).reshape(512, 128)

    anywhere = pl.BlockSpec(memory_space=pl.ANY)
    scalar = pl.BlockSpec(memory_space=pltpu.SMEM)
    forward, backward = pl.pallas_call(
        kernel,
        out_shape=[jax.ShapeDtypeStruct((2048, 128), F32)] * 2,
        in_specs=[anywhere] * 6 + [scalar] * 2,
        out_specs=[anywhere] * 2,
        scratch_shapes=[
            pltpu.VMEM((512, 128), F32),
            pltpu.VMEM((512, 128), F32),
            pltpu.VMEM((2, 4, 256, 256), F32),
            pltpu.VMEM((4, 4, 64, 256), F32),
            pltpu.VMEM((6, 4, 256, 256), F32),
            pltpu.VMEM((4, 4, 256, 256), F32),
            pltpu.VMEM((4, 4, 256, 256), F32),
            pltpu.VMEM((2, 64, 128), F32),
            pltpu.VMEM((8, 64, 128), F32),
            pltpu.VMEM((64, 128), F32),
            pltpu.VMEM((64, 128), F32),
            pltpu.VMEM((8, 64, 128), F32),
            pltpu.VMEM((8, 64, 128), F32),
            pltpu.VMEM((4, 64, 128), F32),
            pltpu.VMEM((3, 16, 64, 128), F32),
            pltpu.VMEM((3, 16, 64, 128), F32),
            pltpu.VMEM((16, 64, 128), F32),
            pltpu.VMEM((16, 64, 128), F32),
            pltpu.VMEM((16, 64, 128), F32),
            pltpu.VMEM((3, 4, 64, 128), F32),
            pltpu.VMEM((3, 3, 64, 128), F32),
            pltpu.VMEM((3, 4, 64, 128), F32),
            pltpu.VMEM((256, 128), F32),
            pltpu.VMEM((4, 2, 256, 128), F32),
            pltpu.VMEM((3, 4, 64, 128), F32),
            pltpu.VMEM((4, 8, 64, 128), F32),
            pltpu.VMEM((4, 4, 64, 256), F32),
            pltpu.VMEM((4, 64, 128), F32),
        ]
        + [pltpu.VMEM((4, 256, 512), BF16)] * 6
        + [
            pltpu.VMEM((2048, 128), F32),
            pltpu.VMEM((2048, 128), F32),
            pltpu.SemaphoreType.DMA((PHASES,)),
            pltpu.SemaphoreType.DMA((PHASES,)),
            pltpu.SemaphoreType.DMA((20,)),
            pltpu.SemaphoreType.DMA((8,)),
        ],
        compiler_params=pltpu.CompilerParams(
            collective_id=0, has_side_effects=True, vmem_limit_bytes=58 * 1024 * 1024
        ),
    )(
        tiled(right_side), tiled(layer_sums[0]), lower_blocks, upper_blocks, lower_inverse,
        upper_diagonal_inverses, pattern.T, parents,
    )

    def untiled(x):
        return x.reshape(4, 128, 4, 128).transpose(0, 2, 1, 3).reshape(4, 4, 16384)

    return untiled(forward), untiled(backward)


def solution(mesh):
    in_specs = (
        P(None, "col", "row"),
        P("gz", None, "col", "row"),
        P(None, "col", "row", None),
        P(None, "col", "row", None),
        P(None, "col", None, None),
        P(None, "col", None, None),
        P(None, "col"),
        P(),
    )
    out_specs = (P(None, "col", None), P(None, "col", None))
    return jax.shard_map(body, mesh=mesh, in_specs=in_specs, out_specs=out_specs, check_vma=False)
```

```python
import jax
import jax.numpy as jnp
from jax import lax
from jax.experimental import pallas as pl
from jax.experimental.pallas import tpu as pltpu
from jax.sharding import PartitionSpec as P

MESH = pl.DeviceIdType.MESH
F32 = jnp.float32
BF16 = jnp.bfloat16
LANES = 128
PART = 64
NODES_HERE = 4
OFFSETS = sorted(
    [(dz, dy) for dz in range(4) for dy in range(4) if dz or dy],
    key=lambda o: -(min(o[0], 4 - o[0]) + min(o[1], 4 - o[1])),
)
INPUT, SCATTER, GATHER, RHS, F_GZ, Y_ROW, Y_GZ, PX = 0, 1, 4, 7, 11, 15, 19, 22
L_NEAR, L_FAR, L_GZ, U_NEAR, U_FAR, U_GZ, TOP_IN, NEXT_IN, PHASES = 25, 28, 31, 34, 40, 46, 52, 53, 54


def place_of(height, distance):
    return height * (height - 1) // 2 + distance - 1


def lane_ids(rows):
    return lax.broadcasted_iota(jnp.int32, (rows, LANES), 1)


def split(x):
    high = x.astype(BF16)
    return high, (x - high.astype(F32)).astype(BF16)


def dot(a, b):
    return jnp.dot(a, b, preferred_element_type=F32)


def wide_of(a):
    return jnp.concatenate(split(a), axis=1)


def rolled(x, lanes):
    lanes = lanes % LANES
    return pltpu.roll(x, lanes, 1) if lanes else x


def operand_of(x):
    full = jnp.concatenate([rolled(x, -8 * part) for part in range(4)], axis=0)
    high = full.astype(BF16).astype(F32)
    low = full - high
    first = (lane_ids(256) // 8) % 4 == 0
    both = jnp.where(first, high, rolled(low.astype(BF16).astype(F32), 8))
    alone = jnp.where(first, high, 0.0)
    return jnp.concatenate([both.astype(BF16), alone.astype(BF16)], axis=0)


def apply(matrix_of, operand):
    node = lane_ids(256) // 32
    total = None
    for m in range(NODES_HERE):
        out = dot(matrix_of(m), operand)
        total = out if total is None else jnp.where(node == m, out, total)
    total = total + rolled(total, -8)
    quarter = (lane_ids(PART) // 8) % 4
    packed = None
    for part in range(4):
        moved = rolled(total[part * PART:(part + 1) * PART], 8 * part)
        packed = moved if packed is None else jnp.where(quarter == part, moved, packed)
    return packed


def pair_of(b):
    high, low = split(b)
    return high, jnp.concatenate([high, low], axis=1)


def product(a, b_pair):
    a_high, a_low = split(a)
    b_high, b_both = b_pair
    wide = dot(a_high, b_both)
    return wide[:, :LANES] + wide[:, LANES:] + dot(a_low, b_high)


def exchange(arrays):
    octet = lane_ids(arrays[0].shape[0]) // 8
    arrays = list(arrays)
    for bit in (1, 2, 4, 8)[: len(arrays).bit_length() - 1]:
        low = (octet // bit) % 2 == 0
        for i in range(len(arrays)):
            if i & bit:
                continue
            a, b = arrays[i], arrays[i | bit]
            arrays[i] = jnp.where(low, a, rolled(b, 8 * bit))
            arrays[i | bit] = jnp.where(low, rolled(a, -8 * bit), b)
    return arrays


def kernel(
    right_hbm, sums_hbm, lower_hbm, upper_hbm, linv_hbm, uinv_hbm, pattern_ref, parents_ref,
    fwd_hbm, bwd_hbm,
    right, sums, lower, lpart, upper, linv, uinv,
    topsend, toprecv, nextsend, nextrecv, xsend, xrecv, init, sbuf, qbuf, gbuf0, gbuf1, gbuf2, rbuf, pxsend, pxrecv,
    full, fbuf, fown, ybuf, vpart, ownrhs, v21, v11, ul, w11, w21, w31, out_f, out_b,
    send_sem, recv_sem, load_sem, store_sem,
):
    g = lax.axis_index("gz")
    r = lax.axis_index("row")
    c = lax.axis_index("col")
    z, y = c // 4, c % 4
    me = g * 4 + r
    gbuf = (gbuf0, gbuf1, gbuf2)

    def column(offset):
        return ((z + offset[0]) % 4) * 4 + (y + offset[1]) % 4

    loads = {}

    def load(name, source, target):
        loads[name] = pltpu.make_async_copy(source, target, load_sem.at[len(loads)])
        loads[name].start()

    my_rows = pl.ds(pl.multiple_of(r * PART, PART), PART)
    my_nodes = pl.ds(g * 2, 2)
    load("right", right_hbm, right)
    load("sums", sums_hbm, sums)
    load("linv3", linv_hbm.at[3], linv.at[3])
    for height in (3, 2, 1):
        if height < 3:
            load(
                "lower%d" % height, lower_hbm.at[place_of(height, 1), my_nodes],
                lower.at[height - 1, my_nodes, my_rows, :],
            )
        else:
            load("lpart3", lower_hbm.at[place_of(3, 1)], lpart.at[3])
        for distance in range(2, height + 1):
            place = height + distance - 4
            load("lpart%d" % place, lower_hbm.at[place_of(height, distance)], lpart.at[place])
    load("linv2", linv_hbm.at[2], linv.at[2])
    load("linv1", linv_hbm.at[1], linv.at[1])
    load("upper", upper_hbm.at[:, my_nodes], upper.at[:, my_nodes, my_rows, :])
    load("linv0", linv_hbm.at[0], linv.at[0])
    for height in (0, 1, 2, 3):
        load("uinv%d" % height, uinv_hbm.at[height], uinv.at[height])

    barrier = pltpu.get_barrier_semaphore()
    for offset in OFFSETS:
        pl.semaphore_signal(
            barrier, inc=1, device_id={"col": column(offset)}, device_id_type=MESH
        )
    row_steps = (2, 1, 3)
    others = []
    for step in (2, 1, 3):
        others.append((g, (r + step) % 4))
        others.append((1 - g, (r + step) % 4))
    others.append((1 - g, r))
    for place in others:
        pl.semaphore_signal(
            barrier, inc=1, device_id={"gz": place[0], "row": place[1]}, device_id_type=MESH
        )

    def send(source, target, phase, place):
        pltpu.make_async_remote_copy(
            src_ref=source, dst_ref=target, send_sem=send_sem.at[phase],
            recv_sem=recv_sem.at[phase], device_id=place, device_id_type=MESH,
        ).start()

    def wait_bytes(whole, sem):
        pltpu.make_async_copy(whole, whole, sem).wait()

    def wait_blocks(sem, blocks):
        wait_bytes(qbuf.at[0, pl.ds(0, blocks)], sem)

    ancestor, stored = {}, {}
    for height in (1, 2, 3):
        for m in range(NODES_HERE):
            current = parents_ref[height - 1, c * NODES_HERE + m]
            for distance in range(1, height + 1):
                if distance > 1:
                    current = parents_ref[height - distance, current]
                ancestor[height, distance, m] = current
                stored[height, distance, m] = pattern_ref[m, place_of(height, distance)] != 0

    node_of = lane_ids(PART) // 32
    right_mate, left_mate = (r + 1) % 4, (r + 3) % 4

    def rows_of(part):
        return pl.ds(pl.multiple_of(part * PART, PART), PART)

    def near(source, q, target, at, phase):
        for mate in (right_mate, left_mate):
            send(
                source.at[q, my_nodes], target.at[at, my_nodes, my_rows, :], phase + at,
                {"row": mate},
            )

    def far(target, at, phase_near, phase_far):
        wait_bytes(upper.at[0, pl.ds(0, 2), pl.ds(0, 128), :], recv_sem.at[phase_near + at])
        for node, part, mate in ((2 * g, left_mate, right_mate), (2 * g + 1, right_mate, left_mate)):
            block = target.at[at, node, rows_of(part), :]
            send(block, block, phase_far + at, {"row": mate})

    def hand(target, at, phase_far, phase_gz):
        wait_bytes(upper.at[0, pl.ds(0, 2), pl.ds(0, 64), :], recv_sem.at[phase_far + at])
        send(target.at[at, my_nodes], target.at[at, my_nodes], phase_gz + at, {"gz": 1 - g})

    def l_near(height):
        near(lower_hbm, place_of(height, 1), lower, height - 1, L_NEAR)

    def l_far(height):
        far(lower, height - 1, L_NEAR, L_FAR)

    def l_hand(height):
        loads["lower%d" % height].wait()
        hand(lower, height - 1, L_FAR, L_GZ)

    def l_wait(height):
        wait_bytes(upper.at[0, pl.ds(0, 2)], recv_sem.at[L_GZ + height - 1])

    def u_near(q):
        near(upper_hbm, q, upper, q, U_NEAR)

    def u_far(q):
        far(upper, q, U_NEAR, U_FAR)

    def u_hand(q):
        hand(upper, q, U_FAR, U_GZ)

    def u_wait(q):
        wait_bytes(upper.at[0, pl.ds(0, 2)], recv_sem.at[U_GZ + q])

    def multiply(target, a_of, b_of):
        def one(m, carry):
            a_high, a_low = split(a_of(m))
            b_high, b_low = split(b_of(m))
            target[m] = wide_of(dot(a_high, b_high) + dot(a_high, b_low) + dot(a_low, b_high))
            return carry
        lax.fori_loop(0, NODES_HERE, one, 0)

    def scatter_terms(height, distance, terms_in, first, out):
        target = height - distance
        moved = {shift: rolled(terms_in, 32 * shift) for shift in range(-3, 4)}
        terms = []
        for m in range(NODES_HERE):
            spread = moved[-m]
            for t in range(1, 4):
                spread = jnp.where(node_of == t, moved[t - m], spread)
            terms.append(spread)
        wanted = [
            jnp.where(stored[height, distance, m], ancestor[height, distance, m], -1)
            for m in range(NODES_HERE)
        ]
        for offset in OFFSETS + [(0, 0)]:
            slot = offset[0] * 4 + offset[1]
            base = column(offset) * NODES_HERE
            total = jnp.zeros((PART, LANES), F32) if first else sbuf[target, slot]
            for m in range(NODES_HERE):
                total = total + jnp.where(node_of == wanted[m] - base, terms[m], 0.0)
            sbuf[target, slot] = total
            if out and slot:
                send(
                    sbuf.at[target, slot], qbuf.at[target, slot], SCATTER + target,
                    {"col": column(offset)},
                )

    def sum_received(target):
        wait_blocks(recv_sem.at[SCATTER + target], 15)
        total = init[target] - sbuf[target, 0]
        for slot in range(1, 16):
            total = total - qbuf[target, slot]
        return total

    def spread_rhs(height, value):
        rbuf[height, r] = value
        for step in row_steps:
            send(
                rbuf.at[height, r], rbuf.at[height, r], RHS + height, {"row": (r + step) % 4}
            )

    def take_rhs(height):
        wait_blocks(recv_sem.at[RHS + height], 3)
        blocks = [rbuf[height, mate] for mate in range(4)]
        if height == 2:
            own = exchange(blocks)
            for mate in range(4):
                ownrhs[mate] = own[mate]
        else:
            blocks = exchange(blocks)
        return pair_of(jnp.concatenate(blocks, axis=0))

    def make_vpart(height, distance):
        place = 3 if distance == 1 else height + distance - 4
        q_rows = lpart.at[place]

        def one(m, carry):
            a_high, a_low = split(q_rows[m])
            b_high, b_low = split(linv[height, m])
            vpart[place, m] = dot(a_high, b_high) + dot(a_high, b_low) + dot(a_low, b_high)
            return carry

        lax.fori_loop(0, NODES_HERE, one, 0)

    def part_terms(place, b_pair):
        total = None
        for m in range(NODES_HERE):
            out = product(vpart[place, m], b_pair)
            total = out if total is None else jnp.where(node_of == m, out, total)
        return total

    def send_terms(height, distance, b_pair):
        place = height + distance - 4
        total = part_terms(place, b_pair)
        blocks = exchange([total[16 * part:16 * part + 16] for part in range(4)])
        for mate in range(4):
            pxsend[place, mate] = blocks[mate]
        pxrecv[place, r] = pxsend[place, r]
        for step in row_steps:
            to = (r + step) % 4
            send(pxsend.at[place, to], pxrecv.at[place, r], PX + place, {"row": to})

    def take_terms(height, distance):
        place = height + distance - 4
        wait_bytes(pxrecv.at[place, pl.ds(0, 3)], recv_sem.at[PX + place])
        return jnp.concatenate(exchange([pxrecv[place, mate] for mate in range(4)]), axis=0)

    def finish_forward(height, b_pair):
        node = lane_ids(256) // 32

        def one(m, carry):
            full[...] = jnp.where(node == m, product(linv[height, m], b_pair), full[...])
            return carry

        lax.fori_loop(0, NODES_HERE, one, 0)
        fbuf[height, g] = full[...]
        send(fbuf.at[height, g], fbuf.at[height, g], F_GZ + height, {"gz": 1 - g})
        if height:
            own = exchange([full[part * PART:(part + 1) * PART, :] for part in range(4)])
            for mate in range(4):
                fown[height - 1, mate] = own[mate]

    def write_forward(height, slot):
        wait_blocks(recv_sem.at[F_GZ + height], 4)
        group = lane_ids(128) // 32
        pieces = [
            fbuf[height, half, pl.ds(parity, 128, stride=2), :]
            for parity in range(2) for half in range(2)
        ]
        for m in range(NODES_HERE):
            total = None
            for place in range(4):
                moved = rolled(pieces[place], 32 * (place - m))
                total = moved if total is None else jnp.where(group == place, moved, total)
            out_f[pl.ds(height * 512 + m, 128, stride=4), :] = total
        rows = pl.ds(height * 512, 512)
        pltpu.make_async_copy(out_f.at[rows], fwd_hbm.at[rows], store_sem.at[slot]).start()

    my_octets = pl.ds(pl.multiple_of(g * 4, 4), 4)

    def spread_solution(height, value):
        ybuf[height, me] = value
        places = others if height == 3 else [(g, (r + step) % 4) for step in row_steps]
        for place in places:
            send(
                ybuf.at[height, me], ybuf.at[height, me], Y_ROW + height,
                {"gz": place[0], "row": place[1]},
            )

    def hand_solution(height):
        wait_blocks(recv_sem.at[Y_ROW + height], 3)
        send(ybuf.at[height, my_octets], ybuf.at[height, my_octets], Y_GZ + height, {"gz": 1 - g})

    def write_backward(height, slot):
        if height == 3:
            wait_blocks(recv_sem.at[Y_ROW + height], 7)
        else:
            wait_blocks(recv_sem.at[Y_GZ + height], 4)
        pieces = exchange([
            ybuf[height, octet, pl.ds(parity, 32, stride=2), :]
            for parity in range(2) for octet in range(8)
        ])
        for index in range(16):
            m, part = index // 4, index % 4
            out_b[pl.ds(height * 512 + part * 128 + m, 32, stride=4), :] = pieces[index]
        rows = pl.ds(height * 512, 512)
        pltpu.make_async_copy(out_b.at[rows], bwd_hbm.at[rows], store_sem.at[slot]).start()

    def chosen(height, distance):
        total = jnp.zeros((PART, LANES), F32)
        for m in range(NODES_HERE):
            a = ancestor[height, distance, m]
            chip = a // NODES_HERE
            slot = ((z + 4 - chip // 4) % 4) * 4 + (y + 4 - chip % 4) % 4
            block = gbuf[height - distance][slot]
            present = stored[height, distance, m]
            for source in range(4):
                here = jnp.where(jnp.logical_and(present, a % NODES_HERE == source), m, -1)
                total = jnp.where(node_of == here, rolled(block, 32 * (m - source)), total)
        return total

    def share_solution(height, value):
        gbuf[height][0] = value
        for offset in OFFSETS:
            slot = offset[0] * 4 + offset[1]
            send(
                gbuf[height].at[0], gbuf[height].at[slot], GATHER + height,
                {"col": column(offset)},
            )

    loads["right"].wait()
    loads["sums"].wait()

    def source_of(height, m):
        rows = pl.ds(height * 128 + m, 32, stride=4)
        return jnp.where(g == 0, right[rows, :], 0.0) - sums[rows, :]

    group32 = lane_ids(32) // 32

    def half_of(blocks, parity, half):
        total = None
        for m in range(NODES_HERE):
            moved = rolled(blocks[m], 32 * (m - 2 * parity - half))
            total = moved if total is None else jnp.where(group32 == m, moved, total)
        return total

    for height in (3, 2):
        blocks = [source_of(height, m) for m in range(NODES_HERE)]
        for parity in range(2):
            rows = pl.ds(parity, 32, stride=2)
            halves = [half_of(blocks, parity, half) for half in range(2)]
            if height == 3:
                topsend[0, rows, :] = halves[0]
                topsend[1, rows, :] = halves[1]
            else:
                init[2, rows, :] = jnp.where(g == 0, halves[0], halves[1])
                nextsend[rows, :] = jnp.where(g == 0, halves[1], halves[0])
    toprecv[me] = topsend[g]
    pl.semaphore_wait(barrier, len(OFFSETS) + len(others))
    for place in others:
        send(
            topsend.at[place[0]], toprecv.at[me], TOP_IN, {"gz": place[0], "row": place[1]},
        )
    send(nextsend, nextrecv, NEXT_IN, {"gz": 1 - g})
    l_near(2)
    loads["linv3"].wait()
    loads["lpart3"].wait()
    make_vpart(3, 1)
    loads["lpart1"].wait()
    make_vpart(3, 2)
    wait_blocks(recv_sem.at[TOP_IN], 7)

    b_pair = pair_of(jnp.concatenate([toprecv[part] + toprecv[4 + part] for part in range(4)], axis=0))
    scatter_terms(3, 1, part_terms(3, b_pair), True, True)
    send_terms(3, 2, b_pair)
    l_far(2)
    loads["lpart2"].wait()
    make_vpart(3, 3)
    send_terms(3, 3, b_pair)
    pieces = exchange([source_of(height, m) for height in range(2) for m in range(NODES_HERE)])
    for octet in range(8):
        xsend[octet] = pieces[octet]
    for place in others:
        send(
            xsend.at[place[0] * 4 + place[1]], xrecv.at[me], INPUT,
            {"gz": place[0], "row": place[1]},
        )
    xrecv[me] = xsend[me]
    l_near(1)
    u_near(0)
    finish_forward(3, b_pair)
    l_hand(2)
    loads["linv2"].wait()
    loads["lpart0"].wait()
    make_vpart(2, 2)
    wait_blocks(recv_sem.at[NEXT_IN], 1)
    init[2] = init[2] + nextrecv[...]
    l_wait(2)
    multiply(v21, lambda m: lower[1, m], lambda m: linv[2, m])
    scatter_terms(3, 2, take_terms(3, 2), True, False)

    spread_rhs(2, sum_received(2))
    l_far(1)
    scatter_terms(3, 3, take_terms(3, 3), True, False)
    wait_bytes(xrecv.at[pl.ds(0, 7)], recv_sem.at[INPUT])
    parts = exchange([xrecv[part] + xrecv[4 + part] for part in range(4)])
    for height in range(2):
        for parity in range(2):
            init[height, pl.ds(parity, 32, stride=2), :] = half_of(parts, parity, height)
    b_pair = take_rhs(2)
    scatter_terms(2, 1, apply(lambda m: v21[m], operand_of(ownrhs[r])), False, True)
    send_terms(2, 2, b_pair)
    u_far(0)
    u_near(2)
    l_hand(1)
    u_near(1)
    finish_forward(2, b_pair)
    loads["linv1"].wait()
    l_wait(1)
    multiply(v11, lambda m: lower[0, m], lambda m: linv[1, m])
    scatter_terms(2, 2, take_terms(2, 2), False, False)

    rhs = sum_received(1)
    spread_rhs(1, rhs)
    scatter_terms(1, 1, apply(lambda m: v11[m], operand_of(rhs)), False, True)
    loads["upper"].wait()
    u_hand(0)
    u_far(2)
    u_far(1)
    u_near(5)
    finish_forward(1, take_rhs(1))
    u_near(4)
    loads["linv0"].wait()
    loads["uinv0"].wait()
    multiply(ul, lambda m: uinv[0, m], lambda m: linv[0, m])
    loads["uinv1"].wait()
    rest1 = apply(lambda m: wide_of(uinv[1, m]), operand_of(fown[0, r]))
    u_wait(0)
    multiply(w11, lambda m: uinv[1, m], lambda m: upper[0, m])

    rhs = sum_received(0)
    value = apply(lambda m: ul[m], operand_of(rhs))
    share_solution(0, value)
    spread_rhs(0, rhs)
    spread_solution(0, value)
    u_hand(1)
    u_hand(2)
    u_far(5)
    u_far(4)
    finish_forward(0, take_rhs(0))
    u_near(3)
    hand_solution(0)
    u_wait(1)
    loads["uinv2"].wait()
    multiply(w21, lambda m: uinv[2, m], lambda m: upper[1, m])
    write_forward(3, 0)

    wait_blocks(recv_sem.at[GATHER + 0], 15)
    value = rest1 - apply(lambda m: w11[m], operand_of(chosen(1, 1)))
    share_solution(1, value)
    spread_solution(1, value)
    u_hand(5)
    u_hand(4)
    u_far(3)
    u_wait(2)
    rest = fown[1, r] - apply(lambda m: wide_of(upper[2, m]), operand_of(chosen(2, 2)))
    rest2 = apply(lambda m: wide_of(uinv[2, m]), operand_of(rest))
    write_forward(2, 1)
    hand_solution(1)

    wait_blocks(recv_sem.at[GATHER + 1], 15)
    value = rest2 - apply(lambda m: w21[m], operand_of(chosen(2, 1)))
    share_solution(2, value)
    spread_solution(2, value)
    u_hand(3)
    u_wait(5)
    rest = fown[2, r] - apply(lambda m: wide_of(upper[5, m]), operand_of(chosen(3, 3)))
    u_wait(4)
    rest = rest - apply(lambda m: wide_of(upper[4, m]), operand_of(chosen(3, 2)))
    loads["uinv3"].wait()
    rest3 = apply(lambda m: wide_of(uinv[3, m]), operand_of(rest))
    u_wait(3)
    multiply(w31, lambda m: uinv[3, m], lambda m: upper[3, m])
    hand_solution(2)

    wait_blocks(recv_sem.at[GATHER + 2], 15)
    value = rest3 - apply(lambda m: w31[m], operand_of(chosen(3, 1)))
    spread_solution(3, value)
    write_forward(1, 2)
    write_forward(0, 3)
    write_backward(0, 4)
    write_backward(1, 5)
    write_backward(2, 6)
    write_backward(3, 7)

    for phase, blocks in (
        [(TOP_IN, 7), (NEXT_IN, 1)]
        + [(SCATTER + t, 15) for t in range(3)]
        + [(GATHER + t, 15) for t in range(3)]
        + [(RHS + h, 3) for h in range(3)]
        + [(F_GZ + h, 4) for h in range(4)]
        + [(Y_ROW + h, 7 if h == 3 else 3) for h in range(4)]
        + [(Y_GZ + h, 4) for h in range(3)]
        + [(L_NEAR + p, 8) for p in range(2)]
        + [(L_FAR + p, 4) for p in range(2)]
        + [(L_GZ + p, 16) for p in range(2)]
        + [(U_NEAR + p, 8) for p in range(6)]
        + [(U_FAR + p, 4) for p in range(6)]
        + [(U_GZ + p, 16) for p in range(6)]
    ):
        wait_blocks(send_sem.at[phase], blocks)
    wait_bytes(xrecv.at[pl.ds(0, 7)], send_sem.at[INPUT])
    for place in range(3):
        wait_bytes(pxrecv.at[place, pl.ds(0, 3)], send_sem.at[PX + place])
    for slot, (height, out, hbm) in enumerate(
        [(h, out_f, fwd_hbm) for h in (3, 2, 1, 0)] + [(h, out_b, bwd_hbm) for h in (0, 1, 2, 3)]
    ):
        rows = pl.ds(height * 512, 512)
        pltpu.make_async_copy(out.at[rows], hbm.at[rows], store_sem.at[slot]).wait()


def body(
    right_side, layer_sums, lower_blocks, upper_blocks, lower_inverse, upper_diagonal_inverses,
    pattern, parents,
):
    def tiled(x):
        return x.reshape(4, 4, 32, 128).transpose(0, 2, 1, 3).reshape(512, 128)

    anywhere = pl.BlockSpec(memory_space=pl.ANY)
    scalar = pl.BlockSpec(memory_space=pltpu.SMEM)
    forward, backward = pl.pallas_call(
        kernel,
        out_shape=[jax.ShapeDtypeStruct((2048, 128), F32)] * 2,
        in_specs=[anywhere] * 6 + [scalar] * 2,
        out_specs=[anywhere] * 2,
        scratch_shapes=[
            pltpu.VMEM((512, 128), F32),
            pltpu.VMEM((512, 128), F32),
            pltpu.VMEM((2, 4, 256, 256), F32),
            pltpu.VMEM((4, 4, 64, 256), F32),
            pltpu.VMEM((6, 4, 256, 256), F32),
            pltpu.VMEM((4, 4, 256, 256), F32),
            pltpu.VMEM((4, 4, 256, 256), F32),
            pltpu.VMEM((2, 64, 128), F32),
            pltpu.VMEM((8, 64, 128), F32),
            pltpu.VMEM((64, 128), F32),
            pltpu.VMEM((64, 128), F32),
            pltpu.VMEM((8, 32, 128), F32),
            pltpu.VMEM((8, 32, 128), F32),
            pltpu.VMEM((4, 64, 128), F32),
            pltpu.VMEM((3, 16, 64, 128), F32),
            pltpu.VMEM((3, 16, 64, 128), F32),
            pltpu.VMEM((16, 64, 128), F32),
            pltpu.VMEM((16, 64, 128), F32),
            pltpu.VMEM((16, 64, 128), F32),
            pltpu.VMEM((3, 4, 64, 128), F32),
            pltpu.VMEM((3, 4, 16, 128), F32),
            pltpu.VMEM((3, 4, 16, 128), F32),
            pltpu.VMEM((256, 128), F32),
            pltpu.VMEM((4, 2, 256, 128), F32),
            pltpu.VMEM((3, 4, 64, 128), F32),
            pltpu.VMEM((4, 8, 64, 128), F32),
            pltpu.VMEM((4, 4, 64, 256), F32),
            pltpu.VMEM((4, 64, 128), F32),
        ]
        + [pltpu.VMEM((4, 256, 512), BF16)] * 6
        + [
            pltpu.VMEM((2048, 128), F32),
            pltpu.VMEM((2048, 128), F32),
            pltpu.SemaphoreType.DMA((PHASES,)),
            pltpu.SemaphoreType.DMA((PHASES,)),
            pltpu.SemaphoreType.DMA((20,)),
            pltpu.SemaphoreType.DMA((8,)),
        ],
        compiler_params=pltpu.CompilerParams(
            collective_id=0, has_side_effects=True, vmem_limit_bytes=58 * 1024 * 1024
        ),
    )(
        tiled(right_side), tiled(layer_sums[0]), lower_blocks, upper_blocks, lower_inverse,
        upper_diagonal_inverses, pattern.T, parents,
    )

    def untiled(x):
        return x.reshape(4, 128, 4, 128).transpose(0, 2, 1, 3).reshape(4, 4, 16384)

    return untiled(forward), untiled(backward)


def solution(mesh):
    in_specs = (
        P(None, "col", "row"),
        P("gz", None, "col", "row"),
        P(None, "col", "row", None),
        P(None, "col", "row", None),
        P(None, "col", None, None),
        P(None, "col", None, None),
        P(None, "col"),
        P(),
    )
    out_specs = (P(None, "col", None), P(None, "col", None))
    return jax.shard_map(body, mesh=mesh, in_specs=in_specs, out_specs=out_specs, check_vma=False)
```

```python
import jax
import jax.numpy as jnp
from jax import lax
from jax.experimental import pallas as pl
from jax.experimental.pallas import tpu as pltpu
from jax.sharding import PartitionSpec as P

MESH = pl.DeviceIdType.MESH
F32 = jnp.float32
BF16 = jnp.bfloat16
LANES = 128
PART = 64
NODES_HERE = 4
OFFSETS = [
    (2, 2), (1, 2), (2, 3), (3, 1), (0, 2), (3, 3), (1, 3), (2, 1), (3, 2), (1, 1),
    (2, 0), (1, 0), (0, 1), (0, 3), (3, 0),
]
INPUT, SCATTER, GATHER, RHS, F_GZ, Y_ROW, Y_GZ, PX = 0, 1, 4, 7, 11, 15, 19, 22
L_NEAR, L_FAR, L_GZ, U_NEAR, U_FAR, U_GZ, TOP_IN, NEXT_IN, OWN, PHASES = 25, 28, 31, 34, 40, 46, 52, 53, 54, 55


def place_of(height, distance):
    return height * (height - 1) // 2 + distance - 1


def lane_ids(rows):
    return lax.broadcasted_iota(jnp.int32, (rows, LANES), 1)


def split(x):
    high = x.astype(BF16)
    return high, (x - high.astype(F32)).astype(BF16)


def dot(a, b):
    return jnp.dot(a, b, preferred_element_type=F32)


def wide_of(a):
    return jnp.concatenate(split(a), axis=1)


def rolled(x, lanes):
    lanes = lanes % LANES
    return pltpu.roll(x, lanes, 1) if lanes else x


def operand_of(x):
    full = jnp.concatenate([rolled(x, -8 * part) for part in range(4)], axis=0)
    high = full.astype(BF16).astype(F32)
    low = full - high
    first = (lane_ids(256) // 8) % 4 == 0
    both = jnp.where(first, high, rolled(low.astype(BF16).astype(F32), 8))
    alone = jnp.where(first, high, 0.0)
    return jnp.concatenate([both.astype(BF16), alone.astype(BF16)], axis=0)


def apply(matrix_of, operand):
    node = lane_ids(256) // 32
    total = None
    for m in range(NODES_HERE):
        out = dot(matrix_of(m), operand)
        total = out if total is None else jnp.where(node == m, out, total)
    total = total + rolled(total, -8)
    quarter = (lane_ids(PART) // 8) % 4
    packed = None
    for part in range(4):
        moved = rolled(total[part * PART:(part + 1) * PART], 8 * part)
        packed = moved if packed is None else jnp.where(quarter == part, moved, packed)
    return packed


def pair_of(b):
    high, low = split(b)
    return high, jnp.concatenate([high, low], axis=1)


def product(a, b_pair):
    a_high, a_low = split(a)
    b_high, b_both = b_pair
    wide = dot(a_high, b_both)
    return wide[:, :LANES] + wide[:, LANES:] + dot(a_low, b_high)


def exchange(arrays):
    octet = lane_ids(arrays[0].shape[0]) // 8
    arrays = list(arrays)
    for bit in (1, 2, 4, 8)[: len(arrays).bit_length() - 1]:
        low = (octet // bit) % 2 == 0
        for i in range(len(arrays)):
            if i & bit:
                continue
            a, b = arrays[i], arrays[i | bit]
            arrays[i] = jnp.where(low, a, rolled(b, 8 * bit))
            arrays[i | bit] = jnp.where(low, rolled(a, -8 * bit), b)
    return arrays


def kernel(
    right_hbm, sums_hbm, lower_hbm, upper_hbm, linv_hbm, uinv_hbm, pattern_ref, parents_ref,
    fwd_hbm, bwd_hbm,
    right, sums, lower, lpart, upper, linv, uinv,
    topsend, toprecv, nextsend, nextrecv, xsend, xrecv, init, sbuf, qbuf, gbuf0, gbuf1, gbuf2, rbuf, pxsend, pxrecv,
    full, fbuf, fown, ybuf, vpart, v21, v11, ul, w11, w21, w31, out_f, out_b,
    send_sem, recv_sem, load_sem, store_sem,
):
    g = lax.axis_index("gz")
    r = lax.axis_index("row")
    c = lax.axis_index("col")
    z, y = c // 4, c % 4
    me = g * 4 + r
    gbuf = (gbuf0, gbuf1, gbuf2)

    def column(offset):
        return ((z + offset[0]) % 4) * 4 + (y + offset[1]) % 4

    loads = {}

    def load(name, source, target):
        loads[name] = pltpu.make_async_copy(source, target, load_sem.at[len(loads)])
        loads[name].start()

    my_rows = pl.ds(pl.multiple_of(r * PART, PART), PART)
    my_nodes = pl.ds(g * 2, 2)
    load("right", right_hbm, right)
    load("sums", sums_hbm, sums)
    load("linv3", linv_hbm.at[3], linv.at[3])
    for height in (3, 2, 1):
        if height < 3:
            load(
                "lower%d" % height, lower_hbm.at[place_of(height, 1), my_nodes],
                lower.at[height - 1, my_nodes, my_rows, :],
            )
        else:
            load("lpart3", lower_hbm.at[place_of(3, 1)], lpart.at[3])
        for distance in range(2, height + 1):
            place = height + distance - 4
            load("lpart%d" % place, lower_hbm.at[place_of(height, distance)], lpart.at[place])
    load("linv2", linv_hbm.at[2], linv.at[2])
    load("linv1", linv_hbm.at[1], linv.at[1])
    load("upper", upper_hbm.at[:, my_nodes], upper.at[:, my_nodes, my_rows, :])
    load("linv0", linv_hbm.at[0], linv.at[0])
    for height in (0, 1, 2, 3):
        load("uinv%d" % height, uinv_hbm.at[height], uinv.at[height])

    barrier = pltpu.get_barrier_semaphore()
    for offset in OFFSETS:
        pl.semaphore_signal(
            barrier, inc=1, device_id={"col": column(offset)}, device_id_type=MESH
        )
    row_steps = (2, 1, 3)
    others = []
    for step in (2, 1, 3):
        others.append((g, (r + step) % 4))
        others.append((1 - g, (r + step) % 4))
    others.append((1 - g, r))
    for place in others:
        pl.semaphore_signal(
            barrier, inc=1, device_id={"gz": place[0], "row": place[1]}, device_id_type=MESH
        )

    def send(source, target, phase, place):
        pltpu.make_async_remote_copy(
            src_ref=source, dst_ref=target, send_sem=send_sem.at[phase],
            recv_sem=recv_sem.at[phase], device_id=place, device_id_type=MESH,
        ).start()

    def wait_bytes(whole, sem):
        pltpu.make_async_copy(whole, whole, sem).wait()

    def wait_blocks(sem, blocks):
        wait_bytes(qbuf.at[0, pl.ds(0, blocks)], sem)

    ancestor, stored = {}, {}
    for height in (1, 2, 3):
        for m in range(NODES_HERE):
            current = parents_ref[height - 1, c * NODES_HERE + m]
            for distance in range(1, height + 1):
                if distance > 1:
                    current = parents_ref[height - distance, current]
                ancestor[height, distance, m] = current
                stored[height, distance, m] = pattern_ref[m, place_of(height, distance)] != 0

    node_of = lane_ids(PART) // 32
    right_mate, left_mate = (r + 1) % 4, (r + 3) % 4

    def rows_of(part):
        return pl.ds(pl.multiple_of(part * PART, PART), PART)

    def near(source, q, target, at, phase):
        for mate in (right_mate, left_mate):
            send(
                source.at[q, my_nodes], target.at[at, my_nodes, my_rows, :], phase + at,
                {"row": mate},
            )

    def far(target, at, phase_near, phase_far):
        wait_bytes(upper.at[0, pl.ds(0, 2), pl.ds(0, 128), :], recv_sem.at[phase_near + at])
        for node, part, mate in ((2 * g, left_mate, right_mate), (2 * g + 1, right_mate, left_mate)):
            block = target.at[at, node, rows_of(part), :]
            send(block, block, phase_far + at, {"row": mate})

    def hand(target, at, phase_far, phase_gz):
        wait_bytes(upper.at[0, pl.ds(0, 2), pl.ds(0, 64), :], recv_sem.at[phase_far + at])
        send(target.at[at, my_nodes], target.at[at, my_nodes], phase_gz + at, {"gz": 1 - g})

    def l_near(height):
        near(lower_hbm, place_of(height, 1), lower, height - 1, L_NEAR)

    def l_far(height):
        far(lower, height - 1, L_NEAR, L_FAR)

    def l_hand(height):
        loads["lower%d" % height].wait()
        hand(lower, height - 1, L_FAR, L_GZ)

    def l_wait(height):
        wait_bytes(upper.at[0, pl.ds(0, 2)], recv_sem.at[L_GZ + height - 1])

    def u_near(q):
        near(upper_hbm, q, upper, q, U_NEAR)

    def u_far(q):
        far(upper, q, U_NEAR, U_FAR)

    def u_hand(q):
        hand(upper, q, U_FAR, U_GZ)

    def u_wait(q):
        wait_bytes(upper.at[0, pl.ds(0, 2)], recv_sem.at[U_GZ + q])

    def multiply(target, a_of, b_of):
        def one(m, carry):
            a_high, a_low = split(a_of(m))
            b_high, b_low = split(b_of(m))
            target[m] = wide_of(dot(a_high, b_high) + dot(a_high, b_low) + dot(a_low, b_high))
            return carry
        lax.fori_loop(0, NODES_HERE, one, 0)

    def scatter_terms(height, distance, terms_in, first, out):
        target = height - distance
        moved = {shift: rolled(terms_in, 32 * shift) for shift in range(-3, 4)}
        terms = []
        for m in range(NODES_HERE):
            spread = moved[-m]
            for t in range(1, 4):
                spread = jnp.where(node_of == t, moved[t - m], spread)
            terms.append(spread)
        wanted = [
            jnp.where(stored[height, distance, m], ancestor[height, distance, m], -1)
            for m in range(NODES_HERE)
        ]
        for offset in OFFSETS + [(0, 0)]:
            slot = offset[0] * 4 + offset[1]
            base = column(offset) * NODES_HERE
            total = jnp.zeros((PART, LANES), F32) if first else sbuf[target, slot]
            for m in range(NODES_HERE):
                total = total + jnp.where(node_of == wanted[m] - base, terms[m], 0.0)
            sbuf[target, slot] = total
            if out and slot:
                send(
                    sbuf.at[target, slot], qbuf.at[target, slot], SCATTER + target,
                    {"col": column(offset)},
                )

    def sum_received(target):
        wait_blocks(recv_sem.at[SCATTER + target], 15)
        total = init[target] - sbuf[target, 0]
        for slot in range(1, 16):
            total = total - qbuf[target, slot]
        return total

    def spread_rhs(height, value):
        rbuf[height, r] = value
        for step in row_steps:
            send(
                rbuf.at[height, r], rbuf.at[height, r], RHS + height, {"row": (r + step) % 4}
            )

    def take_rhs(height):
        wait_blocks(recv_sem.at[RHS + height], 3)
        blocks = [rbuf[height, mate] for mate in range(4)]
        if height < 2:
            blocks = exchange(blocks)
        return pair_of(jnp.concatenate(blocks, axis=0))

    def make_vpart(height, distance):
        place = 3 if distance == 1 else height + distance - 4
        q_rows = lpart.at[place]

        def one(m, carry):
            a_high, a_low = split(q_rows[m])
            b_high, b_low = split(linv[height, m])
            vpart[place, m] = dot(a_high, b_high) + dot(a_high, b_low) + dot(a_low, b_high)
            return carry

        lax.fori_loop(0, NODES_HERE, one, 0)

    def part_terms(place, b_pair):
        total = None
        for m in range(NODES_HERE):
            out = product(vpart[place, m], b_pair)
            total = out if total is None else jnp.where(node_of == m, out, total)
        return total

    def send_terms(height, distance, b_pair):
        place = height + distance - 4
        send_parts(place, PX + place, part_terms(place, b_pair))

    def send_parts(place, phase, total):
        blocks = exchange([total[16 * part:16 * part + 16] for part in range(4)])
        for mate in range(4):
            pxsend[place, mate] = blocks[mate]
        pxrecv[place, r] = pxsend[place, r]
        for step in row_steps:
            to = (r + step) % 4
            send(pxsend.at[place, to], pxrecv.at[place, r], phase, {"row": to})

    def take_terms(height, distance):
        place = height + distance - 4
        return take_parts(place, PX + place)

    def take_parts(place, phase):
        wait_bytes(pxrecv.at[place, pl.ds(0, 3)], recv_sem.at[phase])
        return jnp.concatenate(exchange([pxrecv[place, mate] for mate in range(4)]), axis=0)

    def finish_forward(height, b_pair):
        node = lane_ids(256) // 32

        def one(m, carry):
            full[...] = jnp.where(node == m, product(linv[height, m], b_pair), full[...])
            return carry

        lax.fori_loop(0, NODES_HERE, one, 0)
        fbuf[height, g] = full[...]
        send(fbuf.at[height, g], fbuf.at[height, g], F_GZ + height, {"gz": 1 - g})
        if height:
            own = exchange([full[part * PART:(part + 1) * PART, :] for part in range(4)])
            for mate in range(4):
                fown[height - 1, mate] = own[mate]

    def write_forward(height, slot):
        wait_blocks(recv_sem.at[F_GZ + height], 4)
        group = lane_ids(128) // 32
        pieces = [
            fbuf[height, half, pl.ds(parity, 128, stride=2), :]
            for parity in range(2) for half in range(2)
        ]
        for m in range(NODES_HERE):
            total = None
            for place in range(4):
                moved = rolled(pieces[place], 32 * (place - m))
                total = moved if total is None else jnp.where(group == place, moved, total)
            out_f[pl.ds(height * 512 + m, 128, stride=4), :] = total
        rows = pl.ds(height * 512, 512)
        pltpu.make_async_copy(out_f.at[rows], fwd_hbm.at[rows], store_sem.at[slot]).start()

    my_octets = pl.ds(pl.multiple_of(g * 4, 4), 4)

    def spread_solution(height, value):
        ybuf[height, me] = value
        places = others if height == 3 else [(g, (r + step) % 4) for step in row_steps]
        for place in places:
            send(
                ybuf.at[height, me], ybuf.at[height, me], Y_ROW + height,
                {"gz": place[0], "row": place[1]},
            )

    def hand_solution(height):
        wait_blocks(recv_sem.at[Y_ROW + height], 3)
        send(ybuf.at[height, my_octets], ybuf.at[height, my_octets], Y_GZ + height, {"gz": 1 - g})

    def write_backward(height, slot):
        if height == 3:
            wait_blocks(recv_sem.at[Y_ROW + height], 7)
        else:
            wait_blocks(recv_sem.at[Y_GZ + height], 4)
        pieces = exchange([
            ybuf[height, octet, pl.ds(parity, 32, stride=2), :]
            for parity in range(2) for octet in range(8)
        ])
        for index in range(16):
            m, part = index // 4, index % 4
            out_b[pl.ds(height * 512 + part * 128 + m, 32, stride=4), :] = pieces[index]
        rows = pl.ds(height * 512, 512)
        pltpu.make_async_copy(out_b.at[rows], bwd_hbm.at[rows], store_sem.at[slot]).start()

    def chosen(height, distance):
        total = jnp.zeros((PART, LANES), F32)
        for m in range(NODES_HERE):
            a = ancestor[height, distance, m]
            chip = a // NODES_HERE
            slot = ((z + 4 - chip // 4) % 4) * 4 + (y + 4 - chip % 4) % 4
            block = gbuf[height - distance][slot]
            present = stored[height, distance, m]
            for source in range(4):
                here = jnp.where(jnp.logical_and(present, a % NODES_HERE == source), m, -1)
                total = jnp.where(node_of == here, rolled(block, 32 * (m - source)), total)
        return total

    def share_solution(height, value):
        gbuf[height][0] = value
        for offset in OFFSETS:
            slot = offset[0] * 4 + offset[1]
            send(
                gbuf[height].at[0], gbuf[height].at[slot], GATHER + height,
                {"col": column(offset)},
            )

    loads["right"].wait()
    loads["sums"].wait()

    def source_of(height, m):
        rows = pl.ds(height * 128 + m, 32, stride=4)
        return jnp.where(g == 0, right[rows, :], 0.0) - sums[rows, :]

    group32 = lane_ids(32) // 32

    def half_of(blocks, parity, half):
        total = None
        for m in range(NODES_HERE):
            moved = rolled(blocks[m], 32 * (m - 2 * parity - half))
            total = moved if total is None else jnp.where(group32 == m, moved, total)
        return total

    for height in (3, 2):
        blocks = [source_of(height, m) for m in range(NODES_HERE)]
        for parity in range(2):
            rows = pl.ds(parity, 32, stride=2)
            halves = [half_of(blocks, parity, half) for half in range(2)]
            if height == 3:
                topsend[0, rows, :] = halves[0]
                topsend[1, rows, :] = halves[1]
            else:
                init[2, rows, :] = jnp.where(g == 0, halves[0], halves[1])
                nextsend[rows, :] = jnp.where(g == 0, halves[1], halves[0])
    toprecv[me] = topsend[g]
    pl.semaphore_wait(barrier, len(OFFSETS) + len(others))
    for place in others:
        send(
            topsend.at[place[0]], toprecv.at[me], TOP_IN, {"gz": place[0], "row": place[1]},
        )
    send(nextsend, nextrecv, NEXT_IN, {"gz": 1 - g})
    l_near(2)
    loads["linv3"].wait()
    loads["lpart3"].wait()
    make_vpart(3, 1)
    loads["lpart1"].wait()
    make_vpart(3, 2)
    wait_blocks(recv_sem.at[TOP_IN], 7)

    b_pair = pair_of(jnp.concatenate([toprecv[part] + toprecv[4 + part] for part in range(4)], axis=0))
    scatter_terms(3, 1, part_terms(3, b_pair), True, True)
    send_terms(3, 2, b_pair)
    l_far(2)
    loads["lpart2"].wait()
    make_vpart(3, 3)
    send_terms(3, 3, b_pair)
    pieces = exchange([source_of(height, m) for height in range(2) for m in range(NODES_HERE)])
    for octet in range(8):
        xsend[octet] = pieces[octet]
    for place in others:
        send(
            xsend.at[place[0] * 4 + place[1]], xrecv.at[me], INPUT,
            {"gz": place[0], "row": place[1]},
        )
    xrecv[me] = xsend[me]
    l_near(1)
    u_near(0)
    finish_forward(3, b_pair)
    l_hand(2)
    loads["linv2"].wait()
    loads["lpart0"].wait()
    make_vpart(2, 2)
    wait_blocks(recv_sem.at[NEXT_IN], 1)
    init[2] = init[2] + nextrecv[...]
    l_wait(2)
    multiply(v21, lambda m: lower[1, m], lambda m: linv[2, m])
    scatter_terms(3, 2, take_terms(3, 2), True, False)

    rhs = sum_received(2)
    send_parts(3, OWN, rhs)
    spread_rhs(2, rhs)
    l_far(1)
    scatter_terms(3, 3, take_terms(3, 3), True, False)
    wait_bytes(xrecv.at[pl.ds(0, 7)], recv_sem.at[INPUT])
    parts = exchange([xrecv[part] + xrecv[4 + part] for part in range(4)])
    for height in range(2):
        for parity in range(2):
            init[height, pl.ds(parity, 32, stride=2), :] = half_of(parts, parity, height)
    scatter_terms(2, 1, apply(lambda m: v21[m], operand_of(take_parts(3, OWN))), False, True)
    b_pair = take_rhs(2)
    send_terms(2, 2, b_pair)
    u_far(0)
    u_near(2)
    l_hand(1)
    u_near(1)
    finish_forward(2, b_pair)
    loads["linv1"].wait()
    l_wait(1)
    multiply(v11, lambda m: lower[0, m], lambda m: linv[1, m])
    scatter_terms(2, 2, take_terms(2, 2), False, False)

    rhs = sum_received(1)
    spread_rhs(1, rhs)
    scatter_terms(1, 1, apply(lambda m: v11[m], operand_of(rhs)), False, True)
    loads["upper"].wait()
    u_hand(0)
    u_far(2)
    u_far(1)
    u_near(5)
    finish_forward(1, take_rhs(1))
    u_near(4)
    loads["linv0"].wait()
    loads["uinv0"].wait()
    multiply(ul, lambda m: uinv[0, m], lambda m: linv[0, m])
    loads["uinv1"].wait()
    rest1 = apply(lambda m: wide_of(uinv[1, m]), operand_of(fown[0, r]))
    u_wait(0)
    multiply(w11, lambda m: uinv[1, m], lambda m: upper[0, m])

    rhs = sum_received(0)
    value = apply(lambda m: ul[m], operand_of(rhs))
    share_solution(0, value)
    spread_rhs(0, rhs)
    spread_solution(0, value)
    u_hand(1)
    u_hand(2)
    u_far(5)
    u_far(4)
    finish_forward(0, take_rhs(0))
    u_near(3)
    hand_solution(0)
    u_wait(1)
    loads["uinv2"].wait()
    multiply(w21, lambda m: uinv[2, m], lambda m: upper[1, m])
    write_forward(3, 0)

    wait_blocks(recv_sem.at[GATHER + 0], 15)
    value = rest1 - apply(lambda m: w11[m], operand_of(chosen(1, 1)))
    share_solution(1, value)
    spread_solution(1, value)
    u_hand(5)
    u_hand(4)
    u_far(3)
    u_wait(2)
    rest = fown[1, r] - apply(lambda m: wide_of(upper[2, m]), operand_of(chosen(2, 2)))
    rest2 = apply(lambda m: wide_of(uinv[2, m]), operand_of(rest))
    write_forward(2, 1)
    hand_solution(1)

    wait_blocks(recv_sem.at[GATHER + 1], 15)
    value = rest2 - apply(lambda m: w21[m], operand_of(chosen(2, 1)))
    share_solution(2, value)
    spread_solution(2, value)
    u_hand(3)
    u_wait(5)
    rest = fown[2, r] - apply(lambda m: wide_of(upper[5, m]), operand_of(chosen(3, 3)))
    u_wait(4)
    rest = rest - apply(lambda m: wide_of(upper[4, m]), operand_of(chosen(3, 2)))
    loads["uinv3"].wait()
    rest3 = apply(lambda m: wide_of(uinv[3, m]), operand_of(rest))
    u_wait(3)
    multiply(w31, lambda m: uinv[3, m], lambda m: upper[3, m])
    hand_solution(2)

    wait_blocks(recv_sem.at[GATHER + 2], 15)
    value = rest3 - apply(lambda m: w31[m], operand_of(chosen(3, 1)))
    spread_solution(3, value)
    write_forward(1, 2)
    write_forward(0, 3)
    write_backward(0, 4)
    write_backward(1, 5)
    write_backward(2, 6)
    write_backward(3, 7)

    for phase, blocks in (
        [(TOP_IN, 7), (NEXT_IN, 1)]
        + [(SCATTER + t, 15) for t in range(3)]
        + [(GATHER + t, 15) for t in range(3)]
        + [(RHS + h, 3) for h in range(3)]
        + [(F_GZ + h, 4) for h in range(4)]
        + [(Y_ROW + h, 7 if h == 3 else 3) for h in range(4)]
        + [(Y_GZ + h, 4) for h in range(3)]
        + [(L_NEAR + p, 8) for p in range(2)]
        + [(L_FAR + p, 4) for p in range(2)]
        + [(L_GZ + p, 16) for p in range(2)]
        + [(U_NEAR + p, 8) for p in range(6)]
        + [(U_FAR + p, 4) for p in range(6)]
        + [(U_GZ + p, 16) for p in range(6)]
    ):
        wait_blocks(send_sem.at[phase], blocks)
    wait_bytes(xrecv.at[pl.ds(0, 7)], send_sem.at[INPUT])
    for phase in (PX, PX + 1, PX + 2, OWN):
        wait_bytes(pxrecv.at[0, pl.ds(0, 3)], send_sem.at[phase])
    for slot, (height, out, hbm) in enumerate(
        [(h, out_f, fwd_hbm) for h in (3, 2, 1, 0)] + [(h, out_b, bwd_hbm) for h in (0, 1, 2, 3)]
    ):
        rows = pl.ds(height * 512, 512)
        pltpu.make_async_copy(out.at[rows], hbm.at[rows], store_sem.at[slot]).wait()


def body(
    right_side, layer_sums, lower_blocks, upper_blocks, lower_inverse, upper_diagonal_inverses,
    pattern, parents,
):
    def tiled(x):
        return x.reshape(4, 4, 32, 128).transpose(0, 2, 1, 3).reshape(512, 128)

    anywhere = pl.BlockSpec(memory_space=pl.ANY)
    scalar = pl.BlockSpec(memory_space=pltpu.SMEM)
    forward, backward = pl.pallas_call(
        kernel,
        out_shape=[jax.ShapeDtypeStruct((2048, 128), F32)] * 2,
        in_specs=[anywhere] * 6 + [scalar] * 2,
        out_specs=[anywhere] * 2,
        scratch_shapes=[
            pltpu.VMEM((512, 128), F32),
            pltpu.VMEM((512, 128), F32),
            pltpu.VMEM((2, 4, 256, 256), F32),
            pltpu.VMEM((4, 4, 64, 256), F32),
            pltpu.VMEM((6, 4, 256, 256), F32),
            pltpu.VMEM((4, 4, 256, 256), F32),
            pltpu.VMEM((4, 4, 256, 256), F32),
            pltpu.VMEM((2, 64, 128), F32),
            pltpu.VMEM((8, 64, 128), F32),
            pltpu.VMEM((64, 128), F32),
            pltpu.VMEM((64, 128), F32),
            pltpu.VMEM((8, 32, 128), F32),
            pltpu.VMEM((8, 32, 128), F32),
            pltpu.VMEM((4, 64, 128), F32),
            pltpu.VMEM((3, 16, 64, 128), F32),
            pltpu.VMEM((3, 16, 64, 128), F32),
            pltpu.VMEM((16, 64, 128), F32),
            pltpu.VMEM((16, 64, 128), F32),
            pltpu.VMEM((16, 64, 128), F32),
            pltpu.VMEM((3, 4, 64, 128), F32),
            pltpu.VMEM((4, 4, 16, 128), F32),
            pltpu.VMEM((4, 4, 16, 128), F32),
            pltpu.VMEM((256, 128), F32),
            pltpu.VMEM((4, 2, 256, 128), F32),
            pltpu.VMEM((3, 4, 64, 128), F32),
            pltpu.VMEM((4, 8, 64, 128), F32),
            pltpu.VMEM((4, 4, 64, 256), F32),
        ]
        + [pltpu.VMEM((4, 256, 512), BF16)] * 6
        + [
            pltpu.VMEM((2048, 128), F32),
            pltpu.VMEM((2048, 128), F32),
            pltpu.SemaphoreType.DMA((PHASES,)),
            pltpu.SemaphoreType.DMA((PHASES,)),
            pltpu.SemaphoreType.DMA((20,)),
            pltpu.SemaphoreType.DMA((8,)),
        ],
        compiler_params=pltpu.CompilerParams(
            collective_id=0, has_side_effects=True, vmem_limit_bytes=58 * 1024 * 1024
        ),
    )(
        tiled(right_side), tiled(layer_sums[0]), lower_blocks, upper_blocks, lower_inverse,
        upper_diagonal_inverses, pattern.T, parents,
    )

    def copy_out(f_in, b_in, f_to, b_to, sems):
        moves = []
        for source, target in ((f_in, f_to), (b_in, b_to)):
            for part in range(4):
                rows = pl.ds(part * 512, 512)
                moves.append(pltpu.make_async_copy(source.at[rows], target.at[rows], sems.at[len(moves)]))
        for move in moves:
            move.start()
        for move in moves:
            move.wait()

    forward, backward = pl.pallas_call(
        copy_out,
        out_shape=[jax.ShapeDtypeStruct((2048, 128), F32)] * 2,
        in_specs=[anywhere] * 2,
        out_specs=[pl.BlockSpec(memory_space=pltpu.HBM)] * 2,
        scratch_shapes=[pltpu.SemaphoreType.DMA((8,))],
        compiler_params=pltpu.CompilerParams(vmem_limit_bytes=8 * 1024 * 1024),
    )(forward, backward)

    def untiled(x):
        return x.reshape(4, 128, 4, 128).transpose(0, 2, 1, 3).reshape(4, 4, 16384)

    return untiled(forward), untiled(backward)


def solution(mesh):
    in_specs = (
        P(None, "col", "row"),
        P("gz", None, "col", "row"),
        P(None, "col", "row", None),
        P(None, "col", "row", None),
        P(None, "col", None, None),
        P(None, "col", None, None),
        P(None, "col"),
        P(),
    )
    out_specs = (P(None, "col", None), P(None, "col", None))
    return jax.shard_map(body, mesh=mesh, in_specs=in_specs, out_specs=out_specs, check_vma=False)
```

```python
import jax
import jax.numpy as jnp
from jax import lax
from jax.experimental import pallas as pl
from jax.experimental.pallas import tpu as pltpu
from jax.sharding import PartitionSpec as P

MESH = pl.DeviceIdType.MESH
F32 = jnp.float32
BF16 = jnp.bfloat16
LANES = 128
PART = 64
NODES_HERE = 4
OFFSETS = [
    (2, 2), (1, 2), (2, 3), (3, 1), (0, 2), (3, 3), (1, 3), (2, 1), (3, 2), (1, 1),
    (2, 0), (1, 0), (0, 1), (0, 3), (3, 0),
]
INPUT, SCATTER, GATHER, RHS, F_GZ, Y_ROW, Y_GZ, PX = 0, 1, 4, 7, 11, 15, 19, 22
L_NEAR, L_FAR, L_GZ, U_NEAR, U_FAR, U_GZ, TOP_IN, NEXT_IN, OWN, PHASES = 25, 28, 31, 34, 40, 46, 52, 53, 54, 55


def place_of(height, distance):
    return height * (height - 1) // 2 + distance - 1


def lane_ids(rows):
    return lax.broadcasted_iota(jnp.int32, (rows, LANES), 1)


def split(x):
    high = x.astype(BF16)
    return high, (x - high.astype(F32)).astype(BF16)


def dot(a, b):
    return jnp.dot(a, b, preferred_element_type=F32)


def wide_of(a):
    return jnp.concatenate(split(a), axis=1)


def rolled(x, lanes):
    lanes = lanes % LANES
    return pltpu.roll(x, lanes, 1) if lanes else x


def operand_of(x):
    full = jnp.concatenate([rolled(x, -8 * part) for part in range(4)], axis=0)
    high = full.astype(BF16).astype(F32)
    low = full - high
    first = (lane_ids(256) // 8) % 4 == 0
    both = jnp.where(first, high, rolled(low.astype(BF16).astype(F32), 8))
    alone = jnp.where(first, high, 0.0)
    return jnp.concatenate([both.astype(BF16), alone.astype(BF16)], axis=0)


def apply(matrix_of, operand):
    node = lane_ids(256) // 32
    total = None
    for m in range(NODES_HERE):
        out = dot(matrix_of(m), operand)
        total = out if total is None else jnp.where(node == m, out, total)
    total = total + rolled(total, -8)
    quarter = (lane_ids(PART) // 8) % 4
    packed = None
    for part in range(4):
        moved = rolled(total[part * PART:(part + 1) * PART], 8 * part)
        packed = moved if packed is None else jnp.where(quarter == part, moved, packed)
    return packed


def pair_of(b):
    high, low = split(b)
    return high, jnp.concatenate([high, low], axis=1)


def product(a, b_pair):
    a_high, a_low = split(a)
    b_high, b_both = b_pair
    wide = dot(a_high, b_both)
    return wide[:, :LANES] + wide[:, LANES:] + dot(a_low, b_high)


def exchange(arrays):
    octet = lane_ids(arrays[0].shape[0]) // 8
    arrays = list(arrays)
    for bit in (1, 2, 4, 8)[: len(arrays).bit_length() - 1]:
        low = (octet // bit) % 2 == 0
        for i in range(len(arrays)):
            if i & bit:
                continue
            a, b = arrays[i], arrays[i | bit]
            arrays[i] = jnp.where(low, a, rolled(b, 8 * bit))
            arrays[i | bit] = jnp.where(low, rolled(a, -8 * bit), b)
    return arrays


def kernel(
    right_hbm, sums_hbm, lower_hbm, upper_hbm, linv_hbm, uinv_hbm, pattern_ref, parents_ref,
    fwd_hbm, bwd_hbm,
    right, sums, lower, lpart, upper, linv, uinv,
    topsend, toprecv, nextsend, nextrecv, xsend, xrecv, init, sbuf, qbuf, gbuf0, gbuf1, gbuf2, rbuf, pxsend, pxrecv,
    full, fbuf, fown, ybuf, vpart, v21, v11, ul, w11, w21, w31, out_f, out_b,
    send_sem, recv_sem, load_sem, store_sem,
):
    g = lax.axis_index("gz")
    r = lax.axis_index("row")
    c = lax.axis_index("col")
    z, y = c // 4, c % 4
    me = g * 4 + r
    gbuf = (gbuf0, gbuf1, gbuf2)

    def column(offset):
        return ((z + offset[0]) % 4) * 4 + (y + offset[1]) % 4

    loads = {}

    def load(name, source, target):
        loads[name] = pltpu.make_async_copy(source, target, load_sem.at[len(loads)])
        loads[name].start()

    my_rows = pl.ds(pl.multiple_of(r * PART, PART), PART)
    my_nodes = pl.ds(g * 2, 2)
    load("right", right_hbm, right)
    load("sums", sums_hbm, sums)
    load("linv3", linv_hbm.at[3], linv.at[3])
    for height in (3, 2, 1):
        if height < 3:
            load(
                "lower%d" % height, lower_hbm.at[place_of(height, 1), my_nodes],
                lower.at[height - 1, my_nodes, my_rows, :],
            )
        else:
            load("lpart3", lower_hbm.at[place_of(3, 1)], lpart.at[3])
        for distance in range(2, height + 1):
            place = height + distance - 4
            load("lpart%d" % place, lower_hbm.at[place_of(height, distance)], lpart.at[place])
    load("linv2", linv_hbm.at[2], linv.at[2])
    load("linv1", linv_hbm.at[1], linv.at[1])
    load("upper", upper_hbm.at[:, my_nodes], upper.at[:, my_nodes, my_rows, :])
    load("linv0", linv_hbm.at[0], linv.at[0])
    for height in (0, 1, 2, 3):
        load("uinv%d" % height, uinv_hbm.at[height], uinv.at[height])

    barrier = pltpu.get_barrier_semaphore()
    for offset in OFFSETS:
        pl.semaphore_signal(
            barrier, inc=1, device_id={"col": column(offset)}, device_id_type=MESH
        )
    row_steps = (2, 1, 3)
    others = []
    for step in (2, 1, 3):
        others.append((g, (r + step) % 4))
        others.append((1 - g, (r + step) % 4))
    others.append((1 - g, r))
    for place in others:
        pl.semaphore_signal(
            barrier, inc=1, device_id={"gz": place[0], "row": place[1]}, device_id_type=MESH
        )

    def send(source, target, phase, place):
        pltpu.make_async_remote_copy(
            src_ref=source, dst_ref=target, send_sem=send_sem.at[phase],
            recv_sem=recv_sem.at[phase], device_id=place, device_id_type=MESH,
        ).start()

    def wait_bytes(whole, sem):
        pltpu.make_async_copy(whole, whole, sem).wait()

    def wait_blocks(sem, blocks):
        wait_bytes(qbuf.at[0, pl.ds(0, blocks)], sem)

    ancestor, stored = {}, {}
    for height in (1, 2, 3):
        for m in range(NODES_HERE):
            current = parents_ref[height - 1, c * NODES_HERE + m]
            for distance in range(1, height + 1):
                if distance > 1:
                    current = parents_ref[height - distance, current]
                ancestor[height, distance, m] = current
                stored[height, distance, m] = pattern_ref[m, place_of(height, distance)] != 0

    node_of = lane_ids(PART) // 32
    right_mate, left_mate = (r + 1) % 4, (r + 3) % 4

    def rows_of(part):
        return pl.ds(pl.multiple_of(part * PART, PART), PART)

    def near(source, q, target, at, phase):
        for mate in (right_mate, left_mate):
            send(
                source.at[q, my_nodes], target.at[at, my_nodes, my_rows, :], phase + at,
                {"row": mate},
            )

    def far(target, at, phase_near, phase_far):
        wait_bytes(upper.at[0, pl.ds(0, 2), pl.ds(0, 128), :], recv_sem.at[phase_near + at])
        for node, part, mate in ((2 * g, left_mate, right_mate), (2 * g + 1, right_mate, left_mate)):
            block = target.at[at, node, rows_of(part), :]
            send(block, block, phase_far + at, {"row": mate})

    def hand(target, at, phase_far, phase_gz):
        wait_bytes(upper.at[0, pl.ds(0, 2), pl.ds(0, 64), :], recv_sem.at[phase_far + at])
        send(target.at[at, my_nodes], target.at[at, my_nodes], phase_gz + at, {"gz": 1 - g})

    def l_near(height):
        near(lower_hbm, place_of(height, 1), lower, height - 1, L_NEAR)

    def l_far(height):
        far(lower, height - 1, L_NEAR, L_FAR)

    def l_hand(height):
        loads["lower%d" % height].wait()
        hand(lower, height - 1, L_FAR, L_GZ)

    def l_wait(height):
        wait_bytes(upper.at[0, pl.ds(0, 2)], recv_sem.at[L_GZ + height - 1])

    def u_near(q):
        near(upper_hbm, q, upper, q, U_NEAR)

    def u_far(q):
        far(upper, q, U_NEAR, U_FAR)

    def u_hand(q):
        hand(upper, q, U_FAR, U_GZ)

    def u_wait(q):
        wait_bytes(upper.at[0, pl.ds(0, 2)], recv_sem.at[U_GZ + q])

    def multiply(target, a_of, b_of):
        def one(m, carry):
            a_high, a_low = split(a_of(m))
            b_high, b_low = split(b_of(m))
            target[m] = wide_of(dot(a_high, b_high) + dot(a_high, b_low) + dot(a_low, b_high))
            return carry
        lax.fori_loop(0, NODES_HERE, one, 0)

    def scatter_terms(height, distance, terms_in, first, out):
        target = height - distance
        moved = {shift: rolled(terms_in, 32 * shift) for shift in range(-3, 4)}
        terms = []
        for m in range(NODES_HERE):
            spread = moved[-m]
            for t in range(1, 4):
                spread = jnp.where(node_of == t, moved[t - m], spread)
            terms.append(spread)
        wanted = [
            jnp.where(stored[height, distance, m], ancestor[height, distance, m], -1)
            for m in range(NODES_HERE)
        ]
        for offset in OFFSETS + [(0, 0)]:
            slot = offset[0] * 4 + offset[1]
            base = column(offset) * NODES_HERE
            total = jnp.zeros((PART, LANES), F32) if first else sbuf[target, slot]
            for m in range(NODES_HERE):
                total = total + jnp.where(node_of == wanted[m] - base, terms[m], 0.0)
            sbuf[target, slot] = total
            if out and slot:
                send(
                    sbuf.at[target, slot], qbuf.at[target, slot], SCATTER + target,
                    {"col": column(offset)},
                )

    def sum_received(target):
        wait_blocks(recv_sem.at[SCATTER + target], 15)
        total = init[target] - sbuf[target, 0]
        for slot in range(1, 16):
            total = total - qbuf[target, slot]
        return total

    def spread_rhs(height, value):
        rbuf[height, r] = value
        for step in row_steps:
            send(
                rbuf.at[height, r], rbuf.at[height, r], RHS + height, {"row": (r + step) % 4}
            )

    def take_rhs(height):
        wait_blocks(recv_sem.at[RHS + height], 3)
        blocks = [rbuf[height, mate] for mate in range(4)]
        if height < 2:
            blocks = exchange(blocks)
        return pair_of(jnp.concatenate(blocks, axis=0))

    def make_vpart(height, distance):
        place = 3 if distance == 1 else height + distance - 4
        q_rows = lpart.at[place]

        def one(m, carry):
            a_high, a_low = split(q_rows[m])
            b_high, b_low = split(linv[height, m])
            vpart[place, m] = dot(a_high, b_high) + dot(a_high, b_low) + dot(a_low, b_high)
            return carry

        lax.fori_loop(0, NODES_HERE, one, 0)

    def part_terms(place, b_pair):
        total = None
        for m in range(NODES_HERE):
            out = product(vpart[place, m], b_pair)
            total = out if total is None else jnp.where(node_of == m, out, total)
        return total

    def send_terms(height, distance, b_pair):
        place = height + distance - 4
        send_parts(place, PX + place, part_terms(place, b_pair))

    def send_parts(place, phase, total):
        blocks = exchange([total[16 * part:16 * part + 16] for part in range(4)])
        for mate in range(4):
            pxsend[place, mate] = blocks[mate]
        pxrecv[place, r] = pxsend[place, r]
        for step in row_steps:
            to = (r + step) % 4
            send(pxsend.at[place, to], pxrecv.at[place, r], phase, {"row": to})

    def take_terms(height, distance):
        place = height + distance - 4
        return take_parts(place, PX + place)

    def take_parts(place, phase):
        wait_bytes(pxrecv.at[place, pl.ds(0, 3)], recv_sem.at[phase])
        return jnp.concatenate(exchange([pxrecv[place, mate] for mate in range(4)]), axis=0)

    def finish_forward(height, b_pair):
        node = lane_ids(256) // 32

        def one(m, carry):
            full[...] = jnp.where(node == m, product(linv[height, m], b_pair), full[...])
            return carry

        lax.fori_loop(0, NODES_HERE, one, 0)
        fbuf[height, g] = full[...]
        send(fbuf.at[height, g], fbuf.at[height, g], F_GZ + height, {"gz": 1 - g})
        if height:
            own = exchange([full[part * PART:(part + 1) * PART, :] for part in range(4)])
            for mate in range(4):
                fown[height - 1, mate] = own[mate]

    def write_forward(height, slot):
        wait_blocks(recv_sem.at[F_GZ + height], 4)
        group = lane_ids(128) // 32
        pieces = [
            fbuf[height, half, pl.ds(parity, 128, stride=2), :]
            for parity in range(2) for half in range(2)
        ]
        for m in range(NODES_HERE):
            total = None
            for place in range(4):
                moved = rolled(pieces[place], 32 * (place - m))
                total = moved if total is None else jnp.where(group == place, moved, total)
            out_f[pl.ds(height * 512 + m, 128, stride=4), :] = total
        rows = pl.ds(height * 512, 512)
        pltpu.make_async_copy(out_f.at[rows], fwd_hbm.at[rows], store_sem.at[slot]).start()

    my_octets = pl.ds(pl.multiple_of(g * 4, 4), 4)

    def spread_solution(height, value):
        ybuf[height, me] = value
        places = others if height == 3 else [(g, (r + step) % 4) for step in row_steps]
        for place in places:
            send(
                ybuf.at[height, me], ybuf.at[height, me], Y_ROW + height,
                {"gz": place[0], "row": place[1]},
            )

    def hand_solution(height):
        wait_blocks(recv_sem.at[Y_ROW + height], 3)
        send(ybuf.at[height, my_octets], ybuf.at[height, my_octets], Y_GZ + height, {"gz": 1 - g})

    def write_backward(height, slot):
        if height == 3:
            wait_blocks(recv_sem.at[Y_ROW + height], 7)
        else:
            wait_blocks(recv_sem.at[Y_GZ + height], 4)
        pieces = exchange([
            ybuf[height, octet, pl.ds(parity, 32, stride=2), :]
            for parity in range(2) for octet in range(8)
        ])
        for index in range(16):
            m, part = index // 4, index % 4
            out_b[pl.ds(height * 512 + part * 128 + m, 32, stride=4), :] = pieces[index]
        rows = pl.ds(height * 512, 512)
        pltpu.make_async_copy(out_b.at[rows], bwd_hbm.at[rows], store_sem.at[slot]).start()

    def chosen(height, distance):
        total = jnp.zeros((PART, LANES), F32)
        for m in range(NODES_HERE):
            a = ancestor[height, distance, m]
            chip = a // NODES_HERE
            slot = ((z + 4 - chip // 4) % 4) * 4 + (y + 4 - chip % 4) % 4
            block = gbuf[height - distance][slot]
            present = stored[height, distance, m]
            for source in range(4):
                here = jnp.where(jnp.logical_and(present, a % NODES_HERE == source), m, -1)
                total = jnp.where(node_of == here, rolled(block, 32 * (m - source)), total)
        return total

    def share_solution(height, value):
        gbuf[height][0] = value
        for offset in OFFSETS:
            slot = offset[0] * 4 + offset[1]
            send(
                gbuf[height].at[0], gbuf[height].at[slot], GATHER + height,
                {"col": column(offset)},
            )

    loads["right"].wait()
    loads["sums"].wait()

    def source_of(height, m):
        rows = pl.ds(height * 128 + m, 32, stride=4)
        return jnp.where(g == 0, right[rows, :], 0.0) - sums[rows, :]

    group32 = lane_ids(32) // 32

    def half_of(blocks, parity, half):
        total = None
        for m in range(NODES_HERE):
            moved = rolled(blocks[m], 32 * (m - 2 * parity - half))
            total = moved if total is None else jnp.where(group32 == m, moved, total)
        return total

    for height in (3, 2):
        blocks = [source_of(height, m) for m in range(NODES_HERE)]
        for parity in range(2):
            rows = pl.ds(parity, 32, stride=2)
            halves = [half_of(blocks, parity, half) for half in range(2)]
            if height == 3:
                topsend[0, rows, :] = halves[0]
                topsend[1, rows, :] = halves[1]
            else:
                init[2, rows, :] = jnp.where(g == 0, halves[0], halves[1])
                nextsend[rows, :] = jnp.where(g == 0, halves[1], halves[0])
    toprecv[me] = topsend[g]
    pl.semaphore_wait(barrier, len(OFFSETS) + len(others))
    for place in others:
        send(
            topsend.at[place[0]], toprecv.at[me], TOP_IN, {"gz": place[0], "row": place[1]},
        )
    send(nextsend, nextrecv, NEXT_IN, {"gz": 1 - g})
    l_near(2)
    loads["linv3"].wait()
    loads["lpart3"].wait()
    make_vpart(3, 1)
    loads["lpart1"].wait()
    make_vpart(3, 2)
    wait_blocks(recv_sem.at[TOP_IN], 7)

    b_pair = pair_of(jnp.concatenate([toprecv[part] + toprecv[4 + part] for part in range(4)], axis=0))
    scatter_terms(3, 1, part_terms(3, b_pair), True, True)
    send_terms(3, 2, b_pair)
    l_far(2)
    loads["lpart2"].wait()
    make_vpart(3, 3)
    send_terms(3, 3, b_pair)
    pieces = exchange([source_of(height, m) for height in range(2) for m in range(NODES_HERE)])
    for octet in range(8):
        xsend[octet] = pieces[octet]
    for place in others:
        send(
            xsend.at[place[0] * 4 + place[1]], xrecv.at[me], INPUT,
            {"gz": place[0], "row": place[1]},
        )
    xrecv[me] = xsend[me]
    l_near(1)
    u_near(0)
    finish_forward(3, b_pair)
    l_hand(2)
    loads["linv2"].wait()
    loads["lpart0"].wait()
    make_vpart(2, 2)
    wait_blocks(recv_sem.at[NEXT_IN], 1)
    init[2] = init[2] + nextrecv[...]
    l_wait(2)
    multiply(v21, lambda m: lower[1, m], lambda m: linv[2, m])
    scatter_terms(3, 2, take_terms(3, 2), True, False)

    rhs = sum_received(2)
    send_parts(3, OWN, rhs)
    spread_rhs(2, rhs)
    l_far(1)
    scatter_terms(3, 3, take_terms(3, 3), True, False)
    wait_bytes(xrecv.at[pl.ds(0, 7)], recv_sem.at[INPUT])
    parts = exchange([xrecv[part] + xrecv[4 + part] for part in range(4)])
    for height in range(2):
        for parity in range(2):
            init[height, pl.ds(parity, 32, stride=2), :] = half_of(parts, parity, height)
    scatter_terms(2, 1, apply(lambda m: v21[m], operand_of(take_parts(3, OWN))), False, True)
    b_pair = take_rhs(2)
    send_terms(2, 2, b_pair)
    u_far(0)
    u_near(2)
    l_hand(1)
    u_near(1)
    finish_forward(2, b_pair)
    loads["linv1"].wait()
    l_wait(1)
    multiply(v11, lambda m: lower[0, m], lambda m: linv[1, m])
    scatter_terms(2, 2, take_terms(2, 2), False, False)

    rhs = sum_received(1)
    spread_rhs(1, rhs)
    scatter_terms(1, 1, apply(lambda m: v11[m], operand_of(rhs)), False, True)
    loads["upper"].wait()
    u_hand(0)
    u_far(2)
    u_far(1)
    u_near(5)
    finish_forward(1, take_rhs(1))
    u_near(4)
    loads["linv0"].wait()
    loads["uinv0"].wait()
    multiply(ul, lambda m: uinv[0, m], lambda m: linv[0, m])
    loads["uinv1"].wait()
    rest1 = apply(lambda m: wide_of(uinv[1, m]), operand_of(fown[0, r]))
    u_wait(0)
    multiply(w11, lambda m: uinv[1, m], lambda m: upper[0, m])

    rhs = sum_received(0)
    value = apply(lambda m: ul[m], operand_of(rhs))
    share_solution(0, value)
    spread_rhs(0, rhs)
    spread_solution(0, value)
    u_hand(1)
    u_hand(2)
    u_far(5)
    u_far(4)
    finish_forward(0, take_rhs(0))
    u_near(3)
    hand_solution(0)
    u_wait(1)
    loads["uinv2"].wait()
    multiply(w21, lambda m: uinv[2, m], lambda m: upper[1, m])
    write_forward(3, 0)

    wait_blocks(recv_sem.at[GATHER + 0], 15)
    value = rest1 - apply(lambda m: w11[m], operand_of(chosen(1, 1)))
    share_solution(1, value)
    spread_solution(1, value)
    u_hand(5)
    u_hand(4)
    u_far(3)
    u_wait(2)
    rest = fown[1, r] - apply(lambda m: wide_of(upper[2, m]), operand_of(chosen(2, 2)))
    rest2 = apply(lambda m: wide_of(uinv[2, m]), operand_of(rest))
    write_forward(2, 1)
    hand_solution(1)

    wait_blocks(recv_sem.at[GATHER + 1], 15)
    value = rest2 - apply(lambda m: w21[m], operand_of(chosen(2, 1)))
    share_solution(2, value)
    spread_solution(2, value)
    u_hand(3)
    u_wait(5)
    rest = fown[2, r] - apply(lambda m: wide_of(upper[5, m]), operand_of(chosen(3, 3)))
    u_wait(4)
    rest = rest - apply(lambda m: wide_of(upper[4, m]), operand_of(chosen(3, 2)))
    loads["uinv3"].wait()
    rest3 = apply(lambda m: wide_of(uinv[3, m]), operand_of(rest))
    u_wait(3)
    multiply(w31, lambda m: uinv[3, m], lambda m: upper[3, m])
    hand_solution(2)

    wait_blocks(recv_sem.at[GATHER + 2], 15)
    value = rest3 - apply(lambda m: w31[m], operand_of(chosen(3, 1)))
    spread_solution(3, value)
    write_forward(1, 2)
    write_forward(0, 3)
    write_backward(0, 4)
    write_backward(1, 5)
    write_backward(2, 6)
    write_backward(3, 7)

    for phase, blocks in (
        [(TOP_IN, 7), (NEXT_IN, 1)]
        + [(SCATTER + t, 15) for t in range(3)]
        + [(GATHER + t, 15) for t in range(3)]
        + [(RHS + h, 3) for h in range(3)]
        + [(F_GZ + h, 4) for h in range(4)]
        + [(Y_ROW + h, 7 if h == 3 else 3) for h in range(4)]
        + [(Y_GZ + h, 4) for h in range(3)]
        + [(L_NEAR + p, 8) for p in range(2)]
        + [(L_FAR + p, 4) for p in range(2)]
        + [(L_GZ + p, 16) for p in range(2)]
        + [(U_NEAR + p, 8) for p in range(6)]
        + [(U_FAR + p, 4) for p in range(6)]
        + [(U_GZ + p, 16) for p in range(6)]
    ):
        wait_blocks(send_sem.at[phase], blocks)
    wait_bytes(xrecv.at[pl.ds(0, 7)], send_sem.at[INPUT])
    for phase in (PX, PX + 1, PX + 2, OWN):
        wait_bytes(pxrecv.at[0, pl.ds(0, 3)], send_sem.at[phase])
    for slot, (height, out, hbm) in enumerate(
        [(h, out_f, fwd_hbm) for h in (3, 2, 1, 0)] + [(h, out_b, bwd_hbm) for h in (0, 1, 2, 3)]
    ):
        rows = pl.ds(height * 512, 512)
        pltpu.make_async_copy(out.at[rows], hbm.at[rows], store_sem.at[slot]).wait()


def body(
    right_side, layer_sums, lower_blocks, upper_blocks, lower_inverse, upper_diagonal_inverses,
    pattern, parents,
):
    def tiled(x):
        return x.reshape(4, 4, 32, 128).transpose(0, 2, 1, 3).reshape(512, 128)

    anywhere = pl.BlockSpec(memory_space=pl.ANY)
    scalar = pl.BlockSpec(memory_space=pltpu.SMEM)
    forward, backward = pl.pallas_call(
        kernel,
        out_shape=[jax.ShapeDtypeStruct((2048, 128), F32)] * 2,
        in_specs=[anywhere] * 6 + [scalar] * 2,
        out_specs=[anywhere] * 2,
        scratch_shapes=[
            pltpu.VMEM((512, 128), F32),
            pltpu.VMEM((512, 128), F32),
            pltpu.VMEM((2, 4, 256, 256), F32),
            pltpu.VMEM((4, 4, 64, 256), F32),
            pltpu.VMEM((6, 4, 256, 256), F32),
            pltpu.VMEM((4, 4, 256, 256), F32),
            pltpu.VMEM((4, 4, 256, 256), F32),
            pltpu.VMEM((2, 64, 128), F32),
            pltpu.VMEM((8, 64, 128), F32),
            pltpu.VMEM((64, 128), F32),
            pltpu.VMEM((64, 128), F32),
            pltpu.VMEM((8, 32, 128), F32),
            pltpu.VMEM((8, 32, 128), F32),
            pltpu.VMEM((4, 64, 128), F32),
            pltpu.VMEM((3, 16, 64, 128), F32),
            pltpu.VMEM((3, 16, 64, 128), F32),
            pltpu.VMEM((16, 64, 128), F32),
            pltpu.VMEM((16, 64, 128), F32),
            pltpu.VMEM((16, 64, 128), F32),
            pltpu.VMEM((3, 4, 64, 128), F32),
            pltpu.VMEM((4, 4, 16, 128), F32),
            pltpu.VMEM((4, 4, 16, 128), F32),
            pltpu.VMEM((256, 128), F32),
            pltpu.VMEM((4, 2, 256, 128), F32),
            pltpu.VMEM((3, 4, 64, 128), F32),
            pltpu.VMEM((4, 8, 64, 128), F32),
            pltpu.VMEM((4, 4, 64, 256), F32),
        ]
        + [pltpu.VMEM((4, 256, 512), BF16)] * 6
        + [
            pltpu.VMEM((2048, 128), F32),
            pltpu.VMEM((2048, 128), F32),
            pltpu.SemaphoreType.DMA((PHASES,)),
            pltpu.SemaphoreType.DMA((PHASES,)),
            pltpu.SemaphoreType.DMA((20,)),
            pltpu.SemaphoreType.DMA((8,)),
        ],
        compiler_params=pltpu.CompilerParams(
            collective_id=0, has_side_effects=True, vmem_limit_bytes=50 * 1024 * 1024
        ),
    )(
        *[
            pltpu.with_memory_space_constraint(x, pltpu.HBM)
            for x in (
                tiled(right_side), tiled(layer_sums[0]), lower_blocks, upper_blocks,
                lower_inverse, upper_diagonal_inverses,
            )
        ],
        pattern.T, parents,
    )

    def copy_out(f_in, b_in, f_to, b_to, sems):
        moves = []
        for source, target in ((f_in, f_to), (b_in, b_to)):
            for part in range(4):
                rows = pl.ds(part * 512, 512)
                moves.append(pltpu.make_async_copy(source.at[rows], target.at[rows], sems.at[len(moves)]))
        for move in moves:
            move.start()
        for move in moves:
            move.wait()

    forward, backward = pl.pallas_call(
        copy_out,
        out_shape=[jax.ShapeDtypeStruct((2048, 128), F32)] * 2,
        in_specs=[anywhere] * 2,
        out_specs=[pl.BlockSpec(memory_space=pltpu.HBM)] * 2,
        scratch_shapes=[pltpu.SemaphoreType.DMA((8,))],
        compiler_params=pltpu.CompilerParams(vmem_limit_bytes=8 * 1024 * 1024),
    )(forward, backward)

    def untiled(x):
        return x.reshape(4, 128, 4, 128).transpose(0, 2, 1, 3).reshape(4, 4, 16384)

    return untiled(forward), untiled(backward)


def solution(mesh):
    in_specs = (
        P(None, "col", "row"),
        P("gz", None, "col", "row"),
        P(None, "col", "row", None),
        P(None, "col", "row", None),
        P(None, "col", None, None),
        P(None, "col", None, None),
        P(None, "col"),
        P(),
    )
    out_specs = (P(None, "col", None), P(None, "col", None))
    return jax.shard_map(body, mesh=mesh, in_specs=in_specs, out_specs=out_specs, check_vma=False)
```

```python
import jax
import jax.numpy as jnp
from jax import lax
from jax.experimental import pallas as pl
from jax.experimental.pallas import tpu as pltpu
from jax.sharding import PartitionSpec as P

MESH = pl.DeviceIdType.MESH
F32 = jnp.float32
BF16 = jnp.bfloat16
LANES = 128
PART = 64
NODES_HERE = 4
OFFSETS = [
    (2, 2), (1, 2), (2, 3), (3, 1), (0, 2), (3, 3), (1, 3), (2, 1), (3, 2), (1, 1),
    (2, 0), (1, 0), (0, 1), (0, 3), (3, 0),
]
INPUT, SCATTER, GATHER, RHS, F_GZ, Y_ROW, Y_GZ, PX = 0, 1, 4, 7, 11, 15, 19, 22
L_NEAR, L_FAR, L_GZ, U_NEAR, U_FAR, U_GZ, TOP_IN, NEXT_IN, OWN, PHASES = 25, 28, 31, 34, 40, 46, 52, 53, 54, 55


def place_of(height, distance):
    return height * (height - 1) // 2 + distance - 1


def lane_ids(rows):
    return lax.broadcasted_iota(jnp.int32, (rows, LANES), 1)


def split(x):
    high = x.astype(BF16)
    return high, (x - high.astype(F32)).astype(BF16)


def dot(a, b):
    return jnp.dot(a, b, preferred_element_type=F32)


def wide_of(a):
    return jnp.concatenate(split(a), axis=1)


def rolled(x, lanes):
    lanes = lanes % LANES
    return pltpu.roll(x, lanes, 1) if lanes else x


def operand_of(x):
    full = jnp.concatenate([rolled(x, -8 * part) for part in range(4)], axis=0)
    high = full.astype(BF16).astype(F32)
    low = full - high
    first = (lane_ids(256) // 8) % 4 == 0
    both = jnp.where(first, high, rolled(low.astype(BF16).astype(F32), 8))
    alone = jnp.where(first, high, 0.0)
    return jnp.concatenate([both.astype(BF16), alone.astype(BF16)], axis=0)


def apply(matrix_of, operand):
    node = lane_ids(256) // 32
    total = None
    for m in range(NODES_HERE):
        out = dot(matrix_of(m), operand)
        total = out if total is None else jnp.where(node == m, out, total)
    total = total + rolled(total, -8)
    quarter = (lane_ids(PART) // 8) % 4
    packed = None
    for part in range(4):
        moved = rolled(total[part * PART:(part + 1) * PART], 8 * part)
        packed = moved if packed is None else jnp.where(quarter == part, moved, packed)
    return packed


def pair_of(b):
    high, low = split(b)
    return high, jnp.concatenate([high, low], axis=1)


def product(a, b_pair):
    a_high, a_low = split(a)
    b_high, b_both = b_pair
    wide = dot(a_high, b_both)
    return wide[:, :LANES] + wide[:, LANES:] + dot(a_low, b_high)


def exchange(arrays):
    octet = lane_ids(arrays[0].shape[0]) // 8
    arrays = list(arrays)
    for bit in (1, 2, 4, 8)[: len(arrays).bit_length() - 1]:
        low = (octet // bit) % 2 == 0
        for i in range(len(arrays)):
            if i & bit:
                continue
            a, b = arrays[i], arrays[i | bit]
            arrays[i] = jnp.where(low, a, rolled(b, 8 * bit))
            arrays[i | bit] = jnp.where(low, rolled(a, -8 * bit), b)
    return arrays


def kernel(
    right_hbm, sums_hbm, lower_hbm, upper_hbm, linv_hbm, uinv_hbm, pattern_ref, parents_ref,
    fwd_hbm, bwd_hbm,
    right, sums, lower, lpart, upper, linv, uinv,
    topsend, toprecv, nextsend, nextrecv, xsend, xrecv, init, sbuf, qbuf, gbuf0, gbuf1, gbuf2, rbuf, pxsend, pxrecv,
    full, fbuf, fown, ybuf, vpart, v21, v11, ul, w11, w21, w31, out_f, out_b,
    send_sem, recv_sem, load_sem, store_sem,
):
    g = lax.axis_index("gz")
    r = lax.axis_index("row")
    c = lax.axis_index("col")
    z, y = c // 4, c % 4
    me = g * 4 + r
    gbuf = (gbuf0, gbuf1, gbuf2)

    def column(offset):
        return ((z + offset[0]) % 4) * 4 + (y + offset[1]) % 4

    loads = {}

    def load(name, source, target):
        loads[name] = pltpu.make_async_copy(source, target, load_sem.at[len(loads)])
        loads[name].start()

    my_rows = pl.ds(pl.multiple_of(r * PART, PART), PART)
    my_nodes = pl.ds(g * 2, 2)
    load("right", right_hbm, right)
    load("sums", sums_hbm, sums)
    load("linv3", linv_hbm.at[3], linv.at[3])
    for height in (3, 2, 1):
        if height < 3:
            load(
                "lower%d" % height, lower_hbm.at[place_of(height, 1), my_nodes],
                lower.at[height - 1, my_nodes, my_rows, :],
            )
        else:
            load("lpart3", lower_hbm.at[place_of(3, 1)], lpart.at[3])
        for distance in range(2, height + 1):
            place = height + distance - 4
            load("lpart%d" % place, lower_hbm.at[place_of(height, distance)], lpart.at[place])
    load("linv2", linv_hbm.at[2], linv.at[2])
    load("linv1", linv_hbm.at[1], linv.at[1])
    load("upper", upper_hbm.at[:, my_nodes], upper.at[:, my_nodes, my_rows, :])
    load("linv0", linv_hbm.at[0], linv.at[0])
    for height in (0, 1, 2, 3):
        load("uinv%d" % height, uinv_hbm.at[height], uinv.at[height])

    barrier = pltpu.get_barrier_semaphore()
    for offset in OFFSETS:
        pl.semaphore_signal(
            barrier, inc=1, device_id={"col": column(offset)}, device_id_type=MESH
        )
    row_steps = (2, 1, 3)
    others = []
    for step in (2, 1, 3):
        others.append((g, (r + step) % 4))
        others.append((1 - g, (r + step) % 4))
    others.append((1 - g, r))
    for place in others:
        pl.semaphore_signal(
            barrier, inc=1, device_id={"gz": place[0], "row": place[1]}, device_id_type=MESH
        )

    def send(source, target, phase, place):
        pltpu.make_async_remote_copy(
            src_ref=source, dst_ref=target, send_sem=send_sem.at[phase],
            recv_sem=recv_sem.at[phase], device_id=place, device_id_type=MESH,
        ).start()

    def wait_bytes(whole, sem):
        pltpu.make_async_copy(whole, whole, sem).wait()

    def wait_blocks(sem, blocks):
        wait_bytes(qbuf.at[0, pl.ds(0, blocks)], sem)

    ancestor, stored = {}, {}
    for height in (1, 2, 3):
        for m in range(NODES_HERE):
            current = parents_ref[height - 1, c * NODES_HERE + m]
            for distance in range(1, height + 1):
                if distance > 1:
                    current = parents_ref[height - distance, current]
                ancestor[height, distance, m] = current
                stored[height, distance, m] = pattern_ref[m, place_of(height, distance)] != 0

    node_of = lane_ids(PART) // 32
    right_mate, left_mate = (r + 1) % 4, (r + 3) % 4

    def rows_of(part):
        return pl.ds(pl.multiple_of(part * PART, PART), PART)

    def near(source, q, target, at, phase):
        for mate in (right_mate, left_mate):
            send(
                source.at[q, my_nodes], target.at[at, my_nodes, my_rows, :], phase + at,
                {"row": mate},
            )

    def far(target, at, phase_near, phase_far):
        wait_bytes(upper.at[0, pl.ds(0, 2), pl.ds(0, 128), :], recv_sem.at[phase_near + at])
        for node, part, mate in ((2 * g, left_mate, right_mate), (2 * g + 1, right_mate, left_mate)):
            block = target.at[at, node, rows_of(part), :]
            send(block, block, phase_far + at, {"row": mate})

    def hand(target, at, phase_far, phase_gz):
        wait_bytes(upper.at[0, pl.ds(0, 2), pl.ds(0, 64), :], recv_sem.at[phase_far + at])
        send(target.at[at, my_nodes], target.at[at, my_nodes], phase_gz + at, {"gz": 1 - g})

    def l_near(height):
        near(lower_hbm, place_of(height, 1), lower, height - 1, L_NEAR)

    def l_far(height):
        far(lower, height - 1, L_NEAR, L_FAR)

    def l_hand(height):
        loads["lower%d" % height].wait()
        hand(lower, height - 1, L_FAR, L_GZ)

    def l_wait(height):
        wait_bytes(upper.at[0, pl.ds(0, 2)], recv_sem.at[L_GZ + height - 1])

    def u_near(q):
        near(upper_hbm, q, upper, q, U_NEAR)

    def u_far(q):
        far(upper, q, U_NEAR, U_FAR)

    def u_hand(q):
        hand(upper, q, U_FAR, U_GZ)

    def u_wait(q):
        wait_bytes(upper.at[0, pl.ds(0, 2)], recv_sem.at[U_GZ + q])

    def multiply(target, a_of, b_of):
        def one(m, carry):
            a_high, a_low = split(a_of(m))
            b_high, b_low = split(b_of(m))
            target[m] = wide_of(dot(a_high, b_high) + dot(a_high, b_low) + dot(a_low, b_high))
            return carry
        lax.fori_loop(0, NODES_HERE, one, 0)

    def scatter_terms(height, distance, terms_in, first, out):
        target = height - distance
        moved = {shift: rolled(terms_in, 32 * shift) for shift in range(-3, 4)}
        terms = []
        for m in range(NODES_HERE):
            spread = moved[-m]
            for t in range(1, 4):
                spread = jnp.where(node_of == t, moved[t - m], spread)
            terms.append(spread)
        wanted = [
            jnp.where(stored[height, distance, m], ancestor[height, distance, m], -1)
            for m in range(NODES_HERE)
        ]
        for offset in OFFSETS + [(0, 0)]:
            slot = offset[0] * 4 + offset[1]
            base = column(offset) * NODES_HERE
            total = jnp.zeros((PART, LANES), F32) if first else sbuf[target, slot]
            for m in range(NODES_HERE):
                total = total + jnp.where(node_of == wanted[m] - base, terms[m], 0.0)
            sbuf[target, slot] = total
            if out and slot:
                send(
                    sbuf.at[target, slot], qbuf.at[target, slot], SCATTER + target,
                    {"col": column(offset)},
                )

    def sum_received(target):
        wait_blocks(recv_sem.at[SCATTER + target], 15)
        total = init[target] - sbuf[target, 0]
        for slot in range(1, 16):
            total = total - qbuf[target, slot]
        return total

    def spread_rhs(height, value):
        rbuf[height, r] = value
        for step in row_steps:
            send(
                rbuf.at[height, r], rbuf.at[height, r], RHS + height, {"row": (r + step) % 4}
            )

    def take_rhs(height):
        wait_blocks(recv_sem.at[RHS + height], 3)
        blocks = [rbuf[height, mate] for mate in range(4)]
        if height < 2:
            blocks = exchange(blocks)
        return pair_of(jnp.concatenate(blocks, axis=0))

    def make_vpart(height, distance):
        place = 3 if distance == 1 else height + distance - 4
        q_rows = lpart.at[place]

        def one(m, carry):
            a_high, a_low = split(q_rows[m])
            b_high, b_low = split(linv[height, m])
            vpart[place, m] = dot(a_high, b_high) + dot(a_high, b_low) + dot(a_low, b_high)
            return carry

        lax.fori_loop(0, NODES_HERE, one, 0)

    def part_terms(place, b_pair):
        total = None
        for m in range(NODES_HERE):
            out = product(vpart[place, m], b_pair)
            total = out if total is None else jnp.where(node_of == m, out, total)
        return total

    def send_terms(height, distance, b_pair):
        place = height + distance - 4
        send_parts(place, PX + place, part_terms(place, b_pair))

    def send_parts(place, phase, total):
        blocks = exchange([total[16 * part:16 * part + 16] for part in range(4)])
        for mate in range(4):
            pxsend[place, mate] = blocks[mate]
        pxrecv[place, r] = pxsend[place, r]
        for step in row_steps:
            to = (r + step) % 4
            send(pxsend.at[place, to], pxrecv.at[place, r], phase, {"row": to})

    def take_terms(height, distance):
        place = height + distance - 4
        return take_parts(place, PX + place)

    def take_parts(place, phase):
        wait_bytes(pxrecv.at[place, pl.ds(0, 3)], recv_sem.at[phase])
        return jnp.concatenate(exchange([pxrecv[place, mate] for mate in range(4)]), axis=0)

    def finish_forward(height, b_pair):
        node = lane_ids(256) // 32

        def one(m, carry):
            full[...] = jnp.where(node == m, product(linv[height, m], b_pair), full[...])
            return carry

        lax.fori_loop(0, NODES_HERE, one, 0)
        fbuf[height, g] = full[...]
        send(fbuf.at[height, g], fbuf.at[height, g], F_GZ + height, {"gz": 1 - g})
        if height:
            own = exchange([full[part * PART:(part + 1) * PART, :] for part in range(4)])
            for mate in range(4):
                fown[height - 1, mate] = own[mate]

    def write_forward(height, slot):
        wait_blocks(recv_sem.at[F_GZ + height], 4)
        group = lane_ids(128) // 32
        pieces = [
            fbuf[height, half, pl.ds(parity, 128, stride=2), :]
            for parity in range(2) for half in range(2)
        ]
        for m in range(NODES_HERE):
            total = None
            for place in range(4):
                moved = rolled(pieces[place], 32 * (place - m))
                total = moved if total is None else jnp.where(group == place, moved, total)
            out_f[pl.ds(height * 512 + m, 128, stride=4), :] = total
        rows = pl.ds(height * 512, 512)
        pltpu.make_async_copy(out_f.at[rows], fwd_hbm.at[rows], store_sem.at[slot]).start()

    my_octets = pl.ds(pl.multiple_of(g * 4, 4), 4)

    def spread_solution(height, value):
        ybuf[height, me] = value
        places = others if height == 3 else [(g, (r + step) % 4) for step in row_steps]
        for place in places:
            send(
                ybuf.at[height, me], ybuf.at[height, me], Y_ROW + height,
                {"gz": place[0], "row": place[1]},
            )

    def hand_solution(height):
        wait_blocks(recv_sem.at[Y_ROW + height], 3)
        send(ybuf.at[height, my_octets], ybuf.at[height, my_octets], Y_GZ + height, {"gz": 1 - g})

    def write_backward(height, slot):
        if height == 3:
            wait_blocks(recv_sem.at[Y_ROW + height], 7)
        else:
            wait_blocks(recv_sem.at[Y_GZ + height], 4)
        pieces = exchange([
            ybuf[height, octet, pl.ds(parity, 32, stride=2), :]
            for parity in range(2) for octet in range(8)
        ])
        for index in range(16):
            m, part = index // 4, index % 4
            out_b[pl.ds(height * 512 + part * 128 + m, 32, stride=4), :] = pieces[index]
        rows = pl.ds(height * 512, 512)
        pltpu.make_async_copy(out_b.at[rows], bwd_hbm.at[rows], store_sem.at[slot]).start()

    def chosen(height, distance):
        total = jnp.zeros((PART, LANES), F32)
        for m in range(NODES_HERE):
            a = ancestor[height, distance, m]
            chip = a // NODES_HERE
            slot = ((z + 4 - chip // 4) % 4) * 4 + (y + 4 - chip % 4) % 4
            block = gbuf[height - distance][slot]
            present = stored[height, distance, m]
            for source in range(4):
                here = jnp.where(jnp.logical_and(present, a % NODES_HERE == source), m, -1)
                total = jnp.where(node_of == here, rolled(block, 32 * (m - source)), total)
        return total

    def share_solution(height, value):
        gbuf[height][0] = value
        for offset in OFFSETS:
            slot = offset[0] * 4 + offset[1]
            send(
                gbuf[height].at[0], gbuf[height].at[slot], GATHER + height,
                {"col": column(offset)},
            )

    loads["right"].wait()
    loads["sums"].wait()

    def source_of(height, m):
        rows = pl.ds(height * 128 + m, 32, stride=4)
        return jnp.where(g == 0, right[rows, :], 0.0) - sums[rows, :]

    group32 = lane_ids(32) // 32

    def half_of(blocks, parity, half):
        total = None
        for m in range(NODES_HERE):
            moved = rolled(blocks[m], 32 * (m - 2 * parity - half))
            total = moved if total is None else jnp.where(group32 == m, moved, total)
        return total

    for height in (3, 2):
        blocks = [source_of(height, m) for m in range(NODES_HERE)]
        for parity in range(2):
            rows = pl.ds(parity, 32, stride=2)
            halves = [half_of(blocks, parity, half) for half in range(2)]
            if height == 3:
                topsend[0, rows, :] = halves[0]
                topsend[1, rows, :] = halves[1]
            else:
                init[2, rows, :] = jnp.where(g == 0, halves[0], halves[1])
                nextsend[rows, :] = jnp.where(g == 0, halves[1], halves[0])
    toprecv[me] = topsend[g]
    pl.semaphore_wait(barrier, len(OFFSETS) + len(others))
    for place in others:
        send(
            topsend.at[place[0]], toprecv.at[me], TOP_IN, {"gz": place[0], "row": place[1]},
        )
    send(nextsend, nextrecv, NEXT_IN, {"gz": 1 - g})
    l_near(2)
    loads["linv3"].wait()
    loads["lpart3"].wait()
    make_vpart(3, 1)
    loads["lpart1"].wait()
    make_vpart(3, 2)
    wait_blocks(recv_sem.at[TOP_IN], 7)

    b_pair = pair_of(jnp.concatenate([toprecv[part] + toprecv[4 + part] for part in range(4)], axis=0))
    scatter_terms(3, 1, part_terms(3, b_pair), True, True)
    send_terms(3, 2, b_pair)
    l_far(2)
    loads["lpart2"].wait()
    make_vpart(3, 3)
    send_terms(3, 3, b_pair)
    pieces = exchange([source_of(height, m) for height in range(2) for m in range(NODES_HERE)])
    for octet in range(8):
        xsend[octet] = pieces[octet]
    for place in others:
        send(
            xsend.at[place[0] * 4 + place[1]], xrecv.at[me], INPUT,
            {"gz": place[0], "row": place[1]},
        )
    xrecv[me] = xsend[me]
    l_near(1)
    u_near(0)
    finish_forward(3, b_pair)
    l_hand(2)
    loads["linv2"].wait()
    loads["lpart0"].wait()
    make_vpart(2, 2)
    wait_blocks(recv_sem.at[NEXT_IN], 1)
    init[2] = init[2] + nextrecv[...]
    l_wait(2)
    multiply(v21, lambda m: lower[1, m], lambda m: linv[2, m])
    scatter_terms(3, 2, take_terms(3, 2), True, False)

    rhs = sum_received(2)
    send_parts(3, OWN, rhs)
    spread_rhs(2, rhs)
    l_far(1)
    scatter_terms(3, 3, take_terms(3, 3), True, False)
    wait_bytes(xrecv.at[pl.ds(0, 7)], recv_sem.at[INPUT])
    parts = exchange([xrecv[part] + xrecv[4 + part] for part in range(4)])
    for height in range(2):
        for parity in range(2):
            init[height, pl.ds(parity, 32, stride=2), :] = half_of(parts, parity, height)
    scatter_terms(2, 1, apply(lambda m: v21[m], operand_of(take_parts(3, OWN))), False, True)
    b_pair = take_rhs(2)
    send_terms(2, 2, b_pair)
    u_far(0)
    u_near(2)
    l_hand(1)
    u_near(1)
    finish_forward(2, b_pair)
    loads["linv1"].wait()
    l_wait(1)
    multiply(v11, lambda m: lower[0, m], lambda m: linv[1, m])
    scatter_terms(2, 2, take_terms(2, 2), False, False)

    rhs = sum_received(1)
    spread_rhs(1, rhs)
    scatter_terms(1, 1, apply(lambda m: v11[m], operand_of(rhs)), False, True)
    loads["upper"].wait()
    u_hand(0)
    u_far(2)
    u_far(1)
    u_near(5)
    finish_forward(1, take_rhs(1))
    u_near(4)
    loads["linv0"].wait()
    loads["uinv0"].wait()
    multiply(ul, lambda m: uinv[0, m], lambda m: linv[0, m])
    loads["uinv1"].wait()
    rest1 = apply(lambda m: wide_of(uinv[1, m]), operand_of(fown[0, r]))
    u_wait(0)
    multiply(w11, lambda m: uinv[1, m], lambda m: upper[0, m])

    rhs = sum_received(0)
    value = apply(lambda m: ul[m], operand_of(rhs))
    share_solution(0, value)
    spread_rhs(0, rhs)
    spread_solution(0, value)
    u_hand(1)
    u_hand(2)
    u_far(5)
    u_far(4)
    finish_forward(0, take_rhs(0))
    u_near(3)
    hand_solution(0)
    u_wait(1)
    loads["uinv2"].wait()
    multiply(w21, lambda m: uinv[2, m], lambda m: upper[1, m])
    write_forward(3, 0)

    wait_blocks(recv_sem.at[GATHER + 0], 15)
    value = rest1 - apply(lambda m: w11[m], operand_of(chosen(1, 1)))
    share_solution(1, value)
    spread_solution(1, value)
    u_hand(5)
    u_hand(4)
    u_far(3)
    u_wait(2)
    rest = fown[1, r] - apply(lambda m: wide_of(upper[2, m]), operand_of(chosen(2, 2)))
    rest2 = apply(lambda m: wide_of(uinv[2, m]), operand_of(rest))
    write_forward(2, 1)
    hand_solution(1)

    wait_blocks(recv_sem.at[GATHER + 1], 15)
    value = rest2 - apply(lambda m: w21[m], operand_of(chosen(2, 1)))
    share_solution(2, value)
    spread_solution(2, value)
    u_hand(3)
    u_wait(5)
    rest = fown[2, r] - apply(lambda m: wide_of(upper[5, m]), operand_of(chosen(3, 3)))
    u_wait(4)
    rest = rest - apply(lambda m: wide_of(upper[4, m]), operand_of(chosen(3, 2)))
    loads["uinv3"].wait()
    rest3 = apply(lambda m: wide_of(uinv[3, m]), operand_of(rest))
    u_wait(3)
    multiply(w31, lambda m: uinv[3, m], lambda m: upper[3, m])
    hand_solution(2)

    wait_blocks(recv_sem.at[GATHER + 2], 15)
    value = rest3 - apply(lambda m: w31[m], operand_of(chosen(3, 1)))
    spread_solution(3, value)
    write_forward(1, 2)
    write_forward(0, 3)
    write_backward(0, 4)
    write_backward(1, 5)
    write_backward(2, 6)
    write_backward(3, 7)

    for phase, blocks in (
        [(TOP_IN, 7), (NEXT_IN, 1)]
        + [(SCATTER + t, 15) for t in range(3)]
        + [(GATHER + t, 15) for t in range(3)]
        + [(RHS + h, 3) for h in range(3)]
        + [(F_GZ + h, 4) for h in range(4)]
        + [(Y_ROW + h, 7 if h == 3 else 3) for h in range(4)]
        + [(Y_GZ + h, 4) for h in range(3)]
        + [(L_NEAR + p, 8) for p in range(2)]
        + [(L_FAR + p, 4) for p in range(2)]
        + [(L_GZ + p, 16) for p in range(2)]
        + [(U_NEAR + p, 8) for p in range(6)]
        + [(U_FAR + p, 4) for p in range(6)]
        + [(U_GZ + p, 16) for p in range(6)]
    ):
        wait_blocks(send_sem.at[phase], blocks)
    wait_bytes(xrecv.at[pl.ds(0, 7)], send_sem.at[INPUT])
    for phase in (PX, PX + 1, PX + 2, OWN):
        wait_bytes(pxrecv.at[0, pl.ds(0, 3)], send_sem.at[phase])
    for slot, (height, out, hbm) in enumerate(
        [(h, out_f, fwd_hbm) for h in (3, 2, 1, 0)] + [(h, out_b, bwd_hbm) for h in (0, 1, 2, 3)]
    ):
        rows = pl.ds(height * 512, 512)
        pltpu.make_async_copy(out.at[rows], hbm.at[rows], store_sem.at[slot]).wait()


def body(
    right_side, layer_sums, lower_blocks, upper_blocks, lower_inverse, upper_diagonal_inverses,
    pattern, parents,
):
    def tiled(x):
        return x.reshape(4, 4, 32, 128).transpose(0, 2, 1, 3).reshape(512, 128)

    anywhere = pl.BlockSpec(memory_space=pl.ANY)
    scalar = pl.BlockSpec(memory_space=pltpu.SMEM)
    forward, backward = pl.pallas_call(
        kernel,
        out_shape=[jax.ShapeDtypeStruct((2048, 128), F32)] * 2,
        in_specs=[anywhere] * 6 + [scalar] * 2,
        out_specs=[anywhere] * 2,
        scratch_shapes=[
            pltpu.VMEM((512, 128), F32),
            pltpu.VMEM((512, 128), F32),
            pltpu.VMEM((2, 4, 256, 256), F32),
            pltpu.VMEM((4, 4, 64, 256), F32),
            pltpu.VMEM((6, 4, 256, 256), F32),
            pltpu.VMEM((4, 4, 256, 256), F32),
            pltpu.VMEM((4, 4, 256, 256), F32),
            pltpu.VMEM((2, 64, 128), F32),
            pltpu.VMEM((8, 64, 128), F32),
            pltpu.VMEM((64, 128), F32),
            pltpu.VMEM((64, 128), F32),
            pltpu.VMEM((8, 32, 128), F32),
            pltpu.VMEM((8, 32, 128), F32),
            pltpu.VMEM((4, 64, 128), F32),
            pltpu.VMEM((3, 16, 64, 128), F32),
            pltpu.VMEM((3, 16, 64, 128), F32),
            pltpu.VMEM((16, 64, 128), F32),
            pltpu.VMEM((16, 64, 128), F32),
            pltpu.VMEM((16, 64, 128), F32),
            pltpu.VMEM((3, 4, 64, 128), F32),
            pltpu.VMEM((4, 4, 16, 128), F32),
            pltpu.VMEM((4, 4, 16, 128), F32),
            pltpu.VMEM((256, 128), F32),
            pltpu.VMEM((4, 2, 256, 128), F32),
            pltpu.VMEM((3, 4, 64, 128), F32),
            pltpu.VMEM((4, 8, 64, 128), F32),
            pltpu.VMEM((4, 4, 64, 256), F32),
        ]
        + [pltpu.VMEM((4, 256, 512), BF16)] * 6
        + [
            pltpu.VMEM((2048, 128), F32),
            pltpu.VMEM((2048, 128), F32),
            pltpu.SemaphoreType.DMA((PHASES,)),
            pltpu.SemaphoreType.DMA((PHASES,)),
            pltpu.SemaphoreType.DMA((20,)),
            pltpu.SemaphoreType.DMA((8,)),
        ],
        compiler_params=pltpu.CompilerParams(
            collective_id=0, has_side_effects=True, vmem_limit_bytes=50 * 1024 * 1024
        ),
    )(
        *[
            pltpu.with_memory_space_constraint(x, pltpu.HBM)
            for x in (
                tiled(right_side), tiled(layer_sums[0]), lower_blocks, upper_blocks,
                lower_inverse, upper_diagonal_inverses, pattern.T, parents,
            )
        ],
    )

    def copy_out(f_in, b_in, f_to, b_to, sems):
        moves = []
        for source, target in ((f_in, f_to), (b_in, b_to)):
            for part in range(4):
                rows = pl.ds(part * 512, 512)
                moves.append(pltpu.make_async_copy(source.at[rows], target.at[rows], sems.at[len(moves)]))
        for move in moves:
            move.start()
        for move in moves:
            move.wait()

    forward, backward = pl.pallas_call(
        copy_out,
        out_shape=[jax.ShapeDtypeStruct((2048, 128), F32)] * 2,
        in_specs=[anywhere] * 2,
        out_specs=[pl.BlockSpec(memory_space=pltpu.HBM)] * 2,
        scratch_shapes=[pltpu.SemaphoreType.DMA((8,))],
        compiler_params=pltpu.CompilerParams(vmem_limit_bytes=8 * 1024 * 1024),
    )(forward, backward)

    def untiled(x):
        return x.reshape(4, 128, 4, 128).transpose(0, 2, 1, 3).reshape(4, 4, 16384)

    return untiled(forward), untiled(backward)


def solution(mesh):
    in_specs = (
        P(None, "col", "row"),
        P("gz", None, "col", "row"),
        P(None, "col", "row", None),
        P(None, "col", "row", None),
        P(None, "col", None, None),
        P(None, "col", None, None),
        P(None, "col"),
        P(),
    )
    out_specs = (P(None, "col", None), P(None, "col", None))
    return jax.shard_map(body, mesh=mesh, in_specs=in_specs, out_specs=out_specs, check_vma=False)
```
